512 devices in a mesh: ctx: 64 (over z_hi, y, core), tp: 8 (over x, z_lo).
Axes of the slice: x: 4, y: 8, z: 8 (z_hi: 4, z_lo: 2; z = z_hi * 2 + z_lo), core: 2. Of those that a mesh axis runs over, the one named last changes fastest.
Arguments:
- query_in: bfloat16 [1024, 16384], P('tp', 'ctx'), may hold values from -6 to 6
- key_in: bfloat16 [1024, 16384], P('tp', 'ctx'), may hold values from -6 to 6
- value_in: bfloat16 [1024, 16384], P('tp', 'ctx'), may hold values from -6 to 6
- short_kernel: float32 [3, 1024, 7], P(None, 'tp'), may hold values from -2 to 2
- basis_weight: float32 [64, 33], replicated, may hold values from -96 to 96
- basis_bias: float32 [64], replicated, may hold values from -3.140625 to 3.140625
- filter_proj: float32 [1024, 64], P('tp'), may hold values from -0.75 to 0.75
- decay_rate: float32 [1024], P('tp'), as said below
- skip_gain: float32 [1024], P('tp'), may hold values from -3 to 3
- grad_out: bfloat16 [1024, 16384], P('tp', 'ctx'), may hold values from -6 to 6
Outputs:
- mixed: bfloat16 [1024, 16384], P('tp', 'ctx')
- grad_query: bfloat16 [1024, 16384], P('tp', 'ctx')
- grad_key: bfloat16 [1024, 16384], P('tp', 'ctx')
- grad_value: bfloat16 [1024, 16384], P('tp', 'ctx')
- grad_proj: float32 [1024, 64], P('tp')
- grad_basis: float32 [64, 33], replicated
The draws below stay inside these ranges and needn't reach their ends.
Inputs may be any that keep to these rules, and one draw needn't show every extreme that they name: decay_rate is positive in every channel.
All inputs are finite; a program needn't handle non-finite values.
Results may differ from the reference program's by a relative error of at most 0.0066.
Values may be sent and summed in bfloat16 or wider, within the bound.
No kernel may reach another device: no remote copies, remote signals or barrier semaphores. Data moves between devices by JAX's collectives and lax.ppermute only.
A program may use at most 64 MiB of HBM per device.

```python
import math
import jax
import jax.numpy as jnp
from jax import lax

CH_DEV = 128
FEAT = 64
NFREQ = 16
KSHORT = 7
EMB = 33
TOKENS = 16384
CHANNELS = 1024
N_TP = 8


def draw_decay_rate(key, part):
    pick_key, slow_key, fast_key = jax.random.split(key, 3)
    slow_share = 0.5
    slow_rate = jax.random.uniform(slow_key, (CHANNELS,), jnp.float32, 0.2, 2.0)
    fast_len = jax.random.uniform(fast_key, (CHANNELS,), jnp.float32, 30.0, 50.0)
    fast_rate = TOKENS / fast_len
    chosen = jax.random.bernoulli(pick_key, slow_share, (CHANNELS,))
    return jnp.where(chosen, slow_rate, fast_rate).astype(jnp.float32)


def steps_of(rng, extent, shards, low, largest):
    loudness = 1.0
    for dim, parts in shards:
        draws = jax.random.uniform(jax.random.fold_in(jax.random.fold_in(rng, 6), dim), (parts,), jnp.float32, low / len(shards), largest / len(shards))
        loudness = loudness * jnp.repeat(jnp.exp(draws), extent[dim] // parts).reshape((-1,) + (1,) * (len(extent) - 1 - dim))
    return loudness


def noise(rng, shape, deviation, most, cuts=(), kind=jnp.bfloat16):
    array = jax.random.normal(rng, shape, jnp.float32) * deviation
    if len(cuts) > 0:
        array = steps_of(rng, shape, cuts, -0.22, 0.18) * array
    return jnp.clip(array, min=-most, max=most).astype(kind)


def setup_inputs(seed: int = 0) -> dict:
    keys = jax.random.split(jax.random.key(seed), 11)
    query_in = noise(keys[0], (CHANNELS, TOKENS), 1.0, 6.0, ((0, 8), (1, 64)))
    key_in = noise(keys[1], (CHANNELS, TOKENS), 1.0, 6.0, ((0, 8), (1, 64)))
    value_in = noise(keys[2], (CHANNELS, TOKENS), 1.0, 6.0, ((0, 8), (1, 64)))
    short_kernel = noise(keys[3], (3, CHANNELS, KSHORT), KSHORT ** -0.5, 2.0, ((1, 8),), jnp.float32)
    basis_weight = jnp.clip(jax.random.uniform(keys[4], (FEAT, EMB), jnp.float32, -96.0, 96.0), -96.0, 96.0)
    basis_bias = jnp.clip(jax.random.uniform(keys[5], (FEAT,), jnp.float32, -3.140625, 3.140625), -3.140625, 3.140625)
    filter_proj = noise(keys[6], (CHANNELS, FEAT), FEAT ** -0.5, 0.75, ((0, 8),), jnp.float32)
    decay_rate = draw_decay_rate(jax.random.fold_in(keys[10], 71), 0)
    skip_gain = noise(keys[8], (CHANNELS,), 1.0, 3.0, ((0, 8),), jnp.float32)
    grad_out = noise(keys[9], (CHANNELS, TOKENS), 1.0, 6.0, ((0, 8), (1, 64)))
    return {"query_in": query_in, "key_in": key_in, "value_in": value_in, "short_kernel": short_kernel, "basis_weight": basis_weight, "basis_bias": basis_bias, "filter_proj": filter_proj, "decay_rate": decay_rate, "skip_gain": skip_gain, "grad_out": grad_out}


PRECISE = lax.Precision.HIGHEST

def features(offset_pos, num_pos, seq_total, num_freq):
    positions = offset_pos + jnp.arange(num_pos, dtype=jnp.int32)
    pieces = [positions.astype(jnp.float32) / seq_total]
    for harmonic in range(1, num_freq + 1):
        angles = (harmonic * positions % seq_total).astype(jnp.float32) * (2.0 * math.pi / seq_total)
        pieces.append(jnp.cos(angles))
        pieces.append(jnp.sin(angles))
    return jnp.stack(pieces)

def window(decay_rate, offset_pos, num_pos, seq_total):
    positions = (offset_pos + jnp.arange(num_pos, dtype=jnp.int32)).astype(jnp.float32)
    energy = jnp.expm1(-2.0 * decay_rate) / jnp.expm1(-2.0 * decay_rate / seq_total)
    return jnp.exp(-(decay_rate[:, None] * positions[None, :]) / seq_total) / jnp.sqrt(energy)[:, None]

def featurize(signal, kernel):
    num_taps = kernel.shape[1]
    result = kernel[:, 0:1] * signal
    for offset in range(1, num_taps):
        shifted = jnp.pad(signal[:, :-offset], ((0, 0), (offset, 0)))
        result = result + kernel[:, offset:offset + 1] * shifted
    return result

def featurize_back(signal, kernel):
    num_taps = kernel.shape[1]
    result = kernel[:, 0:1] * signal
    for offset in range(1, num_taps):
        shifted = jnp.pad(signal[:, offset:], ((0, 0), (0, offset)))
        result = result + kernel[:, offset:offset + 1] * shifted
    return result

def long_block(operands):
    filter_block, carried_block, grad_block, skip_block = operands
    seq_total = filter_block.shape[1]
    padded_len = 2 * seq_total
    carried_wide = carried_block.astype(jnp.float32)
    grad_wide = grad_block.astype(jnp.float32)
    carried_spec = jnp.fft.rfft(carried_wide, n=padded_len)
    filter_spec = jnp.fft.rfft(filter_block.astype(jnp.float32), n=padded_len)
    grad_spec = jnp.fft.rfft(grad_wide, n=padded_len)
    long_part = jnp.fft.irfft(filter_spec * carried_spec, n=padded_len)[:, :seq_total] + skip_block[:, None] * carried_wide
    carried_grad = jnp.fft.irfft(jnp.conj(filter_spec) * grad_spec, n=padded_len)[:, :seq_total] + skip_block[:, None] * grad_wide
    filter_grad = jnp.fft.irfft(jnp.conj(carried_spec) * grad_spec, n=padded_len)[:, :seq_total]
    return (long_part.astype(jnp.bfloat16), carried_grad.astype(jnp.bfloat16), filter_grad.astype(jnp.bfloat16))

def reference(query_in, key_in, value_in, short_kernel, basis_weight, basis_bias, filter_proj, decay_rate, skip_gain, grad_out):
    query_feat = featurize(query_in.astype(jnp.float32), short_kernel[0])
    key_feat = featurize(key_in.astype(jnp.float32), short_kernel[1])
    value_feat = featurize(value_in.astype(jnp.float32), short_kernel[2])
    carried = (key_feat * value_feat).astype(jnp.bfloat16)
    basis_rows = features(0, TOKENS, TOKENS, NFREQ)
    hidden_in = jnp.dot(basis_weight, basis_rows, precision=PRECISE, preferred_element_type=jnp.float32) + basis_bias[:, None]
    activation = jnp.sin(hidden_in)
    envelope = window(decay_rate, 0, TOKENS, TOKENS)
    filter_full = (jnp.dot(filter_proj, activation, precision=PRECISE, preferred_element_type=jnp.float32) * envelope).astype(jnp.bfloat16)
    grad_wide = grad_out.astype(jnp.float32)
    grad_long = (grad_wide * query_feat).astype(jnp.bfloat16)
    grouped = (filter_full.reshape(N_TP, CH_DEV, TOKENS), carried.reshape(N_TP, CH_DEV, TOKENS), grad_long.reshape(N_TP, CH_DEV, TOKENS), skip_gain.reshape(N_TP, CH_DEV))
    long_out, carried_grad, filter_grad = lax.map(long_block, grouped)
    long_out = long_out.reshape(CHANNELS, TOKENS)
    carried_grad = carried_grad.reshape(CHANNELS, TOKENS)
    filter_grad = filter_grad.reshape(CHANNELS, TOKENS)
    long_wide = long_out.astype(jnp.float32)
    mixed = (query_feat * long_wide).astype(jnp.bfloat16)
    grad_query_feat = (grad_wide * long_wide).astype(jnp.bfloat16)
    carried_wide = carried_grad.astype(jnp.float32)
    grad_key_feat = (carried_wide * value_feat).astype(jnp.bfloat16)
    grad_value_feat = (carried_wide * key_feat).astype(jnp.bfloat16)
    grad_query = featurize_back(grad_query_feat.astype(jnp.float32), short_kernel[0]).astype(jnp.bfloat16)
    grad_key = featurize_back(grad_key_feat.astype(jnp.float32), short_kernel[1]).astype(jnp.bfloat16)
    grad_value = featurize_back(grad_value_feat.astype(jnp.float32), short_kernel[2]).astype(jnp.bfloat16)
    grad_raw = filter_grad.astype(jnp.float32) * envelope
    grad_proj = jnp.dot(grad_raw, activation.T, precision=PRECISE, preferred_element_type=jnp.float32) * (1.0 / math.sqrt(TOKENS))
    grad_hidden = jnp.dot(filter_proj.T, grad_raw, precision=PRECISE, preferred_element_type=jnp.float32) * jnp.cos(hidden_in)
    grad_basis = jnp.dot(grad_hidden, basis_rows.T, precision=PRECISE, preferred_element_type=jnp.float32) * math.sqrt(FEAT / (TOKENS * CHANNELS))
    return (mixed, grad_query, grad_key, grad_value, grad_proj, grad_basis)
```

```python
import math

import jax
import jax.numpy as jnp
import numpy as np
from jax import lax
from jax.experimental import pallas as pl
from jax.experimental.pallas import tpu as pltpu
from jax.sharding import Mesh
from jax.sharding import PartitionSpec as P
import ml_dtypes

F32 = jnp.float32
BF16 = jnp.bfloat16
EXACT = lax.Precision.HIGHEST

ROWS = 64
COLS = 256
TOTAL = ROWS * COLS
FEAT = 64
EMB = 33
TAPS = 7
CHAN = 2
GROUP = 40
TURN = 1.0 / (2.0 * math.pi)

SIN_COEF = (
    6.2831854820251465,
    -41.34170150756836,
    81.60513305664062,
    -76.70301818847656,
    42.02592849731445,
    -14.899847030639648,
    3.2381374835968018,
)
COS_COEF = (
    1.0,
    -19.73920440673828,
    64.93911743164062,
    -85.45014190673828,
    60.16762924194336,
    -25.967599868774414,
    6.528658390045166,
)


def halves(table, count):
    parts = []
    rest = np.asarray(table, np.float64)
    for _ in range(count):
        part = rest.astype(np.float32).astype(ml_dtypes.bfloat16)
        parts.append(part)
        rest = rest - part.astype(np.float64)
    return parts


def transform_tables():
    rows = np.arange(ROWS)
    cols = np.arange(COLS)
    first = 2.0 * np.pi * ((4 * rows[:, None] + 1) * rows[None, :] % (4 * ROWS)) / (4 * ROWS)
    first_re, first_im = np.cos(first), -np.sin(first)
    forward = np.concatenate([first_re, first_im], axis=0)
    forward_cat = np.concatenate(halves(forward, 2), axis=1)
    last = np.concatenate([first_re.T, -first_im.T], axis=1) / TOTAL
    last_hi, last_lo = halves(last, 2)
    last_cat = np.concatenate([last_hi, last_lo, last_hi], axis=1)
    turn = 2.0 * np.pi * ((4 * rows[:, None] + 1) * cols[None, :]) / (4 * TOTAL)
    twiddle = np.stack([np.cos(turn), -np.sin(turn)]).astype(np.float32)
    inner = 2.0 * np.pi * (cols[:, None] * cols[None, :] % COLS) / COLS
    inner_re, inner_im = np.cos(inner), -np.sin(inner)
    full = np.concatenate(
        [
            np.concatenate([inner_re, inner_im], axis=1),
            np.concatenate([-inner_im, inner_re], axis=1),
        ],
        axis=0,
    )
    full_hi, full_lo = halves(full, 2)
    return forward_cat, last_cat, twiddle, np.stack([full_hi, full_lo])


def basis_tables():
    freq = np.arange(1, 17)
    cols = np.arange(COLS)
    rows = np.arange(ROWS)
    inner = 2.0 * np.pi * (freq[:, None] * cols[None, :] % TOTAL) / TOTAL
    short = np.concatenate(
        [np.cos(inner), np.sin(inner), cols[None, :] / TOTAL, np.ones((1, COLS))], axis=0
    )
    width = short.shape[0]
    hi, mid, lo = halves(short, 3)
    right = np.zeros((256, COLS), ml_dtypes.bfloat16)
    for place, part in ((0, hi), (GROUP, hi), (2 * GROUP, hi)):
        right[place : place + width] = part
    for place, part in ((128, mid), (128 + GROUP, lo), (128 + 2 * GROUP, mid)):
        right[place : place + width] = part
    outer = 2.0 * np.pi * (freq[None, :] * rows[:, None] % ROWS) / ROWS
    cos_out, sin_out = np.cos(outer), np.sin(outer)
    one = np.ones((ROWS, 1))
    block = rows[:, None] / ROWS
    cos_row = np.concatenate([cos_out, cos_out, one, one], axis=1)
    sin_row = np.concatenate([sin_out, sin_out, 0 * one, block], axis=1)
    turn = np.zeros((2, ROWS, 128), np.float32)
    for place in (0, GROUP, 2 * GROUP):
        turn[0, :, place : place + width] = cos_row
        turn[1, :, place : place + width] = sin_row
    pick = np.zeros((2, 128, 128), np.float32)
    for place in (0, GROUP, 2 * GROUP):
        for index in range(16):
            pick[0, 2 * index + 1, place + index] = 1.0
            pick[0, 2 * index + 2, place + 16 + index] = 1.0
            pick[1, 2 * index + 2, place + index] = 1.0
            pick[1, 2 * index + 1, place + 16 + index] = -1.0
        pick[0, 0, place + 32] = 1.0
        pick[0, EMB, place + 33] = 1.0
        pick[1, 0, place + 33] = 1.0
    back = np.zeros((COLS, 128))
    back[:, :width] = short.T
    back[:, 64:80] = short[16:32].T
    back[:, 80:96] = short[:16].T
    back_hi, back_lo = halves(back, 2)
    back_cat = np.concatenate([back_hi, back_lo], axis=1)
    back_turn = np.zeros((ROWS, 128), np.float32)
    back_turn[:, :32] = cos_row[:, :32]
    back_turn[:, 32] = 1.0
    back_turn[:, 33] = rows / ROWS
    back_turn[:, 64:80] = -sin_out
    back_turn[:, 80:96] = sin_out
    place = np.zeros((8, 8, 128), np.float32)
    for wanted in range(EMB):
        row, group = divmod(wanted, 8)
        if wanted == 0:
            lanes = (32, 33)
        elif wanted % 2:
            lanes = ((wanted - 1) // 2, 64 + (wanted - 1) // 2)
        else:
            lanes = (16 + (wanted - 2) // 2, 80 + (wanted - 2) // 2)
        for lane in lanes:
            place[group, row, lane] = 1.0
    return right, turn, pick, back_cat, back_turn, place


def split(value):
    hi = value.astype(BF16)
    lo = (value - hi.astype(F32)).astype(BF16)
    return hi, lo


def dot(left, right):
    return jnp.dot(left, right, preferred_element_type=F32)


def spectrum(signals, forward, twiddle_re, twiddle_im, full_hi, full_lo):
    wide = jnp.concatenate(signals, axis=1)
    section = dot(forward, jnp.concatenate([wide, wide], axis=0))
    turned = []
    for index in range(len(signals)):
        part = section[:, index * COLS : (index + 1) * COLS]
        part_re, part_im = part[:ROWS], part[ROWS:]
        turned.append(
            jnp.concatenate(
                [
                    part_re * twiddle_re - part_im * twiddle_im,
                    part_re * twiddle_im + part_im * twiddle_re,
                ],
                axis=1,
            )
        )
    return full_product(jnp.concatenate(turned, axis=0), full_hi, full_lo)


def full_product(value, full_hi, full_lo):
    hi, lo = split(value)
    return dot(hi, full_hi) + dot(lo, full_hi) + dot(hi, full_lo)


def restore(conj_spec, count, last, twiddle_re, twiddle_im, full_hi, full_lo):
    back = full_product(conj_spec, full_hi, full_lo)
    stacked = []
    for index in range(count):
        part = back[index * ROWS : (index + 1) * ROWS]
        part_re, part_im = part[:, :COLS], part[:, COLS:]
        stacked.append(
            jnp.concatenate(
                [
                    part_re * twiddle_re - part_im * twiddle_im,
                    part_re * twiddle_im + part_im * twiddle_re,
                ],
                axis=0,
            )
        )
    hi, lo = split(jnp.concatenate(stacked, axis=1))
    result = dot(last, jnp.concatenate([hi, hi, lo], axis=0))
    return [result[:, index * COLS : (index + 1) * COLS] for index in range(count)]


def take(ref, start, count, stride):
    return jnp.concatenate(
        [ref[half, pl.ds(start, count, stride=stride), :] for half in range(2)], axis=1
    )


def put(ref, start, count, stride, value):
    for half in range(2):
        ref[half, pl.ds(start, count, stride=stride), :] = value[:, half * 128 : half * 128 + 128]


def fill(ref, value):
    for half in range(2):
        ref[half] = value[..., half * 128 : half * 128 + 128].reshape(ref.shape[1], 128)


def pack_kernel(query, key, value, grad, out, wide):
    for index, ref in enumerate((query, key, value, grad)):
        value = ref[...].astype(F32)
        for half in range(2):
            wide[half, index * 128 : (index + 1) * 128, :] = value[:, half * 128 : half * 128 + 128]
    for peer in range(ROWS):
        out[peer] = take(wide, peer, 8, ROWS).astype(BF16)


def filter_kernel(
    own,
    decay,
    norm,
    layer,
    proj,
    pick,
    turn,
    right,
    forward,
    twiddle,
    full,
    act_out,
    cos_out,
    env_out,
    spec_out,
    column_out,
    left,
    phase,
    filt,
):
    first = own[0]
    layer_all = layer[...]
    same = jnp.dot(layer_all, pick[0], precision=EXACT, preferred_element_type=F32) * TURN
    cross = jnp.dot(layer_all, pick[1], precision=EXACT, preferred_element_type=F32) * TURN
    lane = lax.broadcasted_iota(jnp.int32, (FEAT, 128), 1)
    sublane = lax.broadcasted_iota(jnp.int32, (8, 128), 0)
    proj_turned = proj[...].T
    columns = []
    for chan in range(CHAN):
        hit = lane == first + 64 * chan
        column = jnp.sum(jnp.where(hit, proj_turned, 0.0), axis=1, keepdims=True)
        column_wide = jnp.broadcast_to(column, (FEAT, 128))
        column_out[chan * FEAT : (chan + 1) * FEAT, :] = column_wide
        columns.append(column_wide)

    def make_left(block, carry):
        value = same * turn[0, pl.ds(block, 1), :] + cross * turn[1, pl.ds(block, 1), :]
        hi = value.astype(BF16).astype(F32)
        rest = value - hi
        mid = rest.astype(BF16).astype(F32)
        lo = rest - mid
        one = jnp.where(lane < GROUP, hi, jnp.where(lane < 2 * GROUP, mid, lo))
        two = jnp.where(lane < 2 * GROUP, hi, mid)
        start = pl.multiple_of(block * FEAT, FEAT)
        left[pl.ds(start, FEAT), 0:128] = one.astype(BF16)
        left[pl.ds(start, FEAT), 128:256] = two.astype(BF16)
        return carry

    lax.fori_loop(0, ROWS, make_left, 0, unroll=2)

    def chunk(index, carry):
        base = pl.multiple_of(index * 512, 512)
        phase[...] = dot(left[pl.ds(base, 512), :], right[...])

        def one_block(inner, sums):
            near = pl.multiple_of(inner * FEAT, FEAT)
            kept = []
            for half in range(2):
                lanes = slice(half * 128, half * 128 + 128)
                turns = phase[pl.ds(near, FEAT), lanes]
                rest = turns - jnp.round(turns)
                square = rest * rest
                sine = jnp.full_like(rest, SIN_COEF[-1])
                cosine = jnp.full_like(rest, COS_COEF[-1])
                for coef in SIN_COEF[-2::-1]:
                    sine = sine * square + coef
                for coef in COS_COEF[-2::-1]:
                    cosine = cosine * square + coef
                sine = sine * rest
                act_out[pl.ds(base + near, FEAT), lanes] = sine.astype(BF16)
                cos_out[pl.ds(base + near, FEAT), lanes] = cosine.astype(BF16)
                for chan in range(CHAN):
                    total = jnp.sum(sine * columns[chan], axis=0, keepdims=True)
                    kept.append(jnp.where(sublane == inner, total, sums[2 * half + chan]))
            return tuple(kept)

        sums = lax.fori_loop(0, 8, one_block, (jnp.zeros((8, 128), F32),) * 4)
        for half in range(2):
            for chan in range(CHAN):
                start = pl.multiple_of(chan * ROWS + index * 8, 8)
                filt[pl.ds(start, 8), half * 128 : half * 128 + 128] = sums[2 * half + chan]
        return carry

    lax.fori_loop(0, 8, chunk, 0)
    position = (
        lax.broadcasted_iota(jnp.int32, (ROWS, COLS), 0) * COLS
        + lax.broadcasted_iota(jnp.int32, (ROWS, COLS), 1)
    ).astype(F32)
    signals = []
    for chan in range(CHAN):
        rate = decay[first + 64 * chan]
        envelope = jnp.exp(-(rate * position) * (1.0 / TOTAL)) * norm[first + 64 * chan]
        env_out[chan * ROWS : (chan + 1) * ROWS, :] = envelope
        signals.append((filt[chan * ROWS : (chan + 1) * ROWS, :] * envelope).astype(BF16))
    spec_out[...] = spectrum(signals, forward[...], twiddle[0], twiddle[1], full[0], full[1])


def own_taps(first, short, taps, order):
    lane = lax.broadcasted_iota(jnp.int32, (8, 128), 1)
    taps[...] = jnp.where(lane == 0, 1.0, 0.0)
    for place, which in order:
        for chan in range(CHAN):
            taps[place + chan : place + chan + 1, 0:TAPS] = short[which, pl.ds(first + 64 * chan, 1), :]
    return taps[...]


def gradient_kernel(
    own,
    arrived,
    short,
    act,
    cosine,
    envelope,
    columns,
    back,
    back_turn,
    place,
    forward,
    last,
    twiddle,
    full,
    feat_out,
    spec_out,
    signal_out,
    proj_out,
    basis_out,
    taps,
    raw,
    raw_turned,
    part,
    product,
    proj_product,
):
    first = own[0]
    weights = own_taps(first, short, taps, ((0, 0), (2, 1), (4, 2)))
    signal = arrived[...].astype(F32)
    lane = lax.broadcasted_iota(jnp.int32, (ROWS, 8, COLS), 2)
    result = weights[None, :, 0:1] * signal
    zeros = jnp.zeros((1, 8, COLS), F32)
    for offset in range(1, TAPS):
        moved = pltpu.roll(signal, offset, 2)
        before = jnp.concatenate([zeros, moved[:-1]], axis=0)
        shifted = jnp.where(lane < offset, before, moved)
        result = result + weights[None, :, offset : offset + 1] * shifted
    fill(feat_out, result)

    def plane(index):
        return take(feat_out, index, ROWS, 8)

    signals = []
    for chan in range(CHAN):
        signals.append((plane(2 + chan) * plane(4 + chan)).astype(BF16))
    for chan in range(CHAN):
        signals.append((plane(chan) * plane(6 + chan)).astype(BF16))
    for index in range(4):
        signal_out[index] = signals[index].astype(F32)
    tables = (twiddle[0], twiddle[1], full[0], full[1])
    spec = spectrum(signals, forward[...], *tables)
    spec_out[...] = spec
    carried, grad = spec[: CHAN * ROWS], spec[CHAN * ROWS :]
    carried_re, carried_im = carried[:, :COLS], carried[:, COLS:]
    grad_re, grad_im = grad[:, :COLS], grad[:, COLS:]
    crossed = jnp.concatenate(
        [
            carried_re * grad_re + carried_im * grad_im,
            carried_im * grad_re - carried_re * grad_im,
        ],
        axis=1,
    )
    filter_grad = restore(crossed, CHAN, last[...], *tables)
    for chan in range(CHAN):
        rounded = filter_grad[chan].astype(BF16).astype(F32)
        scaled = rounded * envelope[chan * ROWS : (chan + 1) * ROWS, :]
        for half in range(2):
            raw[half, chan * ROWS : (chan + 1) * ROWS, :] = scaled[:, half * 128 : half * 128 + 128]
    raw_hi, raw_lo = split(jnp.concatenate([raw[half].T for half in range(2)], axis=0))
    raw_turned[:, 0:128] = raw_hi
    raw_turned[:, 128:256] = raw_lo
    column0 = columns[0:FEAT, :]
    column1 = columns[FEAT : 2 * FEAT, :]
    wide_lane = lax.broadcasted_iota(jnp.int32, (FEAT, COLS), 1) % ROWS

    def chunk(index, carry):
        base = pl.multiple_of(index * 512, 512)

        def one_block(inner, carry):
            near = pl.multiple_of(inner * FEAT, FEAT)
            block = index * 8 + inner
            for half in range(2):
                lanes = slice(half * 128, half * 128 + 128)
                value = (
                    column0 * raw[half, pl.ds(block, 1), :]
                    + column1 * raw[half, pl.ds(ROWS + block, 1), :]
                )
                value = value * cosine[pl.ds(base + near, FEAT), lanes].astype(F32)
                part[pl.ds(near, FEAT), lanes] = value.astype(BF16)
            return carry

        lax.fori_loop(0, 8, one_block, 0)
        product[...] = dot(part[...], back[...])
        proj_product[...] = dot(act[pl.ds(base, 512), :], raw_turned[...])

        def gather(inner, carry):
            basis_sum, proj_sum = carry
            near = pl.multiple_of(inner * FEAT, FEAT)
            block = index * 8 + inner
            angle = back_turn[pl.ds(block, 1), :]
            both = product[pl.ds(near, FEAT), 0:128] + product[pl.ds(near, FEAT), 128:256]
            basis_sum = basis_sum + both * angle
            proj_sum = proj_sum + jnp.where(
                wide_lane == block, proj_product[pl.ds(near, FEAT), :], 0.0
            )
            return basis_sum, proj_sum

        return lax.fori_loop(0, 8, gather, carry)

    basis_sum, proj_sum = lax.fori_loop(
        0, 8, chunk, (jnp.zeros((FEAT, 128), F32), jnp.zeros((FEAT, COLS), F32))
    )
    proj_both = proj_sum[:, 0:128] + proj_sum[:, 128:256]
    lane128 = lax.broadcasted_iota(jnp.int32, (FEAT, 128), 1)
    stacked = jnp.concatenate(
        [
            jnp.where(lane128 < ROWS, proj_both, 0.0),
            jnp.where(lane128 >= ROWS, proj_both, 0.0),
        ],
        axis=0,
    )
    proj_out[...] = lax.dot_general(
        jnp.ones((8, 128), F32),
        stacked,
        (((1,), (1,)), ((), ())),
        precision=EXACT,
        preferred_element_type=F32,
    )
    pieces = [
        lax.dot_general(
            place[group],
            basis_sum,
            (((1,), (1,)), ((), ())),
            precision=EXACT,
            preferred_element_type=F32,
        )
        for group in range(8)
    ]
    for core in range(2):
        row = jnp.concatenate([piece[:, core * 32 : core * 32 + 32] for piece in pieces], axis=1)
        for peer in range(8):
            basis_out[core * 8 + peer] = row


def output_kernel(
    own,
    skip,
    short,
    feat,
    spec,
    filter_spec,
    signals,
    proj_row,
    basis_parts,
    last,
    twiddle,
    full,
    out,
    taps,
    mate,
):
    first = own[0]
    weights = own_taps(first, short, taps, ((2, 2), (4, 1), (6, 0)))
    tables = (twiddle[0], twiddle[1], full[0], full[1])
    carried, grad = spec[0 : CHAN * ROWS, :], spec[CHAN * ROWS : 2 * CHAN * ROWS, :]
    filt = filter_spec[...]
    carried_re, carried_im = carried[:, :COLS], carried[:, COLS:]
    grad_re, grad_im = grad[:, :COLS], grad[:, COLS:]
    filt_re, filt_im = filt[:, :COLS], filt[:, COLS:]
    crossed = jnp.concatenate(
        [
            jnp.concatenate(
                [
                    filt_re * carried_re - filt_im * carried_im,
                    -(filt_re * carried_im + filt_im * carried_re),
                ],
                axis=1,
            ),
            jnp.concatenate(
                [
                    filt_re * grad_re + filt_im * grad_im,
                    filt_im * grad_re - filt_re * grad_im,
                ],
                axis=1,
            ),
        ],
        axis=0,
    )
    sums = restore(crossed, 2 * CHAN, last[...], *tables)
    for chan in range(CHAN):
        gain = skip[first + 64 * chan]
        long_out = (sums[chan] + gain * signals[chan]).astype(BF16).astype(F32)
        carried_grad = (sums[CHAN + chan] + gain * signals[CHAN + chan]).astype(BF16).astype(F32)
        put(mate, chan, ROWS, 8, long_out)
        put(mate, 2 + chan, ROWS, 8, carried_grad)
        put(mate, 4 + chan, ROWS, 8, carried_grad)
        put(mate, 6 + chan, ROWS, 8, long_out)
    signal = jnp.concatenate(
        [(feat[half] * mate[half]).astype(BF16).astype(F32).reshape(ROWS, 8, 128) for half in range(2)],
        axis=2,
    )
    lane = lax.broadcasted_iota(jnp.int32, (ROWS, 8, COLS), 2)
    result = weights[None, :, 0:1] * signal
    zeros = jnp.zeros((1, 8, COLS), F32)
    for offset in range(1, TAPS):
        moved = pltpu.roll(signal, COLS - offset, 2)
        after = jnp.concatenate([moved[1:], zeros], axis=0)
        shifted = jnp.where(lane >= COLS - offset, after, moved)
        result = result + weights[None, :, offset : offset + 1] * shifted
    basis = basis_parts[0]
    for source in range(1, 16):
        basis = basis + basis_parts[source]
    proj_wide = proj_row[...]
    proj_hi = proj_wide.astype(BF16).astype(F32)
    proj_lo = proj_wide - proj_hi
    row = lax.broadcasted_iota(jnp.int32, (8, COLS), 0)
    extra = jnp.where(row == 7, jnp.concatenate([proj_hi, proj_lo], axis=1), basis)
    wide = jnp.concatenate([result, jnp.broadcast_to(extra[None], (ROWS, 8, COLS))], axis=1)
    out[...] = wide.astype(BF16)


def unpack_kernel(arrived, mixed, grad_query, grad_key, grad_value, proj, basis, wide):
    fill(wide, arrived[...].astype(F32))
    for ref, start in ((mixed, 0), (grad_value, 2), (grad_key, 4), (grad_query, 6)):
        for chan in range(CHAN):
            ref[chan * ROWS : (chan + 1) * ROWS, :] = take(wide, start + chan, ROWS, 16).astype(BF16)
    last = take(wide, 15, ROWS, 16)
    both = (last[:, 0:128] + last[:, 128:256]) * (1.0 / math.sqrt(TOTAL))
    proj[0:ROWS, :] = both[:, 0:64]
    proj[ROWS : 2 * ROWS, :] = both[:, 64:128]
    for core in range(2):
        for half in range(2):
            total = wide[half, core * 16 + 8 : core * 16 + 16, :]
            for source in range(core + 2, ROWS, 2):
                total = total + wide[half, source * 16 + 8 : source * 16 + 16, :]
            basis[core, :, half * 128 : half * 128 + 128] = total


SMEM = pl.BlockSpec(memory_space=pltpu.SMEM)
VMEM = pl.BlockSpec(memory_space=pltpu.VMEM)


def call(kernel, name, scalars, args, outs, scratch, flops, moved):
    return pl.pallas_call(
        kernel,
        name=name,
        in_specs=[SMEM] * len(scalars) + [VMEM] * len(args),
        out_specs=[VMEM] * len(outs) if isinstance(outs, list) else VMEM,
        out_shape=outs,
        scratch_shapes=scratch,
        compiler_params=pltpu.CompilerParams(vmem_limit_bytes=48 * 1024 * 1024),
        cost_estimate=pl.CostEstimate(flops=flops, bytes_accessed=moved, transcendentals=0),
    )(*scalars, *args)


def shape(dims, kind=F32):
    return jax.ShapeDtypeStruct(dims, kind)


def run_pack(query_in, key_in, value_in, grad_out):
    return call(
        pack_kernel,
        "pack",
        [],
        [query_in, key_in, value_in, grad_out],
        shape((ROWS, 8, COLS), BF16),
        [pltpu.VMEM((2, 512, 128), F32)],
        1 << 20,
        1 << 19,
    )


def run_filter(own, decay, norm, layer, proj, consts):
    return call(
        filter_kernel,
        "filter",
        [own, decay, norm],
        [layer, proj, consts["pick"], consts["turn"], consts["right"], consts["forward"], consts["twiddle"], consts["full"]],
        [
            shape((ROWS * FEAT, COLS), BF16),
            shape((ROWS * FEAT, COLS), BF16),
            shape((CHAN * ROWS, COLS)),
            shape((CHAN * ROWS, 2 * COLS)),
            shape((CHAN * FEAT, 128)),
        ],
        [
            pltpu.VMEM((ROWS * FEAT, COLS), BF16),
            pltpu.VMEM((512, COLS), F32),
            pltpu.VMEM((CHAN * ROWS, COLS), F32),
        ],
        1 << 33,
        1 << 23,
    )


def run_gradient(own, arrived, short, act, cosine, envelope, columns, consts):
    return call(
        gradient_kernel,
        "gradient",
        [own],
        [arrived, short, act, cosine, envelope, columns, consts["back"], consts["back_turn"], consts["place"], consts["forward"], consts["last"], consts["twiddle"], consts["full"]],
        [
            shape((2, ROWS * 8, 128)),
            shape((2 * CHAN * ROWS, 2 * COLS)),
            shape((2 * CHAN, ROWS, COLS)),
            shape((8, 128)),
            shape((16, 8, COLS)),
        ],
        [
            pltpu.VMEM((8, 128), F32),
            pltpu.VMEM((2, CHAN * ROWS, 128), F32),
            pltpu.VMEM((COLS, COLS), BF16),
            pltpu.VMEM((512, COLS), BF16),
            pltpu.VMEM((512, COLS), F32),
            pltpu.VMEM((512, COLS), F32),
        ],
        1 << 32,
        1 << 23,
    )


def run_output(own, skip, short, feat, spec, filter_spec, signals, proj_row, basis_parts, consts):
    return call(
        output_kernel,
        "output",
        [own, skip],
        [short, feat, spec, filter_spec, signals, proj_row, basis_parts, consts["last"], consts["twiddle"], consts["full"]],
        shape((ROWS, 16, COLS), BF16),
        [pltpu.VMEM((8, 128), F32), pltpu.VMEM((2, ROWS * 8, 128), F32)],
        1 << 31,
        1 << 22,
    )


def run_unpack(arrived):
    block = shape((128, COLS), BF16)
    return call(
        unpack_kernel,
        "unpack",
        [],
        [arrived],
        [block, block, block, block, shape((128, FEAT)), shape((2, 8, COLS))],
        [pltpu.VMEM((2, ROWS * 16, 128), F32)],
        1 << 20,
        1 << 20,
    )


def make_consts():
    forward, last, twiddle, full = transform_tables()
    right, turn, pick, back, back_turn, place = basis_tables()
    return dict(
        forward=jnp.asarray(forward),
        last=jnp.asarray(last),
        twiddle=jnp.asarray(twiddle),
        full=jnp.asarray(full),
        right=jnp.asarray(right),
        turn=jnp.asarray(turn),
        pick=jnp.asarray(pick),
        back=jnp.asarray(back),
        back_turn=jnp.asarray(back_turn),
        place=jnp.asarray(place),
    )


def filter_params(basis_weight, basis_bias, decay_rate):
    energy = jnp.expm1(-2.0 * decay_rate) / jnp.expm1(-2.0 * decay_rate / TOTAL)
    norm = 1.0 / jnp.sqrt(energy)
    layer = jnp.pad(
        jnp.concatenate([basis_weight, basis_bias[:, None]], axis=1), ((0, 0), (0, 128 - EMB - 1))
    )
    return norm, layer


CTX = ("zh", "y", "core")
PAIR = ("core", "x", "zl")


def exchange(value, axes):
    return lax.all_to_all(value, axes, split_axis=0, concat_axis=0, tiled=True)


def on_device(
    query_in,
    key_in,
    value_in,
    short_kernel,
    basis_weight,
    basis_bias,
    filter_proj,
    decay_rate,
    skip_gain,
    grad_out,
):
    consts = make_consts()
    own = lax.axis_index(CTX).astype(jnp.int32).reshape(1)
    with jax.named_scope("spread"):
        arrived = exchange(run_pack(query_in, key_in, value_in, grad_out), CTX)
    norm, layer = filter_params(basis_weight, basis_bias, decay_rate)
    act, cosine, envelope, filter_spec, columns = run_filter(
        own, decay_rate, norm, layer, filter_proj, consts
    )
    feat, spec, signals, proj_row, basis_own = run_gradient(
        own, arrived, short_kernel, act, cosine, envelope, columns, consts
    )
    with jax.named_scope("basis"):
        basis_parts = exchange(basis_own, PAIR)
    packed = run_output(
        own, skip_gain, short_kernel, feat, spec, filter_spec, signals, proj_row, basis_parts, consts
    )
    with jax.named_scope("collect"):
        returned = exchange(packed, CTX)
    mixed, grad_query, grad_key, grad_value, grad_proj, basis_sum = run_unpack(returned)
    grad_basis = (
        basis_sum.reshape(2, 8, 8, 32).transpose(0, 3, 1, 2).reshape(FEAT, 64)[:, :EMB]
        * math.sqrt(FEAT / (TOTAL * 1024))
    )
    return (mixed, grad_query, grad_key, grad_value, grad_proj, grad_basis)


def solution(mesh):
    finer = Mesh(mesh.devices.reshape(4, 8, 2, 4, 2), ("zh", "y", "core", "x", "zl"))
    rows = ("x", "zl")
    block = P(rows, CTX)
    return jax.shard_map(
        on_device,
        mesh=finer,
        in_specs=(
            block,
            block,
            block,
            P(None, rows, None),
            P(),
            P(),
            P(rows, None),
            P(rows),
            P(rows),
            block,
        ),
        out_specs=(block, block, block, block, P(rows, None), P()),
        check_vma=False,
    )
```

```python
import math

import jax
import jax.numpy as jnp
import numpy as np
from jax import lax
from jax.experimental import pallas as pl
from jax.experimental.pallas import tpu as pltpu
from jax.sharding import Mesh
from jax.sharding import PartitionSpec as P
import ml_dtypes

F32 = jnp.float32
BF16 = jnp.bfloat16
EXACT = lax.Precision.HIGHEST

ROWS = 64
COLS = 256
TOTAL = ROWS * COLS
FEAT = 64
EMB = 33
TAPS = 7
CHAN = 2
GROUP = 40
TURN = 1.0 / (2.0 * math.pi)

SIN_COEF = (
    4.442883014678955,
    -7.308245658874512,
    3.606354236602783,
    -0.8461116552352905,
    0.1098245158791542,
)
COS_COEF = (
    1.4142135381698608,
    -6.978850841522217,
    5.739460468292236,
    -1.883557915687561,
    0.3106880187988281,
)


def halves(table, count):
    parts = []
    rest = np.asarray(table, np.float64)
    for _ in range(count):
        part = rest.astype(np.float32).astype(ml_dtypes.bfloat16)
        parts.append(part)
        rest = rest - part.astype(np.float64)
    return parts


def transform_tables():
    rows = np.arange(ROWS)
    cols = np.arange(COLS)
    first = 2.0 * np.pi * ((4 * rows[:, None] + 1) * rows[None, :] % (4 * ROWS)) / (4 * ROWS)
    first_re, first_im = np.cos(first), -np.sin(first)
    forward = np.concatenate([first_re, first_im], axis=0)
    forward_cat = np.concatenate(halves(forward, 2), axis=1)
    last = np.concatenate([first_re.T, -first_im.T], axis=1) / TOTAL
    last_hi, last_lo = halves(last, 2)
    last_cat = np.concatenate([last_hi, last_lo, last_hi], axis=1)
    turn = 2.0 * np.pi * ((4 * rows[:, None] + 1) * cols[None, :]) / (4 * TOTAL)
    twiddle = np.stack([np.cos(turn), -np.sin(turn)]).astype(np.float32)
    inner = 2.0 * np.pi * (cols[:, None] * cols[None, :] % COLS) / COLS
    inner_re, inner_im = np.cos(inner), -np.sin(inner)
    full = np.concatenate(
        [
            np.concatenate([inner_re, inner_im], axis=1),
            np.concatenate([-inner_im, inner_re], axis=1),
        ],
        axis=0,
    )
    full_hi, full_lo = halves(full, 2)
    return forward_cat, last_cat, twiddle, np.stack([full_hi, full_lo])


def basis_tables():
    freq = np.arange(1, 17)
    cols = np.arange(COLS)
    rows = np.arange(ROWS)
    inner = 2.0 * np.pi * (freq[:, None] * cols[None, :] % TOTAL) / TOTAL
    short = np.concatenate(
        [np.cos(inner), np.sin(inner), cols[None, :] / TOTAL, np.ones((1, COLS))], axis=0
    )
    width = short.shape[0]
    hi, mid, lo = halves(short, 3)
    right = np.zeros((256, COLS), ml_dtypes.bfloat16)
    for place, part in ((0, hi), (GROUP, hi), (2 * GROUP, hi)):
        right[place : place + width] = part
    for place, part in ((128, mid), (128 + GROUP, lo), (128 + 2 * GROUP, mid)):
        right[place : place + width] = part
    outer = 2.0 * np.pi * (freq[None, :] * rows[:, None] % ROWS) / ROWS
    cos_out, sin_out = np.cos(outer), np.sin(outer)
    one = np.ones((ROWS, 1))
    block = rows[:, None] / ROWS
    cos_row = np.concatenate([cos_out, cos_out, one, one], axis=1)
    sin_row = np.concatenate([sin_out, sin_out, 0 * one, block], axis=1)
    turn = np.zeros((2, ROWS, 128), np.float32)
    for place in (0, GROUP, 2 * GROUP):
        turn[0, :, place : place + width] = cos_row
        turn[1, :, place : place + width] = sin_row
    pick = np.zeros((2, 128, 128), np.float32)
    for place in (0, GROUP, 2 * GROUP):
        for index in range(16):
            pick[0, 2 * index + 1, place + index] = 1.0
            pick[0, 2 * index + 2, place + 16 + index] = 1.0
            pick[1, 2 * index + 2, place + index] = 1.0
            pick[1, 2 * index + 1, place + 16 + index] = -1.0
        pick[0, 0, place + 32] = 1.0
        pick[0, EMB, place + 33] = 1.0
        pick[1, 0, place + 33] = 1.0
    back = np.zeros((COLS, 128))
    back[:, :width] = short.T
    back[:, 64:80] = short[16:32].T
    back[:, 80:96] = short[:16].T
    back_hi, back_lo = halves(back, 2)
    back_cat = np.concatenate([back_hi, back_lo], axis=1)
    back_turn = np.zeros((ROWS, 128), np.float32)
    back_turn[:, :32] = cos_row[:, :32]
    back_turn[:, 32] = 1.0
    back_turn[:, 33] = rows / ROWS
    back_turn[:, 64:80] = -sin_out
    back_turn[:, 80:96] = sin_out
    place = np.zeros((8, 8, 128), np.float32)
    for wanted in range(EMB):
        row, group = divmod(wanted, 8)
        if wanted == 0:
            lanes = (32, 33)
        elif wanted % 2:
            lanes = ((wanted - 1) // 2, 64 + (wanted - 1) // 2)
        else:
            lanes = (16 + (wanted - 2) // 2, 80 + (wanted - 2) // 2)
        for lane in lanes:
            place[group, row, lane] = 1.0
    return right, turn, pick, back_cat, back_turn, place


def split(value):
    hi = value.astype(BF16)
    lo = (value - hi.astype(F32)).astype(BF16)
    return hi, lo


def dot(left, right):
    return jnp.dot(left, right, preferred_element_type=F32)


def spectrum(signals, forward, twiddle_re, twiddle_im, full_hi, full_lo):
    wide = jnp.concatenate(signals, axis=1)
    section = dot(forward, jnp.concatenate([wide, wide], axis=0))
    turned = []
    for index in range(len(signals)):
        part = section[:, index * COLS : (index + 1) * COLS]
        part_re, part_im = part[:ROWS], part[ROWS:]
        turned.append(
            jnp.concatenate(
                [
                    part_re * twiddle_re - part_im * twiddle_im,
                    part_re * twiddle_im + part_im * twiddle_re,
                ],
                axis=1,
            )
        )
    return full_product(jnp.concatenate(turned, axis=0), full_hi, full_lo)


def full_product(value, full_hi, full_lo):
    hi, lo = split(value)
    return dot(hi, full_hi) + dot(lo, full_hi) + dot(hi, full_lo)


def restore(conj_spec, count, last, twiddle_re, twiddle_im, full_hi, full_lo):
    back = full_product(conj_spec, full_hi, full_lo)
    stacked = []
    for index in range(count):
        part = back[index * ROWS : (index + 1) * ROWS]
        part_re, part_im = part[:, :COLS], part[:, COLS:]
        stacked.append(
            jnp.concatenate(
                [
                    part_re * twiddle_re - part_im * twiddle_im,
                    part_re * twiddle_im + part_im * twiddle_re,
                ],
                axis=0,
            )
        )
    hi, lo = split(jnp.concatenate(stacked, axis=1))
    result = dot(last, jnp.concatenate([hi, hi, lo], axis=0))
    return [result[:, index * COLS : (index + 1) * COLS] for index in range(count)]


def take(ref, start, count, stride):
    return jnp.concatenate(
        [ref[half, pl.ds(start, count, stride=stride), :] for half in range(2)], axis=1
    )


def put(ref, start, count, stride, value):
    for half in range(2):
        ref[half, pl.ds(start, count, stride=stride), :] = value[:, half * 128 : half * 128 + 128]


def fill(ref, value):
    for half in range(2):
        ref[half] = value[..., half * 128 : half * 128 + 128].reshape(ref.shape[1], 128)


def begin(sems, pairs):
    copies = [
        pltpu.make_async_copy(source, target, sems.at[index])
        for index, (source, target) in enumerate(pairs)
    ]
    for copy in copies:
        copy.start()
    return copies


def picked(row, wanted):
    lane = lax.broadcasted_iota(jnp.int32, row.shape, 1)
    return jnp.sum(jnp.where(lane == wanted, row, 0.0), axis=1, keepdims=True)


def pack_kernel(query, key, value, grad, out, held, wide, sems):
    copies = begin(sems, [(ref, held.at[index]) for index, ref in enumerate((query, key, value, grad))])
    for index in range(4):
        copies[index].wait()
        block = held[index].astype(F32)
        for half in range(2):
            wide[half, index * 128 : (index + 1) * 128, :] = block[:, half * 128 : half * 128 + 128]
    for peer in range(ROWS):
        out[peer] = take(wide, peer, 8, ROWS).astype(BF16)


def expm1_small(value):
    series = jnp.ones_like(value)
    for order in range(9, 1, -1):
        series = 1.0 + value * series * (1.0 / order)
    return jnp.where(value > -0.5, value * series, jnp.exp(value) - 1.0)


def filter_kernel(
    own,
    weight_src,
    bias_src,
    proj_src,
    decay_src,
    pick_src,
    turn_src,
    right_src,
    forward_src,
    twiddle_src,
    full_src,
    act_out,
    cos_out,
    env_out,
    spec_out,
    column_out,
    weight,
    bias,
    proj,
    decay,
    pick,
    turn,
    right,
    forward,
    twiddle,
    full,
    layer,
    left,
    phase,
    filt,
    act,
    cosv,
    out_sems,
    sems,
):
    first = own[0]
    copies = begin(
        sems,
        [
            (weight_src, weight),
            (bias_src, bias),
            (pick_src, pick),
            (proj_src, proj),
            (turn_src, turn),
            (right_src, right),
            (decay_src, decay),
            (forward_src, forward),
            (twiddle_src, twiddle),
            (full_src, full),
        ],
    )
    layer[...] = jnp.zeros((128, 128), F32)
    for copy in copies[:3]:
        copy.wait()
    layer[0:EMB, 0:FEAT] = weight[...]
    layer[EMB : EMB + 1, 0:FEAT] = bias[...]
    layer_all = layer[...].T[0:FEAT, :]
    same = jnp.dot(layer_all, pick[0], precision=EXACT, preferred_element_type=F32) * TURN
    cross = jnp.dot(layer_all, pick[1], precision=EXACT, preferred_element_type=F32) * TURN
    lane = lax.broadcasted_iota(jnp.int32, (FEAT, 128), 1)
    sublane = lax.broadcasted_iota(jnp.int32, (8, 128), 0)
    for copy in copies[3:7]:
        copy.wait()
    columns = []
    for chan in range(CHAN):
        hit = lane == first + 64 * chan
        column = jnp.sum(jnp.where(hit, proj[...], 0.0), axis=1, keepdims=True)
        column_wide = jnp.broadcast_to(column, (FEAT, 128))
        column_out[chan * FEAT : (chan + 1) * FEAT, :] = column_wide
        columns.append(column_wide)

    def make_left(block, carry):
        value = same * turn[0, pl.ds(block, 1), :] + cross * turn[1, pl.ds(block, 1), :]
        hi = value.astype(BF16).astype(F32)
        rest = value - hi
        mid = rest.astype(BF16).astype(F32)
        lo = rest - mid
        one = jnp.where(lane < GROUP, hi, jnp.where(lane < 2 * GROUP, mid, lo))
        two = jnp.where(lane < 2 * GROUP, hi, mid)
        start = pl.multiple_of(block * FEAT, FEAT)
        left[pl.ds(start, FEAT), 0:128] = one.astype(BF16)
        left[pl.ds(start, FEAT), 128:256] = two.astype(BF16)
        return carry

    lax.fori_loop(0, ROWS, make_left, 0, unroll=4)

    def chunk(index, carry):
        base = pl.multiple_of(index * 512, 512)
        phase[...] = dot(left[pl.ds(base, 512), :], right[...])
        for half in range(2):
            lanes = slice(half * 128, half * 128 + 128)
            sums = [jnp.zeros((8, 128), F32)] * CHAN
            for inner in range(8):
                near = inner * FEAT
                turns = phase[near : near + FEAT, lanes]
                rest = turns - jnp.round(turns)
                square = rest * rest
                sine = SIN_COEF[-1] * square + SIN_COEF[-2]
                cosine = COS_COEF[-1] * square + COS_COEF[-2]
                for coef in SIN_COEF[-3::-1]:
                    sine = sine * square + coef
                for coef in COS_COEF[-3::-1]:
                    cosine = cosine * square + coef
                sine = sine * rest
                whole_sine = sine * cosine
                whole_cosine = 1.0 - sine * sine
                act[pl.ds(base + near, FEAT), lanes] = whole_sine.astype(BF16)
                cosv[pl.ds(base + near, FEAT), lanes] = whole_cosine.astype(BF16)
                for chan in range(CHAN):
                    total = jnp.sum(whole_sine * columns[chan], axis=0, keepdims=True)
                    sums[chan] = jnp.where(sublane == inner, total, sums[chan])
            for chan in range(CHAN):
                start = pl.multiple_of(chan * ROWS + index * 8, 8)
                filt[pl.ds(start, 8), lanes] = sums[chan]
        send(index, 0).start()
        send(index, 1).start()
        return carry

    def send(index, which):
        rows = pl.ds(pl.multiple_of(index * 512, 512), 512)
        source, target = ((act, act_out), (cosv, cos_out))[which]
        return pltpu.make_async_copy(source.at[rows], target.at[rows], out_sems.at[which, index])

    lax.fori_loop(0, 8, chunk, 0)
    ratio = decay[...] * (1.0 / TOTAL)
    energy = expm1_small(-2.0 * decay[...]) / expm1_small(-2.0 * ratio)
    norm = 1.0 / jnp.sqrt(energy)
    for copy in copies[7:]:
        copy.wait()
    position = (
        lax.broadcasted_iota(jnp.int32, (ROWS, COLS), 0) * COLS
        + lax.broadcasted_iota(jnp.int32, (ROWS, COLS), 1)
    ).astype(F32)
    signals = []
    for chan in range(CHAN):
        rate = picked(decay[...], first + 64 * chan)
        envelope = jnp.exp(-(rate * position) * (1.0 / TOTAL)) * picked(norm, first + 64 * chan)
        env_out[chan * ROWS : (chan + 1) * ROWS, :] = envelope
        signals.append((filt[chan * ROWS : (chan + 1) * ROWS, :] * envelope).astype(BF16))
    spec_out[...] = spectrum(signals, forward[...], twiddle[0], twiddle[1], full[0], full[1])
    for index in range(8):
        send(index, 0).wait()
        send(index, 1).wait()


def own_taps(first, short, taps, order):
    row = lax.broadcasted_iota(jnp.int32, (TAPS, 128), 0)
    lane = lax.broadcasted_iota(jnp.int32, (TAPS, 128), 1)
    columns = jnp.where(row == 0, 1.0, 0.0)
    for place, which in order:
        for chan in range(CHAN):
            hit = lane == first + 64 * chan
            column = jnp.sum(jnp.where(hit, short[which], 0.0), axis=1, keepdims=True)
            columns = jnp.where(lane == place + chan, column, columns)
    taps[...] = jnp.zeros((128, 128), F32)
    taps[0:TAPS, :] = columns
    return taps[...].T[0:8, :]


def gradient_kernel(
    own,
    arrived_src,
    act_src,
    cosine_src,
    envelope_src,
    columns_src,
    short_src,
    back_src,
    back_turn_src,
    place_src,
    forward_src,
    last_src,
    twiddle_src,
    full_src,
    feat_out,
    spec_out,
    signal_out,
    proj_out,
    basis_out,
    arrived,
    act,
    cosine,
    envelope,
    columns,
    short,
    back,
    back_turn,
    place,
    forward,
    last,
    twiddle,
    full,
    taps,
    raw,
    feat,
    spec,
    kept,
    out_sems,
    sems,
):
    first = own[0]
    copies = begin(
        sems,
        [
            (short_src, short),
            (arrived_src, arrived),
            (forward_src, forward),
            (twiddle_src, twiddle),
            (full_src, full),
            (last_src, last),
            (envelope_src, envelope),
            (cosine_src, cosine),
            (act_src, act),
            (columns_src, columns),
            (back_src, back),
            (back_turn_src, back_turn),
            (place_src, place),
        ],
    )
    copies[0].wait()
    weights = own_taps(first, short, taps, ((0, 0), (2, 1), (4, 2)))
    copies[1].wait()
    signal = arrived[...].astype(F32)
    lane = lax.broadcasted_iota(jnp.int32, (ROWS, 8, COLS), 2)
    result = weights[None, :, 0:1] * signal
    zeros = jnp.zeros((1, 8, COLS), F32)
    for offset in range(1, TAPS):
        moved = pltpu.roll(signal, offset, 2)
        before = jnp.concatenate([zeros, moved[:-1]], axis=0)
        shifted = jnp.where(lane < offset, before, moved)
        result = result + weights[None, :, offset : offset + 1] * shifted
    fill(feat, result)
    leaving = begin(out_sems.at[pl.ds(0, 1)], [(feat, feat_out)])

    def plane(index):
        return take(feat, index, ROWS, 8)

    signals = []
    for chan in range(CHAN):
        signals.append((plane(2 + chan) * plane(4 + chan)).astype(BF16))
    for chan in range(CHAN):
        signals.append((plane(chan) * plane(6 + chan)).astype(BF16))
    for index in range(4):
        kept[index] = signals[index].astype(F32)
    leaving += begin(out_sems.at[pl.ds(1, 1)], [(kept, signal_out)])
    for copy in copies[2:5]:
        copy.wait()
    tables = (twiddle[0], twiddle[1], full[0], full[1])
    spec_all = spectrum(signals, forward[...], *tables)
    spec[...] = spec_all
    leaving += begin(out_sems.at[pl.ds(2, 1)], [(spec, spec_out)])
    carried, grad = spec_all[: CHAN * ROWS], spec_all[CHAN * ROWS :]
    carried_re, carried_im = carried[:, :COLS], carried[:, COLS:]
    grad_re, grad_im = grad[:, :COLS], grad[:, COLS:]
    crossed = jnp.concatenate(
        [
            carried_re * grad_re + carried_im * grad_im,
            carried_im * grad_re - carried_re * grad_im,
        ],
        axis=1,
    )
    for copy in copies[5:7]:
        copy.wait()
    filter_grad = restore(crossed, CHAN, last[...], *tables)
    for chan in range(CHAN):
        rounded = filter_grad[chan].astype(BF16).astype(F32)
        scaled = rounded * envelope[chan * ROWS : (chan + 1) * ROWS, :]
        for half in range(2):
            raw[half, chan * ROWS : (chan + 1) * ROWS, :] = scaled[:, half * 128 : half * 128 + 128]
    for copy in copies[7:]:
        copy.wait()
    column0 = columns[0:FEAT, :]
    column1 = columns[FEAT : 2 * FEAT, :]
    lane128 = lax.broadcasted_iota(jnp.int32, (FEAT, 128), 1)
    row_lane = lane128 % 8
    back_all = back[...]

    def chunk(index, carry):
        basis_sum, proj_sum = carry
        base = pl.multiple_of(index * 512, 512)
        start = pl.multiple_of(index * 8, 8)
        rows = [
            [raw[half, pl.ds(chan * ROWS + start, 8), :] for half in range(2)] for chan in range(CHAN)
        ]
        wide = jnp.concatenate([jnp.concatenate(rows[chan], axis=1) for chan in range(CHAN)], axis=0)
        hi = wide.astype(BF16).astype(F32)
        packed = jnp.concatenate([hi, wide - hi, jnp.zeros((128 - 4 * 8, COLS), F32)], axis=0)
        turned = jnp.concatenate(
            [packed[:, half * 128 : half * 128 + 128].T for half in range(2)], axis=0
        ).astype(BF16)
        parts = []
        for inner in range(8):
            near = inner * FEAT
            pieces = []
            for half in range(2):
                lanes = slice(half * 128, half * 128 + 128)
                value = (
                    column0 * rows[0][half][inner : inner + 1, :]
                    + column1 * rows[1][half][inner : inner + 1, :]
                )
                value = value * cosine[pl.ds(base + near, FEAT), lanes].astype(F32)
                pieces.append(value.astype(BF16))
            parts.append(jnp.concatenate(pieces, axis=1))
        product = dot(jnp.concatenate(parts, axis=0), back_all)
        proj_product = dot(act[pl.ds(base, 512), :], turned)
        for inner in range(8):
            near = inner * FEAT
            angle = back_turn[pl.ds(start, 8), :][inner : inner + 1, :]
            both = product[near : near + FEAT, 0:128] + product[near : near + FEAT, 128:256]
            basis_sum = basis_sum + both * angle
            proj_sum = proj_sum + jnp.where(
                row_lane == inner, proj_product[near : near + FEAT, :], 0.0
            )
        return basis_sum, proj_sum

    basis_sum, proj_sum = lax.fori_loop(
        0, 8, chunk, (jnp.zeros((FEAT, 128), F32), jnp.zeros((FEAT, 128), F32))
    )
    own_lane = lane128 % 16
    stacked = jnp.concatenate(
        [jnp.where(own_lane < 8, proj_sum, 0.0), jnp.where(own_lane >= 8, proj_sum, 0.0)], axis=0
    )
    proj_out[...] = lax.dot_general(
        jnp.ones((8, 128), F32),
        stacked,
        (((1,), (1,)), ((), ())),
        precision=EXACT,
        preferred_element_type=F32,
    )
    pieces = [
        lax.dot_general(
            place[group],
            basis_sum,
            (((1,), (1,)), ((), ())),
            precision=EXACT,
            preferred_element_type=F32,
        )
        for group in range(8)
    ]
    for core in range(2):
        row = jnp.concatenate([piece[:, core * 32 : core * 32 + 32] for piece in pieces], axis=1)
        for peer in range(8):
            basis_out[core * 8 + peer] = row
    for copy in leaving:
        copy.wait()


def output_kernel(
    own,
    feat_src,
    spec_src,
    filter_spec_src,
    signals_src,
    proj_row_src,
    basis_parts_src,
    skip_src,
    short_src,
    last_src,
    twiddle_src,
    full_src,
    out,
    feat,
    spec,
    filter_spec,
    signals,
    proj_row,
    basis_parts,
    skip,
    short,
    last,
    twiddle,
    full,
    taps,
    mate,
    sems,
):
    first = own[0]
    copies = begin(
        sems,
        [
            (spec_src, spec),
            (filter_spec_src, filter_spec),
            (full_src, full),
            (twiddle_src, twiddle),
            (last_src, last),
            (skip_src, skip),
            (short_src, short),
            (signals_src, signals),
            (feat_src, feat),
            (proj_row_src, proj_row),
            (basis_parts_src, basis_parts),
        ],
    )
    for copy in copies[0:5]:
        copy.wait()
    tables = (twiddle[0], twiddle[1], full[0], full[1])
    carried, grad = spec[0 : CHAN * ROWS, :], spec[CHAN * ROWS : 2 * CHAN * ROWS, :]
    filt = filter_spec[...]
    carried_re, carried_im = carried[:, :COLS], carried[:, COLS:]
    grad_re, grad_im = grad[:, :COLS], grad[:, COLS:]
    filt_re, filt_im = filt[:, :COLS], filt[:, COLS:]
    crossed = jnp.concatenate(
        [
            jnp.concatenate(
                [
                    filt_re * carried_re - filt_im * carried_im,
                    -(filt_re * carried_im + filt_im * carried_re),
                ],
                axis=1,
            ),
            jnp.concatenate(
                [
                    filt_re * grad_re + filt_im * grad_im,
                    filt_im * grad_re - filt_re * grad_im,
                ],
                axis=1,
            ),
        ],
        axis=0,
    )
    sums = restore(crossed, 2 * CHAN, last[...], *tables)
    for copy in copies[5:]:
        copy.wait()
    weights = own_taps(first, short, taps, ((2, 2), (4, 1), (6, 0)))
    for chan in range(CHAN):
        gain = picked(skip[...], first + 64 * chan)
        long_out = (sums[chan] + gain * signals[chan]).astype(BF16).astype(F32)
        carried_grad = (sums[CHAN + chan] + gain * signals[CHAN + chan]).astype(BF16).astype(F32)
        put(mate, chan, ROWS, 8, long_out)
        put(mate, 2 + chan, ROWS, 8, carried_grad)
        put(mate, 4 + chan, ROWS, 8, carried_grad)
        put(mate, 6 + chan, ROWS, 8, long_out)
    signal = jnp.concatenate(
        [(feat[half] * mate[half]).astype(BF16).astype(F32).reshape(ROWS, 8, 128) for half in range(2)],
        axis=2,
    )
    lane = lax.broadcasted_iota(jnp.int32, (ROWS, 8, COLS), 2)
    result = weights[None, :, 0:1] * signal
    zeros = jnp.zeros((1, 8, COLS), F32)
    for offset in range(1, TAPS):
        moved = pltpu.roll(signal, COLS - offset, 2)
        after = jnp.concatenate([moved[1:], zeros], axis=0)
        shifted = jnp.where(lane >= COLS - offset, after, moved)
        result = result + weights[None, :, offset : offset + 1] * shifted
    basis = basis_parts[0]
    for source in range(1, 16):
        basis = basis + basis_parts[source]
    proj_wide = proj_row[...]
    proj_hi = proj_wide.astype(BF16).astype(F32)
    proj_lo = proj_wide - proj_hi
    row = lax.broadcasted_iota(jnp.int32, (8, COLS), 0)
    extra = jnp.where(row == 7, jnp.concatenate([proj_hi, proj_lo], axis=1), basis)
    wide = jnp.concatenate([result, jnp.broadcast_to(extra[None], (ROWS, 8, COLS))], axis=1)
    out[...] = wide.astype(BF16)


def unpack_kernel(
    arrived, mixed, grad_query, grad_key, grad_value, proj, basis, wide, sorted_rows
):
    fill(wide, arrived[...].astype(F32))
    for ref, start in ((mixed, 0), (grad_value, 2), (grad_key, 4), (grad_query, 6)):
        for chan in range(CHAN):
            ref[chan * ROWS : (chan + 1) * ROWS, :] = take(wide, start + chan, ROWS, 16).astype(BF16)
    last = take(wide, 15, ROWS, 16)
    both = (last[:, 0:128] + last[:, 128:256]) * (1.0 / math.sqrt(TOTAL))
    both = jnp.concatenate([both, jnp.zeros_like(both)], axis=0).T
    proj[:, 0:ROWS] = both[0:FEAT, 0:ROWS]
    proj[:, ROWS : 2 * ROWS] = both[FEAT : 2 * FEAT, 0:ROWS]
    totals = []
    for core in range(2):
        pieces = []
        for half in range(2):
            total = wide[half, core * 16 + 8 : core * 16 + 16, :]
            for source in range(core + 2, ROWS, 2):
                total = total + wide[half, source * 16 + 8 : source * 16 + 16, :]
            pieces.append(total)
        totals.append(jnp.concatenate(pieces, axis=1))
    scale = math.sqrt(FEAT / (TOTAL * 1024))
    for group in range(8):
        lanes = slice(group * 32, group * 32 + 32)
        merged = jnp.concatenate(
            [totals[0][:, lanes], totals[1][:, lanes], jnp.zeros((8, 64), F32)], axis=1
        )
        sorted_rows[pl.ds(group, 8, stride=8), :] = merged * scale
    basis[...] = sorted_rows[0:EMB, 0:FEAT]


SMEM = pl.BlockSpec(memory_space=pltpu.SMEM)
VMEM = pl.BlockSpec(memory_space=pltpu.VMEM)
HBM = pl.BlockSpec(memory_space=pltpu.HBM)
LIMIT = 62 * 1024 * 1024


def call(kernel, name, own, near, far, outs, scratch, flops, moved, limit=LIMIT):
    landing = [pltpu.VMEM(value.shape, value.dtype) for value in far]
    return pl.pallas_call(
        kernel,
        name=name,
        in_specs=[SMEM] * len(own) + [VMEM] * len(near) + [HBM] * len(far),
        out_specs=[HBM if direct else VMEM for _, direct in outs],
        out_shape=[value for value, _ in outs],
        scratch_shapes=(landing if kernel is not pack_kernel else [])
        + scratch
        + ([pltpu.SemaphoreType.DMA((len(far),))] if far else []),
        compiler_params=pltpu.CompilerParams(vmem_limit_bytes=limit),
        cost_estimate=pl.CostEstimate(flops=flops, bytes_accessed=moved, transcendentals=0),
    )(*own, *near, *far)


def shape(dims, kind=F32):
    return jax.ShapeDtypeStruct(dims, kind)


def run_pack(query_in, key_in, value_in, grad_out):
    return call(
        pack_kernel,
        "pack",
        [],
        [],
        [query_in, key_in, value_in, grad_out],
        [(shape((ROWS, 8, COLS), BF16), False)],
        [pltpu.VMEM((4, 128, COLS), BF16), pltpu.VMEM((2, 512, 128), F32)],
        1 << 20,
        1 << 19,
    )[0]


def run_filter(own, weight, bias, proj, decay, consts):
    names = ("pick", "turn", "right", "forward", "twiddle", "full")
    return call(
        filter_kernel,
        "filter",
        [own],
        [],
        [weight, bias, proj, decay] + [consts[name] for name in names],
        [
            (shape((ROWS * FEAT, COLS), BF16), True),
            (shape((ROWS * FEAT, COLS), BF16), True),
            (shape((CHAN * ROWS, COLS)), False),
            (shape((CHAN * ROWS, 2 * COLS)), False),
            (shape((CHAN * FEAT, 128)), False),
        ],
        [
            pltpu.VMEM((128, 128), F32),
            pltpu.VMEM((ROWS * FEAT, COLS), BF16),
            pltpu.VMEM((512, COLS), F32),
            pltpu.VMEM((CHAN * ROWS, COLS), F32),
            pltpu.VMEM((ROWS * FEAT, COLS), BF16),
            pltpu.VMEM((ROWS * FEAT, COLS), BF16),
            pltpu.SemaphoreType.DMA((2, 8)),
        ],
        1 << 33,
        1 << 23,
    )


def run_gradient(own, arrived, short, act, cosine, envelope, columns, consts):
    names = ("back", "back_turn", "place", "forward", "last", "twiddle", "full")
    return call(
        gradient_kernel,
        "gradient",
        [own],
        [],
        [arrived, act, cosine, envelope, columns, short] + [consts[name] for name in names],
        [
            (shape((2, ROWS * 8, 128)), True),
            (shape((2 * CHAN * ROWS, 2 * COLS)), True),
            (shape((2 * CHAN, ROWS, COLS)), True),
            (shape((8, 128)), False),
            (shape((16, 8, COLS)), False),
        ],
        [
            pltpu.VMEM((128, 128), F32),
            pltpu.VMEM((2, CHAN * ROWS, 128), F32),
            pltpu.VMEM((2, ROWS * 8, 128), F32),
            pltpu.VMEM((2 * CHAN * ROWS, 2 * COLS), F32),
            pltpu.VMEM((2 * CHAN, ROWS, COLS), F32),
            pltpu.SemaphoreType.DMA((3,)),
        ],
        1 << 32,
        1 << 23,
    )


def run_output(own, skip, short, feat, spec, filter_spec, signals, proj_row, basis_parts, consts):
    names = ("last", "twiddle", "full")
    return call(
        output_kernel,
        "output",
        [own],
        [],
        [feat, spec, filter_spec, signals, proj_row, basis_parts, skip, short] + [consts[name] for name in names],
        [(shape((ROWS, 16, COLS), BF16), False)],
        [pltpu.VMEM((128, 128), F32), pltpu.VMEM((2, ROWS * 8, 128), F32)],
        1 << 31,
        1 << 22,
    )[0]


def run_unpack(arrived):
    block = shape((128, COLS), BF16)
    return call(
        unpack_kernel,
        "unpack",
        [],
        [arrived],
        [],
        [(value, False) for value in [block] * 4 + [shape((FEAT, 128)), shape((EMB, FEAT))]],
        [pltpu.VMEM((2, ROWS * 16, 128), F32), pltpu.VMEM((64, 128), F32)],
        1 << 20,
        1 << 20,
        20 * 1024 * 1024,
    )


def make_consts():
    forward, last, twiddle, full = transform_tables()
    right, turn, pick, back, back_turn, place = basis_tables()
    return dict(
        forward=jnp.asarray(forward),
        last=jnp.asarray(last),
        twiddle=jnp.asarray(twiddle),
        full=jnp.asarray(full),
        right=jnp.asarray(right),
        turn=jnp.asarray(turn),
        pick=jnp.asarray(pick),
        back=jnp.asarray(back),
        back_turn=jnp.asarray(back_turn),
        place=jnp.asarray(place),
    )


CTX = ("zh", "y", "core")
PAIR = ("core", "x", "zl")


def exchange(value, axes):
    return lax.all_to_all(value, axes, split_axis=0, concat_axis=0, tiled=True)


def on_device(
    query_in,
    key_in,
    value_in,
    short_kernel,
    basis_weight,
    basis_bias,
    filter_proj,
    decay_rate,
    skip_gain,
    grad_out,
):
    consts = make_consts()
    own = lax.axis_index(CTX).astype(jnp.int32).reshape(1)
    with jax.named_scope("spread"):
        arrived = exchange(run_pack(query_in, key_in, value_in, grad_out), CTX)
    short = short_kernel.transpose(0, 2, 1)
    act, cosine, envelope, filter_spec, columns = run_filter(
        own,
        basis_weight.T,
        basis_bias.reshape(1, FEAT),
        filter_proj.T,
        decay_rate.reshape(1, 128),
        consts,
    )
    feat, spec, signals, proj_row, basis_own = run_gradient(
        own, arrived, short, act, cosine, envelope, columns, consts
    )
    with jax.named_scope("basis"):
        basis_parts = exchange(basis_own, PAIR)
    packed = run_output(
        own,
        skip_gain.reshape(1, 128),
        short,
        feat,
        spec,
        filter_spec,
        signals,
        proj_row,
        basis_parts,
        consts,
    )
    with jax.named_scope("collect"):
        returned = exchange(packed, CTX)
    mixed, grad_query, grad_key, grad_value, grad_proj, grad_basis = run_unpack(returned)
    return (mixed, grad_query, grad_key, grad_value, grad_proj.T, grad_basis.T)


def solution(mesh):
    finer = Mesh(mesh.devices.reshape(4, 8, 2, 4, 2), ("zh", "y", "core", "x", "zl"))
    rows = ("x", "zl")
    block = P(rows, CTX)
    return jax.shard_map(
        on_device,
        mesh=finer,
        in_specs=(
            block,
            block,
            block,
            P(None, rows, None),
            P(),
            P(),
            P(rows, None),
            P(rows),
            P(rows),
            block,
        ),
        out_specs=(block, block, block, block, P(rows, None), P()),
        check_vma=False,
    )
```

```python
import math

import jax
import jax.numpy as jnp
import numpy as np
from jax import lax
from jax.experimental import pallas as pl
from jax.experimental.pallas import tpu as pltpu
from jax.sharding import Mesh
from jax.sharding import PartitionSpec as P
import ml_dtypes

F32 = jnp.float32
BF16 = jnp.bfloat16
EXACT = lax.Precision.HIGHEST

ROWS = 64
COLS = 256
TOTAL = ROWS * COLS
FEAT = 64
EMB = 33
TAPS = 7
CHAN = 2
GROUP = 40
TURN = 1.0 / (2.0 * math.pi)

SIN_COEF = (
    4.442883014678955,
    -7.308245658874512,
    3.606354236602783,
    -0.8461116552352905,
    0.1098245158791542,
)
COS_COEF = (
    1.4142135381698608,
    -6.978850841522217,
    5.739460468292236,
    -1.883557915687561,
    0.3106880187988281,
)


def halves(table, count):
    parts = []
    rest = np.asarray(table, np.float64)
    for _ in range(count):
        part = rest.astype(np.float32).astype(ml_dtypes.bfloat16)
        parts.append(part)
        rest = rest - part.astype(np.float64)
    return parts


def transform_tables():
    rows = np.arange(ROWS)
    cols = np.arange(COLS)
    first = 2.0 * np.pi * ((4 * rows[:, None] + 1) * rows[None, :] % (4 * ROWS)) / (4 * ROWS)
    first_re, first_im = np.cos(first), -np.sin(first)
    forward = np.concatenate([first_re, first_im], axis=0)
    forward_cat = np.concatenate(halves(forward, 2), axis=1)
    last = np.concatenate([first_re.T, -first_im.T], axis=1) / TOTAL
    last_hi, last_lo = halves(last, 2)
    last_cat = np.concatenate([last_hi, last_lo, last_hi], axis=1)
    turn = 2.0 * np.pi * ((4 * rows[:, None] + 1) * cols[None, :]) / (4 * TOTAL)
    twiddle = np.stack([np.cos(turn), -np.sin(turn)]).astype(np.float32)
    inner = 2.0 * np.pi * (cols[:, None] * cols[None, :] % COLS) / COLS
    inner_re, inner_im = np.cos(inner), -np.sin(inner)
    full = np.concatenate(
        [
            np.concatenate([inner_re, inner_im], axis=1),
            np.concatenate([-inner_im, inner_re], axis=1),
        ],
        axis=0,
    )
    full_hi, full_lo = halves(full, 2)
    return forward_cat, last_cat, twiddle, np.stack([full_hi, full_lo])


def basis_tables():
    freq = np.arange(1, 17)
    cols = np.arange(COLS)
    rows = np.arange(ROWS)
    inner = 2.0 * np.pi * (freq[:, None] * cols[None, :] % TOTAL) / TOTAL
    short = np.concatenate(
        [np.cos(inner), np.sin(inner), cols[None, :] / TOTAL, np.ones((1, COLS))], axis=0
    )
    width = short.shape[0]
    hi, mid, lo = halves(short, 3)
    right = np.zeros((256, COLS), ml_dtypes.bfloat16)
    for place, part in ((0, hi), (GROUP, hi), (2 * GROUP, hi)):
        right[place : place + width] = part
    for place, part in ((128, mid), (128 + GROUP, lo), (128 + 2 * GROUP, mid)):
        right[place : place + width] = part
    outer = 2.0 * np.pi * (freq[None, :] * rows[:, None] % ROWS) / ROWS
    cos_out, sin_out = np.cos(outer), np.sin(outer)
    one = np.ones((ROWS, 1))
    block = rows[:, None] / ROWS
    cos_row = np.concatenate([cos_out, cos_out, one, one], axis=1)
    sin_row = np.concatenate([sin_out, sin_out, 0 * one, block], axis=1)
    turn = np.zeros((2, ROWS, 128), np.float32)
    for place in (0, GROUP, 2 * GROUP):
        turn[0, :, place : place + width] = cos_row
        turn[1, :, place : place + width] = sin_row
    pick = np.zeros((2, 128, 128), np.float32)
    for place in (0, GROUP, 2 * GROUP):
        for index in range(16):
            pick[0, 2 * index + 1, place + index] = 1.0
            pick[0, 2 * index + 2, place + 16 + index] = 1.0
            pick[1, 2 * index + 2, place + index] = 1.0
            pick[1, 2 * index + 1, place + 16 + index] = -1.0
        pick[0, 0, place + 32] = 1.0
        pick[0, EMB, place + 33] = 1.0
        pick[1, 0, place + 33] = 1.0
    back = np.zeros((COLS, 128))
    back[:, :width] = short.T
    back[:, 64:80] = short[16:32].T
    back[:, 80:96] = short[:16].T
    back_hi, back_lo = halves(back, 2)
    back_cat = np.concatenate([back_hi, back_lo], axis=1)
    back_turn = np.zeros((ROWS, 128), np.float32)
    back_turn[:, :32] = cos_row[:, :32]
    back_turn[:, 32] = 1.0
    back_turn[:, 33] = rows / ROWS
    back_turn[:, 64:80] = -sin_out
    back_turn[:, 80:96] = sin_out
    place = np.zeros((8, 8, 128), np.float32)
    for wanted in range(EMB):
        row, group = divmod(wanted, 8)
        if wanted == 0:
            lanes = (32, 33)
        elif wanted % 2:
            lanes = ((wanted - 1) // 2, 64 + (wanted - 1) // 2)
        else:
            lanes = (16 + (wanted - 2) // 2, 80 + (wanted - 2) // 2)
        for lane in lanes:
            place[group, row, lane] = 1.0
    return right, turn, pick, back_cat, back_turn, place


def split(value):
    hi = value.astype(BF16)
    lo = (value - hi.astype(F32)).astype(BF16)
    return hi, lo


def dot(left, right):
    return jnp.dot(left, right, preferred_element_type=F32)


def spectrum(signals, forward, twiddle_re, twiddle_im, full_hi, full_lo):
    wide = jnp.concatenate(signals, axis=1)
    section = dot(forward, jnp.concatenate([wide, wide], axis=0))
    turned = []
    for index in range(len(signals)):
        part = section[:, index * COLS : (index + 1) * COLS]
        part_re, part_im = part[:ROWS], part[ROWS:]
        turned.append(
            jnp.concatenate(
                [
                    part_re * twiddle_re - part_im * twiddle_im,
                    part_re * twiddle_im + part_im * twiddle_re,
                ],
                axis=1,
            )
        )
    return full_product(jnp.concatenate(turned, axis=0), full_hi, full_lo)


def full_product(value, full_hi, full_lo):
    hi, lo = split(value)
    return dot(hi, full_hi) + dot(lo, full_hi) + dot(hi, full_lo)


def restore(conj_spec, count, last, twiddle_re, twiddle_im, full_hi, full_lo):
    back = full_product(conj_spec, full_hi, full_lo)
    stacked = []
    for index in range(count):
        part = back[index * ROWS : (index + 1) * ROWS]
        part_re, part_im = part[:, :COLS], part[:, COLS:]
        stacked.append(
            jnp.concatenate(
                [
                    part_re * twiddle_re - part_im * twiddle_im,
                    part_re * twiddle_im + part_im * twiddle_re,
                ],
                axis=0,
            )
        )
    hi, lo = split(jnp.concatenate(stacked, axis=1))
    result = dot(last, jnp.concatenate([hi, hi, lo], axis=0))
    return [result[:, index * COLS : (index + 1) * COLS] for index in range(count)]


def take(ref, start, count, stride):
    return jnp.concatenate(
        [ref[half, pl.ds(start, count, stride=stride), :] for half in range(2)], axis=1
    )


def put(ref, start, count, stride, value):
    for half in range(2):
        ref[half, pl.ds(start, count, stride=stride), :] = value[:, half * 128 : half * 128 + 128]


def fill(ref, value):
    for half in range(2):
        ref[half] = value[..., half * 128 : half * 128 + 128].reshape(ref.shape[1], 128)


def begin(sems, pairs):
    copies = [
        pltpu.make_async_copy(source, target, sems.at[index])
        for index, (source, target) in enumerate(pairs)
    ]
    for copy in copies:
        copy.start()
    return copies


def picked(row, wanted):
    lane = lax.broadcasted_iota(jnp.int32, row.shape, 1)
    return jnp.sum(jnp.where(lane == wanted, row, 0.0), axis=1, keepdims=True)


def pack_kernel(query, key, value, grad, out, held, wide, sems):
    copies = begin(sems, [(ref, held.at[index]) for index, ref in enumerate((query, key, value, grad))])
    for index in range(4):
        copies[index].wait()
        block = held[index].astype(F32)
        for half in range(2):
            wide[half, index * 128 : (index + 1) * 128, :] = block[:, half * 128 : half * 128 + 128]
    for peer in range(ROWS):
        out[peer] = take(wide, peer, 8, ROWS).astype(BF16)


def expm1_small(value):
    series = jnp.ones_like(value)
    for order in range(9, 1, -1):
        series = 1.0 + value * series * (1.0 / order)
    return jnp.where(value > -0.5, value * series, jnp.exp(value) - 1.0)


def filter_kernel(
    own,
    weight_src,
    bias_src,
    proj_src,
    decay_src,
    pick_src,
    turn_src,
    right_src,
    forward_src,
    twiddle_src,
    full_src,
    act_out,
    cos_out,
    env_out,
    spec_out,
    column_out,
    weight,
    bias,
    proj,
    decay,
    pick,
    turn,
    right,
    forward,
    twiddle,
    full,
    layer,
    left,
    phase,
    filt,
    act,
    cosv,
    out_sems,
    sems,
):
    first = own[0]
    copies = begin(
        sems,
        [
            (weight_src, weight),
            (bias_src, bias),
            (pick_src, pick),
            (proj_src, proj),
            (turn_src, turn),
            (right_src, right),
            (decay_src, decay),
            (forward_src, forward),
            (twiddle_src, twiddle),
            (full_src, full),
        ],
    )
    layer[...] = jnp.zeros((128, 128), F32)
    for copy in copies[:3]:
        copy.wait()
    layer[0:EMB, 0:FEAT] = weight[...]
    layer[EMB : EMB + 1, 0:FEAT] = bias[...]
    layer_all = layer[...].T[0:FEAT, :]
    same = jnp.dot(layer_all, pick[0], precision=EXACT, preferred_element_type=F32) * TURN
    cross = jnp.dot(layer_all, pick[1], precision=EXACT, preferred_element_type=F32) * TURN
    lane = lax.broadcasted_iota(jnp.int32, (FEAT, 128), 1)
    sublane = lax.broadcasted_iota(jnp.int32, (8, 128), 0)
    for copy in copies[3:7]:
        copy.wait()
    columns = []
    for chan in range(CHAN):
        hit = lane == first + 64 * chan
        column = jnp.sum(jnp.where(hit, proj[...], 0.0), axis=1, keepdims=True)
        column_wide = jnp.broadcast_to(column, (FEAT, 128))
        column_out[chan * FEAT : (chan + 1) * FEAT, :] = column_wide
        columns.append(column_wide)

    def make_left(block, carry):
        value = same * turn[0, pl.ds(block, 1), :] + cross * turn[1, pl.ds(block, 1), :]
        hi = value.astype(BF16).astype(F32)
        rest = value - hi
        mid = rest.astype(BF16).astype(F32)
        lo = rest - mid
        one = jnp.where(lane < GROUP, hi, jnp.where(lane < 2 * GROUP, mid, lo))
        two = jnp.where(lane < 2 * GROUP, hi, mid)
        start = pl.multiple_of(block * FEAT, FEAT)
        left[pl.ds(start, FEAT), 0:128] = one.astype(BF16)
        left[pl.ds(start, FEAT), 128:256] = two.astype(BF16)
        return carry

    lax.fori_loop(0, ROWS, make_left, 0, unroll=4)

    def chunk(index, carry):
        base = pl.multiple_of(index * 512, 512)
        phase[...] = dot(left[pl.ds(base, 512), :], right[...])
        for half in range(2):
            lanes = slice(half * 128, half * 128 + 128)
            sums = [jnp.zeros((8, 128), F32)] * CHAN
            for inner in range(8):
                near = inner * FEAT
                turns = phase[near : near + FEAT, lanes]
                rest = turns - jnp.round(turns)
                square = rest * rest
                sine = SIN_COEF[-1] * square + SIN_COEF[-2]
                cosine = COS_COEF[-1] * square + COS_COEF[-2]
                for coef in SIN_COEF[-3::-1]:
                    sine = sine * square + coef
                for coef in COS_COEF[-3::-1]:
                    cosine = cosine * square + coef
                sine = sine * rest
                whole_sine = sine * cosine
                whole_cosine = 1.0 - sine * sine
                act[pl.ds(base + near, FEAT), lanes] = whole_sine.astype(BF16)
                cosv[pl.ds(base + near, FEAT), lanes] = whole_cosine.astype(BF16)
                for chan in range(CHAN):
                    total = jnp.sum(whole_sine * columns[chan], axis=0, keepdims=True)
                    sums[chan] = jnp.where(sublane == inner, total, sums[chan])
            for chan in range(CHAN):
                start = pl.multiple_of(chan * ROWS + index * 8, 8)
                filt[pl.ds(start, 8), lanes] = sums[chan]
        send(index, 0).start()
        send(index, 1).start()
        return carry

    def send(index, which):
        rows = pl.ds(pl.multiple_of(index * 512, 512), 512)
        source, target = ((act, act_out), (cosv, cos_out))[which]
        return pltpu.make_async_copy(source.at[rows], target.at[rows], out_sems.at[which, index])

    lax.fori_loop(0, 8, chunk, 0)
    ratio = decay[...] * (1.0 / TOTAL)
    energy = expm1_small(-2.0 * decay[...]) / expm1_small(-2.0 * ratio)
    norm = 1.0 / jnp.sqrt(energy)
    for copy in copies[7:]:
        copy.wait()
    position = (
        lax.broadcasted_iota(jnp.int32, (ROWS, COLS), 0) * COLS
        + lax.broadcasted_iota(jnp.int32, (ROWS, COLS), 1)
    ).astype(F32)
    signals = []
    for chan in range(CHAN):
        rate = picked(decay[...], first + 64 * chan)
        envelope = jnp.exp(-(rate * position) * (1.0 / TOTAL)) * picked(norm, first + 64 * chan)
        env_out[chan * ROWS : (chan + 1) * ROWS, :] = envelope
        signals.append((filt[chan * ROWS : (chan + 1) * ROWS, :] * envelope).astype(BF16))
    spec_out[...] = spectrum(signals, forward[...], twiddle[0], twiddle[1], full[0], full[1])
    for index in range(8):
        send(index, 0).wait()
        send(index, 1).wait()


def own_taps(first, short, taps, order):
    row = lax.broadcasted_iota(jnp.int32, (TAPS, 128), 0)
    lane = lax.broadcasted_iota(jnp.int32, (TAPS, 128), 1)
    columns = jnp.where(row == 0, 1.0, 0.0)
    for place, which in order:
        for chan in range(CHAN):
            hit = lane == first + 64 * chan
            column = jnp.sum(jnp.where(hit, short[which], 0.0), axis=1, keepdims=True)
            columns = jnp.where(lane == place + chan, column, columns)
    taps[...] = jnp.zeros((128, 128), F32)
    taps[0:TAPS, :] = columns
    return taps[...].T[0:8, :]


def gradient_kernel(
    own,
    arrived_src,
    envelope_src,
    columns_src,
    cosine_src,
    short_src,
    back_src,
    back_turn_src,
    place_src,
    forward_src,
    last_src,
    twiddle_src,
    full_src,
    feat_out,
    spec_out,
    raw_out,
    basis_out,
    arrived,
    envelope,
    columns,
    cosine,
    short,
    back,
    back_turn,
    place,
    forward,
    last,
    twiddle,
    full,
    taps,
    raw,
    feat,
    spec,
    out_sems,
    sems,
):
    first = own[0]
    copies = begin(
        sems,
        [
            (short_src, short),
            (arrived_src, arrived),
            (forward_src, forward),
            (twiddle_src, twiddle),
            (full_src, full),
            (last_src, last),
            (envelope_src, envelope),
            (cosine_src, cosine),
            (columns_src, columns),
            (back_src, back),
            (back_turn_src, back_turn),
            (place_src, place),
        ],
    )
    copies[0].wait()
    weights = own_taps(first, short, taps, ((0, 0), (2, 1), (4, 2)))
    copies[1].wait()
    signal = arrived[...].astype(F32)
    lane = lax.broadcasted_iota(jnp.int32, (ROWS, 8, COLS), 2)
    result = weights[None, :, 0:1] * signal
    zeros = jnp.zeros((1, 8, COLS), F32)
    for offset in range(1, TAPS):
        moved = pltpu.roll(signal, offset, 2)
        before = jnp.concatenate([zeros, moved[:-1]], axis=0)
        shifted = jnp.where(lane < offset, before, moved)
        result = result + weights[None, :, offset : offset + 1] * shifted
    fill(feat, result)
    leaving = begin(out_sems.at[pl.ds(0, 1)], [(feat, feat_out)])

    def plane(index):
        return take(feat, index, ROWS, 8)

    signals = []
    for chan in range(CHAN):
        signals.append((plane(2 + chan) * plane(4 + chan)).astype(BF16))
    for chan in range(CHAN):
        signals.append((plane(chan) * plane(6 + chan)).astype(BF16))
    for copy in copies[2:5]:
        copy.wait()
    tables = (twiddle[0], twiddle[1], full[0], full[1])
    spec_all = spectrum(signals, forward[...], *tables)
    spec[...] = spec_all
    leaving += begin(out_sems.at[pl.ds(1, 1)], [(spec, spec_out)])
    carried, grad = spec_all[: CHAN * ROWS], spec_all[CHAN * ROWS :]
    carried_re, carried_im = carried[:, :COLS], carried[:, COLS:]
    grad_re, grad_im = grad[:, :COLS], grad[:, COLS:]
    crossed = jnp.concatenate(
        [
            carried_re * grad_re + carried_im * grad_im,
            carried_im * grad_re - carried_re * grad_im,
        ],
        axis=1,
    )
    for copy in copies[5:7]:
        copy.wait()
    filter_grad = restore(crossed, CHAN, last[...], *tables)
    for chan in range(CHAN):
        rounded = filter_grad[chan].astype(BF16).astype(F32)
        scaled = rounded * envelope[chan * ROWS : (chan + 1) * ROWS, :]
        for half in range(2):
            raw[half, chan * ROWS : (chan + 1) * ROWS, :] = scaled[:, half * 128 : half * 128 + 128]
    leaving += begin(out_sems.at[pl.ds(2, 1)], [(raw, raw_out)])
    for copy in copies[7:]:
        copy.wait()
    column0 = columns[0:FEAT, :]
    column1 = columns[FEAT : 2 * FEAT, :]
    back_all = back[...]

    def chunk(index, basis_sum):
        base = pl.multiple_of(index * 512, 512)
        start = pl.multiple_of(index * 8, 8)
        rows = [
            [raw[half, pl.ds(chan * ROWS + start, 8), :] for half in range(2)] for chan in range(CHAN)
        ]
        angles = back_turn[pl.ds(start, 8), :]
        parts = []
        for inner in range(8):
            near = inner * FEAT
            pieces = []
            for half in range(2):
                lanes = slice(half * 128, half * 128 + 128)
                value = (
                    column0 * rows[0][half][inner : inner + 1, :]
                    + column1 * rows[1][half][inner : inner + 1, :]
                )
                value = value * cosine[pl.ds(base + near, FEAT), lanes].astype(F32)
                pieces.append(value.astype(BF16))
            parts.append(jnp.concatenate(pieces, axis=1))
        product = dot(jnp.concatenate(parts, axis=0), back_all)
        for inner in range(8):
            near = inner * FEAT
            both = product[near : near + FEAT, 0:128] + product[near : near + FEAT, 128:256]
            basis_sum = basis_sum + both * angles[inner : inner + 1, :]
        return basis_sum

    basis_sum = lax.fori_loop(0, 8, chunk, jnp.zeros((FEAT, 128), F32), unroll=2)
    pieces = [
        lax.dot_general(
            place[group],
            basis_sum,
            (((1,), (1,)), ((), ())),
            precision=EXACT,
            preferred_element_type=F32,
        )
        for group in range(8)
    ]
    for quarter in range(4):
        row = jnp.concatenate(
            [piece[:, quarter * 16 : quarter * 16 + 16] for piece in pieces], axis=1
        )
        for peer in range(8):
            basis_out[quarter * 8 + peer] = row
    for copy in leaving:
        copy.wait()


def output_kernel(
    own,
    feat_src,
    spec_src,
    filter_spec_src,
    raw_src,
    act_src,
    skip_src,
    short_src,
    last_src,
    twiddle_src,
    full_src,
    out,
    feat,
    spec,
    filter_spec,
    raw,
    act,
    skip,
    short,
    last,
    twiddle,
    full,
    taps,
    mate,
    stage,
    out_sems,
    sems,
):
    first = own[0]
    copies = begin(
        sems,
        [
            (spec_src, spec),
            (filter_spec_src, filter_spec),
            (full_src, full),
            (twiddle_src, twiddle),
            (last_src, last),
            (skip_src, skip),
            (short_src, short),
            (feat_src, feat),
            (raw_src, raw),
            (act_src, act),
        ],
    )
    for copy in copies[0:5]:
        copy.wait()
    tables = (twiddle[0], twiddle[1], full[0], full[1])
    carried, grad = spec[0 : CHAN * ROWS, :], spec[CHAN * ROWS : 2 * CHAN * ROWS, :]
    filt = filter_spec[...]
    carried_re, carried_im = carried[:, :COLS], carried[:, COLS:]
    grad_re, grad_im = grad[:, :COLS], grad[:, COLS:]
    filt_re, filt_im = filt[:, :COLS], filt[:, COLS:]
    crossed = jnp.concatenate(
        [
            jnp.concatenate(
                [
                    filt_re * carried_re - filt_im * carried_im,
                    -(filt_re * carried_im + filt_im * carried_re),
                ],
                axis=1,
            ),
            jnp.concatenate(
                [
                    filt_re * grad_re + filt_im * grad_im,
                    filt_im * grad_re - filt_re * grad_im,
                ],
                axis=1,
            ),
        ],
        axis=0,
    )
    sums = restore(crossed, 2 * CHAN, last[...], *tables)
    for copy in copies[5:8]:
        copy.wait()
    weights = own_taps(first, short, taps, ((2, 2), (4, 1), (6, 0)))

    def plane(index):
        return take(feat, index, ROWS, 8)

    for chan in range(CHAN):
        gain = picked(skip[...], first + 64 * chan)
        carried_own = (plane(2 + chan) * plane(4 + chan)).astype(BF16).astype(F32)
        grad_own = (plane(chan) * plane(6 + chan)).astype(BF16).astype(F32)
        long_out = (sums[chan] + gain * carried_own).astype(BF16).astype(F32)
        carried_grad = (sums[CHAN + chan] + gain * grad_own).astype(BF16).astype(F32)
        put(mate, chan, ROWS, 8, long_out)
        put(mate, 2 + chan, ROWS, 8, carried_grad)
        put(mate, 4 + chan, ROWS, 8, carried_grad)
        put(mate, 6 + chan, ROWS, 8, long_out)
    signal = jnp.concatenate(
        [(feat[half] * mate[half]).astype(BF16).astype(F32).reshape(ROWS, 8, 128) for half in range(2)],
        axis=2,
    )
    lane = lax.broadcasted_iota(jnp.int32, (ROWS, 8, COLS), 2)
    result = weights[None, :, 0:1] * signal
    zeros = jnp.zeros((1, 8, COLS), F32)
    for offset in range(1, TAPS):
        moved = pltpu.roll(signal, COLS - offset, 2)
        after = jnp.concatenate([moved[1:], zeros], axis=0)
        shifted = jnp.where(lane >= COLS - offset, after, moved)
        result = result + weights[None, :, offset : offset + 1] * shifted
    stage[:, :, 0:COLS] = result.astype(BF16)

    def leave(start, size, index):
        lanes = pl.ds(start, size)
        return pltpu.make_async_copy(
            stage.at[:, :, lanes], out.at[:, :, lanes], out_sems.at[index]
        )

    leave(0, COLS, 0).start()
    lane128 = lax.broadcasted_iota(jnp.int32, (FEAT, 128), 1)
    row_lane = lane128 % 8
    copies[8].wait()
    copies[9].wait()

    def chunk(index, proj_sum):
        base = pl.multiple_of(index * 512, 512)
        start = pl.multiple_of(index * 8, 8)
        rows = [
            jnp.concatenate(
                [raw[half, pl.ds(chan * ROWS + start, 8), :] for half in range(2)], axis=1
            )
            for chan in range(CHAN)
        ]
        wide = jnp.concatenate(rows, axis=0)
        hi = wide.astype(BF16).astype(F32)
        packed = jnp.concatenate([hi, wide - hi, jnp.zeros((128 - 4 * 8, COLS), F32)], axis=0)
        turned = jnp.concatenate(
            [packed[:, half * 128 : half * 128 + 128].T for half in range(2)], axis=0
        ).astype(BF16)
        product = dot(act[pl.ds(base, 512), :], turned)
        for inner in range(8):
            near = inner * FEAT
            proj_sum = proj_sum + jnp.where(row_lane == inner, product[near : near + FEAT, :], 0.0)
        return proj_sum

    proj_sum = lax.fori_loop(0, 8, chunk, jnp.zeros((FEAT, 128), F32), unroll=2)
    own_lane = lane128 % 16
    stacked = jnp.concatenate(
        [jnp.where(own_lane < 8, proj_sum, 0.0), jnp.where(own_lane >= 8, proj_sum, 0.0)], axis=0
    )
    proj_wide = lax.dot_general(
        jnp.ones((8, 128), F32),
        stacked,
        (((1,), (1,)), ((), ())),
        precision=EXACT,
        preferred_element_type=F32,
    )
    proj_hi = proj_wide.astype(BF16).astype(F32)
    row = lax.broadcasted_iota(jnp.int32, (8, 128), 0)
    extra = jnp.where(row == 5, proj_hi, proj_wide - proj_hi)
    stage[:, :, COLS : COLS + 128] = jnp.broadcast_to(extra[None], (ROWS, 8, 128)).astype(BF16)
    leave(COLS, 128, 1).start()
    leave(0, COLS, 0).wait()
    leave(COLS, 128, 1).wait()


def compose_kernel(packed, basis_parts, out):
    basis = basis_parts[0]
    for source in range(1, 32):
        basis = basis + basis_parts[source]
    row = lax.broadcasted_iota(jnp.int32, (8, 128), 0)
    proj_rows = packed[0, :, COLS : COLS + 128].astype(F32)
    extra = jnp.where(row < 5, basis, proj_rows)
    out[:, :, 0:COLS] = packed[:, :, 0:COLS]
    out[:, :, COLS : COLS + 128] = jnp.broadcast_to(extra[None], (ROWS, 8, 128)).astype(BF16)


def unpack_kernel(
    arrived, mixed, grad_query, grad_key, grad_value, proj, basis, wide, sorted_rows
):
    for part in range(3):
        wide[part] = arrived[:, :, part * 128 : part * 128 + 128].astype(F32).reshape(ROWS * 8, 128)
    for ref, start in ((mixed, 0), (grad_value, 2), (grad_key, 4), (grad_query, 6)):
        for chan in range(CHAN):
            ref[chan * ROWS : (chan + 1) * ROWS, :] = take(wide, start + chan, ROWS, 8).astype(BF16)
    both = wide[2, pl.ds(5, ROWS, stride=8), :] + wide[2, pl.ds(6, ROWS, stride=8), :]
    both = both * (1.0 / math.sqrt(TOTAL))
    both = jnp.concatenate([both, jnp.zeros_like(both)], axis=0).T
    proj[:, 0:ROWS] = both[0:FEAT, 0:ROWS]
    proj[:, ROWS : 2 * ROWS] = both[FEAT : 2 * FEAT, 0:ROWS]
    totals = []
    for quarter in range(4):
        total = wide[2, quarter * 8 : quarter * 8 + 8, :]
        for source in range(quarter + 4, ROWS, 4):
            total = total + wide[2, source * 8 : source * 8 + 8, :]
        totals.append(total)
    scale = math.sqrt(FEAT / (TOTAL * 1024))
    for group in range(8):
        lanes = slice(group * 16, group * 16 + 16)
        merged = jnp.concatenate(
            [total[:, lanes] for total in totals] + [jnp.zeros((8, 64), F32)], axis=1
        )
        sorted_rows[pl.ds(group, 8, stride=8), :] = merged * scale
    basis[...] = sorted_rows[0:EMB, 0:FEAT]


SMEM = pl.BlockSpec(memory_space=pltpu.SMEM)
VMEM = pl.BlockSpec(memory_space=pltpu.VMEM)
HBM = pl.BlockSpec(memory_space=pltpu.HBM)
LIMIT = 62 * 1024 * 1024
ROOMY = 32 * 1024 * 1024


def call(kernel, name, own, near, far, outs, scratch, flops, moved, limit=LIMIT):
    landing = [pltpu.VMEM(value.shape, value.dtype) for value in far]
    return pl.pallas_call(
        kernel,
        name=name,
        in_specs=[SMEM] * len(own) + [VMEM] * len(near) + [HBM] * len(far),
        out_specs=[HBM if direct else VMEM for _, direct in outs],
        out_shape=[value for value, _ in outs],
        scratch_shapes=(landing if kernel is not pack_kernel else [])
        + scratch
        + ([pltpu.SemaphoreType.DMA((len(far),))] if far else []),
        compiler_params=pltpu.CompilerParams(vmem_limit_bytes=limit),
        cost_estimate=pl.CostEstimate(flops=flops, bytes_accessed=moved, transcendentals=0),
    )(*own, *near, *far)


def shape(dims, kind=F32):
    return jax.ShapeDtypeStruct(dims, kind)


def run_pack(query_in, key_in, value_in, grad_out):
    return call(
        pack_kernel,
        "pack",
        [],
        [],
        [query_in, key_in, value_in, grad_out],
        [(shape((ROWS, 8, COLS), BF16), False)],
        [pltpu.VMEM((4, 128, COLS), BF16), pltpu.VMEM((2, 512, 128), F32)],
        1 << 20,
        1 << 19,
    )[0]


def run_filter(own, weight, bias, proj, decay, consts):
    names = ("pick", "turn", "right", "forward", "twiddle", "full")
    return call(
        filter_kernel,
        "filter",
        [own],
        [],
        [weight, bias, proj, decay] + [consts[name] for name in names],
        [
            (shape((ROWS * FEAT, COLS), BF16), True),
            (shape((ROWS * FEAT, COLS), BF16), True),
            (shape((CHAN * ROWS, COLS)), False),
            (shape((CHAN * ROWS, 2 * COLS)), False),
            (shape((CHAN * FEAT, 128)), False),
        ],
        [
            pltpu.VMEM((128, 128), F32),
            pltpu.VMEM((ROWS * FEAT, COLS), BF16),
            pltpu.VMEM((512, COLS), F32),
            pltpu.VMEM((CHAN * ROWS, COLS), F32),
            pltpu.VMEM((ROWS * FEAT, COLS), BF16),
            pltpu.VMEM((ROWS * FEAT, COLS), BF16),
            pltpu.SemaphoreType.DMA((2, 8)),
        ],
        1 << 33,
        1 << 23,
    )


def run_gradient(own, arrived, short, cosine, envelope, columns, consts):
    names = ("back", "back_turn", "place", "forward", "last", "twiddle", "full")
    return call(
        gradient_kernel,
        "gradient",
        [own],
        [],
        [arrived, envelope, columns, cosine, short] + [consts[name] for name in names],
        [
            (shape((2, ROWS * 8, 128)), True),
            (shape((2 * CHAN * ROWS, 2 * COLS)), True),
            (shape((2, CHAN * ROWS, 128)), True),
            (shape((32, 8, 128)), False),
        ],
        [
            pltpu.VMEM((128, 128), F32),
            pltpu.VMEM((2, CHAN * ROWS, 128), F32),
            pltpu.VMEM((2, ROWS * 8, 128), F32),
            pltpu.VMEM((2 * CHAN * ROWS, 2 * COLS), F32),
            pltpu.SemaphoreType.DMA((3,)),
        ],
        1 << 32,
        1 << 23,
    )


def run_output(own, skip, short, feat, spec, filter_spec, raw, act, consts):
    names = ("last", "twiddle", "full")
    return call(
        output_kernel,
        "output",
        [own],
        [],
        [feat, spec, filter_spec, raw, act, skip, short] + [consts[name] for name in names],
        [(shape((ROWS, 8, COLS + 128), BF16), True)],
        [
            pltpu.VMEM((128, 128), F32),
            pltpu.VMEM((2, ROWS * 8, 128), F32),
            pltpu.VMEM((ROWS, 8, COLS + 128), BF16),
            pltpu.SemaphoreType.DMA((2,)),
        ],
        1 << 31,
        1 << 22,
    )[0]


def run_compose(packed, basis_parts):
    return call(
        compose_kernel,
        "compose",
        [],
        [packed, basis_parts],
        [],
        [(shape((ROWS, 8, COLS + 128), BF16), False)],
        [],
        1 << 20,
        1 << 20,
        ROOMY,
    )[0]


def run_unpack(arrived):
    block = shape((128, COLS), BF16)
    return call(
        unpack_kernel,
        "unpack",
        [],
        [arrived],
        [],
        [(value, False) for value in [block] * 4 + [shape((FEAT, 128)), shape((EMB, FEAT))]],
        [pltpu.VMEM((3, ROWS * 8, 128), F32), pltpu.VMEM((64, 128), F32)],
        1 << 20,
        1 << 20,
        ROOMY,
    )


def make_consts():
    forward, last, twiddle, full = transform_tables()
    right, turn, pick, back, back_turn, place = basis_tables()
    return dict(
        forward=jnp.asarray(forward),
        last=jnp.asarray(last),
        twiddle=jnp.asarray(twiddle),
        full=jnp.asarray(full),
        right=jnp.asarray(right),
        turn=jnp.asarray(turn),
        pick=jnp.asarray(pick),
        back=jnp.asarray(back),
        back_turn=jnp.asarray(back_turn),
        place=jnp.asarray(place),
    )


CTX = ("zh", "yh", "yl", "core")
NEAR = ("yl", "core", "x", "zl")


def exchange(value, axes):
    return lax.all_to_all(value, axes, split_axis=0, concat_axis=0, tiled=True)


def on_device(
    query_in,
    key_in,
    value_in,
    short_kernel,
    basis_weight,
    basis_bias,
    filter_proj,
    decay_rate,
    skip_gain,
    grad_out,
):
    consts = make_consts()
    own = lax.axis_index(CTX).astype(jnp.int32).reshape(1)
    with jax.named_scope("spread"):
        arrived = exchange(run_pack(query_in, key_in, value_in, grad_out), CTX)
    short = short_kernel.transpose(0, 2, 1)
    act, cosine, envelope, filter_spec, columns = run_filter(
        own,
        basis_weight.T,
        basis_bias.reshape(1, FEAT),
        filter_proj.T,
        decay_rate.reshape(1, 128),
        consts,
    )
    feat, spec, raw, basis_own = run_gradient(
        own, arrived, short, cosine, envelope, columns, consts
    )
    with jax.named_scope("basis"):
        basis_parts = exchange(basis_own, NEAR)
    packed = run_output(
        own, skip_gain.reshape(1, 128), short, feat, spec, filter_spec, raw, act, consts
    )
    composed = run_compose(packed, basis_parts)
    with jax.named_scope("collect"):
        returned = exchange(composed, CTX)
    mixed, grad_query, grad_key, grad_value, grad_proj, grad_basis = run_unpack(returned)
    return (mixed, grad_query, grad_key, grad_value, grad_proj.T, grad_basis.T)


def solution(mesh):
    finer = Mesh(mesh.devices.reshape(4, 4, 2, 2, 4, 2), CTX + ("x", "zl"))
    rows = ("x", "zl")
    block = P(rows, CTX)
    return jax.shard_map(
        on_device,
        mesh=finer,
        in_specs=(
            block,
            block,
            block,
            P(None, rows, None),
            P(),
            P(),
            P(rows, None),
            P(rows),
            P(rows),
            block,
        ),
        out_specs=(block, block, block, block, P(rows, None), P()),
        check_vma=False,
    )
```

```python
import math

import jax
import jax.numpy as jnp
import numpy as np
from jax import lax
from jax.experimental import pallas as pl
from jax.experimental.pallas import tpu as pltpu
from jax.sharding import Mesh
from jax.sharding import PartitionSpec as P
import ml_dtypes

F32 = jnp.float32
BF16 = jnp.bfloat16
EXACT = lax.Precision.HIGHEST

ROWS = 64
COLS = 256
TOTAL = ROWS * COLS
FEAT = 64
EMB = 33
TAPS = 7
CHAN = 2
GROUP = 40
TURN = 1.0 / (2.0 * math.pi)

SIN_COEF = (
    4.442883014678955,
    -7.308245658874512,
    3.606354236602783,
    -0.8461116552352905,
    0.1098245158791542,
)
COS_COEF = (
    1.4142135381698608,
    -6.978850841522217,
    5.739460468292236,
    -1.883557915687561,
    0.3106880187988281,
)


def halves(table, count):
    parts = []
    rest = np.asarray(table, np.float64)
    for _ in range(count):
        part = rest.astype(np.float32).astype(ml_dtypes.bfloat16)
        parts.append(part)
        rest = rest - part.astype(np.float64)
    return parts


def transform_tables():
    rows = np.arange(ROWS)
    cols = np.arange(COLS)
    first = 2.0 * np.pi * ((4 * rows[:, None] + 1) * rows[None, :] % (4 * ROWS)) / (4 * ROWS)
    first_re, first_im = np.cos(first), -np.sin(first)
    forward = np.concatenate([first_re, first_im], axis=0)
    forward_cat = np.concatenate(halves(forward, 2), axis=1)
    last = np.concatenate([first_re.T, -first_im.T], axis=1) / TOTAL
    last_hi, last_lo = halves(last, 2)
    last_cat = np.concatenate([last_hi, last_lo, last_hi], axis=1)
    turn = 2.0 * np.pi * ((4 * rows[:, None] + 1) * cols[None, :]) / (4 * TOTAL)
    twiddle = np.stack([np.cos(turn), -np.sin(turn)]).astype(np.float32)
    inner = 2.0 * np.pi * (cols[:, None] * cols[None, :] % COLS) / COLS
    inner_re, inner_im = np.cos(inner), -np.sin(inner)
    full = np.concatenate(
        [
            np.concatenate([inner_re, inner_im], axis=1),
            np.concatenate([-inner_im, inner_re], axis=1),
        ],
        axis=0,
    )
    full_hi, full_lo = halves(full, 2)
    return forward_cat, last_cat, twiddle, np.stack([full_hi, full_lo])


def basis_tables():
    freq = np.arange(1, 17)
    cols = np.arange(COLS)
    rows = np.arange(ROWS)
    inner = 2.0 * np.pi * (freq[:, None] * cols[None, :] % TOTAL) / TOTAL
    short = np.concatenate(
        [np.cos(inner), np.sin(inner), cols[None, :] / TOTAL, np.ones((1, COLS))], axis=0
    )
    width = short.shape[0]
    hi, mid, lo = halves(short, 3)
    right = np.zeros((256, COLS), ml_dtypes.bfloat16)
    for place, part in ((0, hi), (GROUP, hi), (2 * GROUP, hi)):
        right[place : place + width] = part
    for place, part in ((128, mid), (128 + GROUP, lo), (128 + 2 * GROUP, mid)):
        right[place : place + width] = part
    outer = 2.0 * np.pi * (freq[None, :] * rows[:, None] % ROWS) / ROWS
    cos_out, sin_out = np.cos(outer), np.sin(outer)
    one = np.ones((ROWS, 1))
    block = rows[:, None] / ROWS
    cos_row = np.concatenate([cos_out, cos_out, one, one], axis=1)
    sin_row = np.concatenate([sin_out, sin_out, 0 * one, block], axis=1)
    turn = np.zeros((2, ROWS, 128), np.float32)
    for place in (0, GROUP, 2 * GROUP):
        turn[0, :, place : place + width] = cos_row
        turn[1, :, place : place + width] = sin_row
    pick = np.zeros((2, 128, 128), np.float32)
    for place in (0, GROUP, 2 * GROUP):
        for index in range(16):
            pick[0, 2 * index + 1, place + index] = 1.0
            pick[0, 2 * index + 2, place + 16 + index] = 1.0
            pick[1, 2 * index + 2, place + index] = 1.0
            pick[1, 2 * index + 1, place + 16 + index] = -1.0
        pick[0, 0, place + 32] = 1.0
        pick[0, EMB, place + 33] = 1.0
        pick[1, 0, place + 33] = 1.0
    back = np.zeros((COLS, 128))
    back[:, :width] = short.T
    back[:, 64:80] = short[16:32].T
    back[:, 80:96] = short[:16].T
    back_hi, back_lo = halves(back, 2)
    back_cat = np.concatenate([back_hi, back_lo], axis=1)
    back_turn = np.zeros((ROWS, 128), np.float32)
    back_turn[:, :32] = cos_row[:, :32]
    back_turn[:, 32] = 1.0
    back_turn[:, 33] = rows / ROWS
    back_turn[:, 64:80] = -sin_out
    back_turn[:, 80:96] = sin_out
    place = np.zeros((8, 8, 128), np.float32)
    for wanted in range(EMB):
        row, group = divmod(wanted, 8)
        if wanted == 0:
            lanes = (32, 33)
        elif wanted % 2:
            lanes = ((wanted - 1) // 2, 64 + (wanted - 1) // 2)
        else:
            lanes = (16 + (wanted - 2) // 2, 80 + (wanted - 2) // 2)
        for lane in lanes:
            place[group, row, lane] = 1.0
    return right, turn, pick, back_cat, back_turn, place


def split(value):
    hi = value.astype(BF16)
    lo = (value - hi.astype(F32)).astype(BF16)
    return hi, lo


def dot(left, right):
    return jnp.dot(left, right, preferred_element_type=F32)


def spectrum(signals, forward, twiddle_re, twiddle_im, full_hi, full_lo):
    wide = jnp.concatenate(signals, axis=1)
    section = dot(forward, jnp.concatenate([wide, wide], axis=0))
    turned = []
    for index in range(len(signals)):
        part = section[:, index * COLS : (index + 1) * COLS]
        part_re, part_im = part[:ROWS], part[ROWS:]
        turned.append(
            jnp.concatenate(
                [
                    part_re * twiddle_re - part_im * twiddle_im,
                    part_re * twiddle_im + part_im * twiddle_re,
                ],
                axis=1,
            )
        )
    return full_product(jnp.concatenate(turned, axis=0), full_hi, full_lo)


def full_product(value, full_hi, full_lo):
    hi, lo = split(value)
    return dot(hi, full_hi) + dot(lo, full_hi) + dot(hi, full_lo)


def restore(conj_spec, count, last, twiddle_re, twiddle_im, full_hi, full_lo):
    back = full_product(conj_spec, full_hi, full_lo)
    stacked = []
    for index in range(count):
        part = back[index * ROWS : (index + 1) * ROWS]
        part_re, part_im = part[:, :COLS], part[:, COLS:]
        stacked.append(
            jnp.concatenate(
                [
                    part_re * twiddle_re - part_im * twiddle_im,
                    part_re * twiddle_im + part_im * twiddle_re,
                ],
                axis=0,
            )
        )
    hi, lo = split(jnp.concatenate(stacked, axis=1))
    result = dot(last, jnp.concatenate([hi, hi, lo], axis=0))
    return [result[:, index * COLS : (index + 1) * COLS] for index in range(count)]


def take(ref, start, count, stride):
    return jnp.concatenate(
        [ref[half, pl.ds(start, count, stride=stride), :] for half in range(2)], axis=1
    )


def put(ref, start, count, stride, value):
    for half in range(2):
        ref[half, pl.ds(start, count, stride=stride), :] = value[:, half * 128 : half * 128 + 128]


def fill(ref, value):
    for half in range(2):
        ref[half] = value[..., half * 128 : half * 128 + 128].reshape(ref.shape[1], 128)


def begin(sems, pairs):
    copies = [
        pltpu.make_async_copy(source, target, sems.at[index])
        for index, (source, target) in enumerate(pairs)
    ]
    for copy in copies:
        copy.start()
    return copies


def picked(row, wanted):
    lane = lax.broadcasted_iota(jnp.int32, row.shape, 1)
    return jnp.sum(jnp.where(lane == wanted, row, 0.0), axis=1, keepdims=True)


def pack_kernel(query, key, value, grad, out, held, wide, sems):
    copies = begin(sems, [(ref, held.at[index]) for index, ref in enumerate((query, key, value, grad))])
    for index in range(4):
        copies[index].wait()
        block = held[index].astype(F32)
        for half in range(2):
            wide[half, index * 128 : (index + 1) * 128, :] = block[:, half * 128 : half * 128 + 128]
    for peer in range(ROWS):
        out[peer] = take(wide, peer, 8, ROWS).astype(BF16)


def expm1_small(value):
    series = jnp.ones_like(value)
    for order in range(9, 1, -1):
        series = 1.0 + value * series * (1.0 / order)
    return jnp.where(value > -0.5, value * series, jnp.exp(value) - 1.0)


def filter_kernel(
    own,
    weight_src,
    bias_src,
    proj_src,
    decay_src,
    pick_src,
    turn_src,
    right_src,
    forward_src,
    twiddle_src,
    full_src,
    act_out,
    cos_out,
    env_out,
    spec_out,
    column_out,
    weight,
    bias,
    proj,
    decay,
    pick,
    turn,
    right,
    forward,
    twiddle,
    full,
    layer,
    left,
    phase,
    filt,
    act,
    cosv,
    out_sems,
    sems,
):
    first = own[0]
    copies = begin(
        sems,
        [
            (weight_src, weight),
            (bias_src, bias),
            (pick_src, pick),
            (proj_src, proj),
            (turn_src, turn),
            (right_src, right),
            (decay_src, decay),
            (forward_src, forward),
            (twiddle_src, twiddle),
            (full_src, full),
        ],
    )
    layer[...] = jnp.zeros((128, 128), F32)
    for copy in copies[:3]:
        copy.wait()
    layer[0:EMB, 0:FEAT] = weight[...]
    layer[EMB : EMB + 1, 0:FEAT] = bias[...]
    layer_all = layer[...].T[0:FEAT, :]
    same = jnp.dot(layer_all, pick[0], precision=EXACT, preferred_element_type=F32) * TURN
    cross = jnp.dot(layer_all, pick[1], precision=EXACT, preferred_element_type=F32) * TURN
    lane = lax.broadcasted_iota(jnp.int32, (FEAT, 128), 1)
    sublane = lax.broadcasted_iota(jnp.int32, (8, 128), 0)
    for copy in copies[3:7]:
        copy.wait()
    columns = []
    for chan in range(CHAN):
        hit = lane == first + 64 * chan
        column = jnp.sum(jnp.where(hit, proj[...], 0.0), axis=1, keepdims=True)
        column_wide = jnp.broadcast_to(column, (FEAT, 128))
        column_out[chan * FEAT : (chan + 1) * FEAT, :] = column_wide
        columns.append(column_wide)

    def make_left(block, carry):
        value = same * turn[0, pl.ds(block, 1), :] + cross * turn[1, pl.ds(block, 1), :]
        hi = value.astype(BF16).astype(F32)
        rest = value - hi
        mid = rest.astype(BF16).astype(F32)
        lo = rest - mid
        one = jnp.where(lane < GROUP, hi, jnp.where(lane < 2 * GROUP, mid, lo))
        two = jnp.where(lane < 2 * GROUP, hi, mid)
        start = pl.multiple_of(block * FEAT, FEAT)
        left[pl.ds(start, FEAT), 0:128] = one.astype(BF16)
        left[pl.ds(start, FEAT), 128:256] = two.astype(BF16)
        return carry

    lax.fori_loop(0, ROWS, make_left, 0, unroll=4)

    def chunk(index, carry):
        base = pl.multiple_of(index * 512, 512)
        phase[...] = dot(left[pl.ds(base, 512), :], right[...])
        for half in range(2):
            lanes = slice(half * 128, half * 128 + 128)
            sums = [jnp.zeros((8, 128), F32)] * CHAN
            for inner in range(8):
                near = inner * FEAT
                turns = phase[near : near + FEAT, lanes]
                rest = turns - jnp.round(turns)
                square = rest * rest
                sine = SIN_COEF[-1] * square + SIN_COEF[-2]
                cosine = COS_COEF[-1] * square + COS_COEF[-2]
                for coef in SIN_COEF[-3::-1]:
                    sine = sine * square + coef
                for coef in COS_COEF[-3::-1]:
                    cosine = cosine * square + coef
                sine = sine * rest
                whole_sine = sine * cosine
                whole_cosine = 1.0 - sine * sine
                act[pl.ds(base + near, FEAT), lanes] = whole_sine.astype(BF16)
                cosv[pl.ds(base + near, FEAT), lanes] = whole_cosine.astype(BF16)
                for chan in range(CHAN):
                    total = jnp.sum(whole_sine * columns[chan], axis=0, keepdims=True)
                    sums[chan] = jnp.where(sublane == inner, total, sums[chan])
            for chan in range(CHAN):
                start = pl.multiple_of(chan * ROWS + index * 8, 8)
                filt[pl.ds(start, 8), lanes] = sums[chan]
        send(index, 0).start()
        send(index, 1).start()
        return carry

    def send(index, which):
        rows = pl.ds(pl.multiple_of(index * 512, 512), 512)
        source, target = ((act, act_out), (cosv, cos_out))[which]
        return pltpu.make_async_copy(source.at[rows], target.at[rows], out_sems.at[which, index])

    lax.fori_loop(0, 8, chunk, 0)
    ratio = decay[...] * (1.0 / TOTAL)
    energy = expm1_small(-2.0 * decay[...]) / expm1_small(-2.0 * ratio)
    norm = 1.0 / jnp.sqrt(energy)
    for copy in copies[7:]:
        copy.wait()
    position = (
        lax.broadcasted_iota(jnp.int32, (ROWS, COLS), 0) * COLS
        + lax.broadcasted_iota(jnp.int32, (ROWS, COLS), 1)
    ).astype(F32)
    signals = []
    for chan in range(CHAN):
        rate = picked(decay[...], first + 64 * chan)
        envelope = jnp.exp(-(rate * position) * (1.0 / TOTAL)) * picked(norm, first + 64 * chan)
        env_out[chan * ROWS : (chan + 1) * ROWS, :] = envelope
        signals.append((filt[chan * ROWS : (chan + 1) * ROWS, :] * envelope).astype(BF16))
    spec_out[...] = spectrum(signals, forward[...], twiddle[0], twiddle[1], full[0], full[1])
    for index in range(8):
        send(index, 0).wait()
        send(index, 1).wait()


def own_taps(first, short, taps, order):
    row = lax.broadcasted_iota(jnp.int32, (TAPS, 128), 0)
    lane = lax.broadcasted_iota(jnp.int32, (TAPS, 128), 1)
    columns = jnp.where(row == 0, 1.0, 0.0)
    for place, which in order:
        for chan in range(CHAN):
            hit = lane == first + 64 * chan
            column = jnp.sum(jnp.where(hit, short[which], 0.0), axis=1, keepdims=True)
            columns = jnp.where(lane == place + chan, column, columns)
    taps[...] = jnp.zeros((128, 128), F32)
    taps[0:TAPS, :] = columns
    return taps[...].T[0:8, :]


def gradient_kernel(
    own,
    arrived_src,
    envelope_src,
    columns_src,
    cosine_src,
    short_src,
    back_src,
    back_turn_src,
    place_src,
    forward_src,
    last_src,
    twiddle_src,
    full_src,
    feat_out,
    spec_out,
    raw_out,
    basis_out,
    arrived,
    envelope,
    columns,
    cosine,
    short,
    back,
    back_turn,
    place,
    forward,
    last,
    twiddle,
    full,
    taps,
    raw,
    feat,
    spec,
    out_sems,
    sems,
):
    first = own[0]
    copies = begin(
        sems,
        [
            (short_src, short),
            (arrived_src, arrived),
            (forward_src, forward),
            (twiddle_src, twiddle),
            (full_src, full),
            (last_src, last),
            (envelope_src, envelope),
            (cosine_src, cosine),
            (columns_src, columns),
            (back_src, back),
            (back_turn_src, back_turn),
            (place_src, place),
        ],
    )
    copies[0].wait()
    weights = own_taps(first, short, taps, ((0, 0), (2, 1), (4, 2)))
    copies[1].wait()
    signal = arrived[...].astype(F32)
    lane = lax.broadcasted_iota(jnp.int32, (ROWS, 8, COLS), 2)
    result = weights[None, :, 0:1] * signal
    zeros = jnp.zeros((1, 8, COLS), F32)
    for offset in range(1, TAPS):
        moved = pltpu.roll(signal, offset, 2)
        before = jnp.concatenate([zeros, moved[:-1]], axis=0)
        shifted = jnp.where(lane < offset, before, moved)
        result = result + weights[None, :, offset : offset + 1] * shifted
    fill(feat, result)
    leaving = begin(out_sems.at[pl.ds(0, 1)], [(feat, feat_out)])

    def plane(index):
        return take(feat, index, ROWS, 8)

    signals = []
    for chan in range(CHAN):
        signals.append((plane(2 + chan) * plane(4 + chan)).astype(BF16))
    for chan in range(CHAN):
        signals.append((plane(chan) * plane(6 + chan)).astype(BF16))
    for copy in copies[2:5]:
        copy.wait()
    tables = (twiddle[0], twiddle[1], full[0], full[1])
    spec_all = spectrum(signals, forward[...], *tables)
    spec[...] = spec_all
    leaving += begin(out_sems.at[pl.ds(1, 1)], [(spec, spec_out)])
    carried, grad = spec_all[: CHAN * ROWS], spec_all[CHAN * ROWS :]
    carried_re, carried_im = carried[:, :COLS], carried[:, COLS:]
    grad_re, grad_im = grad[:, :COLS], grad[:, COLS:]
    crossed = jnp.concatenate(
        [
            carried_re * grad_re + carried_im * grad_im,
            carried_im * grad_re - carried_re * grad_im,
        ],
        axis=1,
    )
    for copy in copies[5:7]:
        copy.wait()
    filter_grad = restore(crossed, CHAN, last[...], *tables)
    for chan in range(CHAN):
        rounded = filter_grad[chan].astype(BF16).astype(F32)
        scaled = rounded * envelope[chan * ROWS : (chan + 1) * ROWS, :]
        for half in range(2):
            raw[half, chan * ROWS : (chan + 1) * ROWS, :] = scaled[:, half * 128 : half * 128 + 128]
    leaving += begin(out_sems.at[pl.ds(2, 1)], [(raw, raw_out)])
    for copy in copies[7:]:
        copy.wait()
    column0 = columns[0:FEAT, :]
    column1 = columns[FEAT : 2 * FEAT, :]
    back_all = back[...]

    def chunk(index, basis_sum):
        base = pl.multiple_of(index * 512, 512)
        start = pl.multiple_of(index * 8, 8)
        rows = [
            [raw[half, pl.ds(chan * ROWS + start, 8), :] for half in range(2)] for chan in range(CHAN)
        ]
        angles = back_turn[pl.ds(start, 8), :]
        parts = []
        for inner in range(8):
            near = inner * FEAT
            pieces = []
            for half in range(2):
                lanes = slice(half * 128, half * 128 + 128)
                value = (
                    column0 * rows[0][half][inner : inner + 1, :]
                    + column1 * rows[1][half][inner : inner + 1, :]
                )
                value = value * cosine[pl.ds(base + near, FEAT), lanes].astype(F32)
                pieces.append(value.astype(BF16))
            parts.append(jnp.concatenate(pieces, axis=1))
        product = dot(jnp.concatenate(parts, axis=0), back_all)
        for inner in range(8):
            near = inner * FEAT
            both = product[near : near + FEAT, 0:128] + product[near : near + FEAT, 128:256]
            basis_sum = basis_sum + both * angles[inner : inner + 1, :]
        return basis_sum

    basis_sum = lax.fori_loop(0, 8, chunk, jnp.zeros((FEAT, 128), F32), unroll=2)
    pieces = [
        lax.dot_general(
            place[group],
            basis_sum,
            (((1,), (1,)), ((), ())),
            precision=EXACT,
            preferred_element_type=F32,
        )
        for group in range(8)
    ]
    for quarter in range(4):
        row = jnp.concatenate(
            [piece[:, quarter * 16 : quarter * 16 + 16] for piece in pieces], axis=1
        )
        for peer in range(8):
            basis_out[quarter * 8 + peer] = row
    for copy in leaving:
        copy.wait()


HALO = TAPS - 1


def output_kernel(
    own,
    feat_src,
    spec_src,
    filter_spec_src,
    raw_src,
    act_src,
    arrived_src,
    skip_src,
    last_src,
    twiddle_src,
    full_src,
    out,
    feat,
    spec,
    filter_spec,
    raw,
    act,
    arrived,
    skip,
    last,
    twiddle,
    full,
    input_tail,
    rows_out,
    sems,
):
    first = own[0]
    copies = begin(
        sems,
        [
            (raw_src, raw),
            (act_src, act),
            (spec_src, spec),
            (filter_spec_src, filter_spec),
            (full_src, full),
            (twiddle_src, twiddle),
            (last_src, last),
            (skip_src, skip),
            (feat_src, feat),
            (arrived_src, arrived),
        ],
    )
    lane128 = lax.broadcasted_iota(jnp.int32, (FEAT, 128), 1)
    row_lane = lane128 % 8
    copies[0].wait()
    copies[1].wait()

    def chunk(index, proj_sum):
        base = pl.multiple_of(index * 512, 512)
        start = pl.multiple_of(index * 8, 8)
        rows = [
            jnp.concatenate(
                [raw[half, pl.ds(chan * ROWS + start, 8), :] for half in range(2)], axis=1
            )
            for chan in range(CHAN)
        ]
        wide = jnp.concatenate(rows, axis=0)
        hi = wide.astype(BF16).astype(F32)
        packed = jnp.concatenate([hi, wide - hi, jnp.zeros((128 - 4 * 8, COLS), F32)], axis=0)
        turned = jnp.concatenate(
            [packed[:, half * 128 : half * 128 + 128].T for half in range(2)], axis=0
        ).astype(BF16)
        product = dot(act[pl.ds(base, 512), :], turned)
        for inner in range(8):
            near = inner * FEAT
            proj_sum = proj_sum + jnp.where(row_lane == inner, product[near : near + FEAT, :], 0.0)
        return proj_sum

    proj_sum = lax.fori_loop(0, 8, chunk, jnp.zeros((FEAT, 128), F32), unroll=2)
    own_lane = lane128 % 16
    stacked = jnp.concatenate(
        [jnp.where(own_lane < 8, proj_sum, 0.0), jnp.where(own_lane >= 8, proj_sum, 0.0)], axis=0
    )
    proj_wide = lax.dot_general(
        jnp.ones((8, 128), F32),
        stacked,
        (((1,), (1,)), ((), ())),
        precision=EXACT,
        preferred_element_type=F32,
    )
    proj_hi = proj_wide.astype(BF16).astype(F32)
    for copy in copies[2:7]:
        copy.wait()
    tables = (twiddle[0], twiddle[1], full[0], full[1])
    carried, grad = spec[0 : CHAN * ROWS, :], spec[CHAN * ROWS : 2 * CHAN * ROWS, :]
    filt = filter_spec[...]
    carried_re, carried_im = carried[:, :COLS], carried[:, COLS:]
    grad_re, grad_im = grad[:, :COLS], grad[:, COLS:]
    filt_re, filt_im = filt[:, :COLS], filt[:, COLS:]
    crossed = jnp.concatenate(
        [
            jnp.concatenate(
                [
                    filt_re * carried_re - filt_im * carried_im,
                    -(filt_re * carried_im + filt_im * carried_re),
                ],
                axis=1,
            ),
            jnp.concatenate(
                [
                    filt_re * grad_re + filt_im * grad_im,
                    filt_im * grad_re - filt_re * grad_im,
                ],
                axis=1,
            ),
        ],
        axis=0,
    )
    sums = restore(crossed, 2 * CHAN, last[...], *tables)
    for copy in copies[7:]:
        copy.wait()
    input_tail[...] = arrived[:, :, 128:256].astype(F32).reshape(ROWS * 8, 128)

    def plane(index):
        return take(feat, index, ROWS, 8)

    blank = jnp.zeros((1, 128), F32)
    for chan in range(CHAN):
        gain = picked(skip[...], first + 64 * chan)
        query, key, value, cotangent = [plane(2 * index + chan) for index in range(4)]
        carried_own = (key * value).astype(BF16).astype(F32)
        grad_own = (query * cotangent).astype(BF16).astype(F32)
        long_out = (sums[chan] + gain * carried_own).astype(BF16).astype(F32)
        carried_grad = (sums[CHAN + chan] + gain * grad_own).astype(BF16).astype(F32)
        put(rows_out, chan, ROWS, 8, long_out)
        put(rows_out, 2 + chan, ROWS, 8, carried_grad)
        follow = jnp.zeros((ROWS, 128), F32)
        before = jnp.zeros((ROWS, 128), F32)
        heads = (
            cotangent[:, 0:128] * long_out[:, 0:128],
            carried_grad[:, 0:128] * value[:, 0:128],
            carried_grad[:, 0:128] * key[:, 0:128],
        )
        for index in range(3):
            head = heads[index].astype(BF16).astype(F32)
            place = HALO * index
            head = pltpu.roll(head, place, 1) if place else head
            follow = jnp.where((lane128 >= place) & (lane128 < place + HALO), head, follow)
            tail = input_tail[pl.ds(2 * index + chan, ROWS, stride=8), :]
            place = HALO * (3 + index)
            tail = pltpu.roll(tail, HALO + place, 1)
            before = jnp.where((lane128 >= place) & (lane128 < place + HALO), tail, before)
        halo = jnp.concatenate([follow[1:], blank], axis=0) + jnp.concatenate(
            [blank, before[:-1]], axis=0
        )
        rows_out[chan, pl.ds(4, ROWS, stride=8), :] = halo
    row = lax.broadcasted_iota(jnp.int32, (ROWS, 8, 128), 1)
    for half, proj_part in enumerate((proj_hi, proj_wide - proj_hi)):
        extra = jnp.where(row == 7, proj_part[None], 0.0)
        value = jnp.where(row < 5, rows_out[half].reshape(ROWS, 8, 128), extra)
        out[:, :, half * 128 : half * 128 + 128] = value.astype(BF16)


def compose_kernel(packed, basis_parts, out):
    basis = basis_parts[0]
    for source in range(1, 32):
        basis = basis + basis_parts[source]
    row = lax.broadcasted_iota(jnp.int32, (8, 128), 0)
    lane = lax.broadcasted_iota(jnp.int32, (8, 128), 1)
    last = jnp.where((lane >= 64) & (lane < 80), pltpu.roll(basis, 64, 1)[4:5], 0.0)
    left = jnp.where(
        row == 4, last, jnp.where(row == 5, basis[0:1], jnp.where(row == 6, basis[2:3], 0.0))
    )
    right = jnp.where(row == 5, basis[1:2], jnp.where(row == 6, basis[3:4], 0.0))
    extra = jnp.concatenate([left, right], axis=1)
    out[...] = (packed[...].astype(F32) + extra[None]).astype(BF16)


def local_kernel(
    query_src, key_src, value_src, short_src, feat_out, taps_out, query, key, value, short, sems
):
    copies = begin(
        sems, [(query_src, query), (key_src, key), (value_src, value), (short_src, short)]
    )
    lane = lax.broadcasted_iota(jnp.int32, (128, 128), 1)
    for copy in copies:
        copy.wait()
    for index, ref in enumerate((query, key, value)):
        taps_out[index] = jnp.concatenate(
            [short[index], jnp.zeros((128 - TAPS, 128), F32)], axis=0
        ).T
        weights = taps_out[index]
        block = ref[...].astype(F32)
        left, right = block[:, 0:128], block[:, 128:256]
        out_left = weights[:, 0:1] * left
        out_right = weights[:, 0:1] * right
        for offset in range(1, TAPS):
            weight = weights[:, offset : offset + 1]
            moved_left = pltpu.roll(left, offset, 1)
            moved_right = pltpu.roll(right, offset, 1)
            out_left = out_left + weight * jnp.where(lane < offset, 0.0, moved_left)
            out_right = out_right + weight * jnp.where(lane < offset, moved_left, moved_right)
        feat_out[index, :, 0:128] = out_left
        feat_out[index, :, 128:256] = out_right


def unpack_kernel(
    arrived,
    feat_src,
    taps_src,
    grad_src,
    mixed,
    grad_query,
    grad_key,
    grad_value,
    proj,
    basis,
    feat,
    taps,
    grad,
    wide,
    sorted_rows,
    sems,
):
    copies = begin(sems, [(feat_src, feat), (taps_src, taps), (grad_src, grad)])
    fill(wide, arrived[...].astype(F32))

    def both(half, row):
        return jnp.concatenate(
            [wide[half, pl.ds(row + chan, ROWS, stride=8), :] for chan in range(CHAN)], axis=0
        )

    long_out = [both(half, 0) for half in range(2)]
    carried_grad = [both(half, 2) for half in range(2)]
    halo = jnp.concatenate([wide[half, pl.ds(4, ROWS, stride=8), :] for half in range(2)], axis=0)
    lane = lax.broadcasted_iota(jnp.int32, (128, 128), 1)
    for copy in copies:
        copy.wait()
    feats = []
    for index in range(3):
        left = feat[index, :, 0:128]
        for offset in range(1, TAPS):
            moved = pltpu.roll(halo, (offset - HALO * (4 + index)) % 128, 1)
            left = left + taps[index, :, offset : offset + 1] * jnp.where(lane < offset, moved, 0.0)
        feats.append((left, feat[index, :, 128:256]))
    cotangent = grad[...].astype(F32)
    cotangent = (cotangent[:, 0:128], cotangent[:, 128:256])
    for half in range(2):
        mixed[:, half * 128 : half * 128 + 128] = (feats[0][half] * long_out[half]).astype(BF16)
    grads = (
        [cotangent[half] * long_out[half] for half in range(2)],
        [carried_grad[half] * feats[2][half] for half in range(2)],
        [carried_grad[half] * feats[1][half] for half in range(2)],
    )
    for index, ref in enumerate((grad_query, grad_key, grad_value)):
        left, right = [part.astype(BF16).astype(F32) for part in grads[index]]
        out_left = taps[index, :, 0:1] * left
        out_right = taps[index, :, 0:1] * right
        for offset in range(1, TAPS):
            weight = taps[index, :, offset : offset + 1]
            moved_left = pltpu.roll(left, 128 - offset, 1)
            moved_right = pltpu.roll(right, 128 - offset, 1)
            moved_halo = pltpu.roll(halo, (128 - offset - HALO * index) % 128, 1)
            edge = lane >= 128 - offset
            out_left = out_left + weight * jnp.where(edge, moved_right, moved_left)
            out_right = out_right + weight * jnp.where(edge, moved_halo, moved_right)
        ref[:, 0:128] = out_left.astype(BF16)
        ref[:, 128:256] = out_right.astype(BF16)
    rows = wide[0, pl.ds(7, ROWS, stride=8), :] + wide[1, pl.ds(7, ROWS, stride=8), :]
    rows = rows * (1.0 / math.sqrt(TOTAL))
    rows = jnp.concatenate([rows, jnp.zeros_like(rows)], axis=0).T
    proj[:, 0:ROWS] = rows[0:FEAT, 0:ROWS]
    proj[:, ROWS : 2 * ROWS] = rows[FEAT : 2 * FEAT, 0:ROWS]
    totals = []
    for quarter in range(4):
        pair = []
        for half in range(2):
            total = wide[half, quarter * 8 : quarter * 8 + 8, :]
            for source in range(quarter + 4, ROWS, 4):
                total = total + wide[half, source * 8 : source * 8 + 8, :]
            pair.append(total)
        totals.append(pair)
    scale = math.sqrt(FEAT / (TOTAL * 1024))
    ordered = [
        jnp.concatenate([left[5:6], right[5:6], left[6:7], right[6:7]], axis=0)
        for left, right in totals
    ]
    for group in range(8):
        lanes = slice(group * 16, group * 16 + 16)
        merged = jnp.concatenate(
            [value[:, lanes] for value in ordered] + [jnp.zeros((4, 64), F32)], axis=1
        )
        sorted_rows[pl.ds(group, 4, stride=8), :] = merged * scale
    sorted_rows[32:33, :] = (
        jnp.concatenate([left[4:5, 64:80] for left, _ in totals] + [jnp.zeros((1, 64), F32)], axis=1)
        * scale
    )
    basis[...] = sorted_rows[0:EMB, 0:FEAT]


SMEM = pl.BlockSpec(memory_space=pltpu.SMEM)
VMEM = pl.BlockSpec(memory_space=pltpu.VMEM)
HBM = pl.BlockSpec(memory_space=pltpu.HBM)
LIMIT = 62 * 1024 * 1024
ROOMY = 32 * 1024 * 1024


def call(kernel, name, own, near, far, outs, scratch, flops, moved, limit=LIMIT):
    landing = [pltpu.VMEM(value.shape, value.dtype) for value in far]
    return pl.pallas_call(
        kernel,
        name=name,
        in_specs=[SMEM] * len(own) + [VMEM] * len(near) + [HBM] * len(far),
        out_specs=[HBM if direct else VMEM for _, direct in outs],
        out_shape=[value for value, _ in outs],
        scratch_shapes=(landing if kernel is not pack_kernel else [])
        + scratch
        + ([pltpu.SemaphoreType.DMA((len(far),))] if far else []),
        compiler_params=pltpu.CompilerParams(vmem_limit_bytes=limit),
        cost_estimate=pl.CostEstimate(flops=flops, bytes_accessed=moved, transcendentals=0),
    )(*own, *near, *far)


def shape(dims, kind=F32):
    return jax.ShapeDtypeStruct(dims, kind)


def run_pack(query_in, key_in, value_in, grad_out):
    return call(
        pack_kernel,
        "pack",
        [],
        [],
        [query_in, key_in, value_in, grad_out],
        [(shape((ROWS, 8, COLS), BF16), False)],
        [pltpu.VMEM((4, 128, COLS), BF16), pltpu.VMEM((2, 512, 128), F32)],
        1 << 20,
        1 << 19,
    )[0]


def run_filter(own, weight, bias, proj, decay, consts):
    names = ("pick", "turn", "right", "forward", "twiddle", "full")
    return call(
        filter_kernel,
        "filter",
        [own],
        [],
        [weight, bias, proj, decay] + [consts[name] for name in names],
        [
            (shape((ROWS * FEAT, COLS), BF16), True),
            (shape((ROWS * FEAT, COLS), BF16), True),
            (shape((CHAN * ROWS, COLS)), False),
            (shape((CHAN * ROWS, 2 * COLS)), False),
            (shape((CHAN * FEAT, 128)), False),
        ],
        [
            pltpu.VMEM((128, 128), F32),
            pltpu.VMEM((ROWS * FEAT, COLS), BF16),
            pltpu.VMEM((512, COLS), F32),
            pltpu.VMEM((CHAN * ROWS, COLS), F32),
            pltpu.VMEM((ROWS * FEAT, COLS), BF16),
            pltpu.VMEM((ROWS * FEAT, COLS), BF16),
            pltpu.SemaphoreType.DMA((2, 8)),
        ],
        1 << 33,
        1 << 23,
    )


def run_gradient(own, arrived, short, cosine, envelope, columns, consts):
    names = ("back", "back_turn", "place", "forward", "last", "twiddle", "full")
    return call(
        gradient_kernel,
        "gradient",
        [own],
        [],
        [arrived, envelope, columns, cosine, short] + [consts[name] for name in names],
        [
            (shape((2, ROWS * 8, 128)), True),
            (shape((2 * CHAN * ROWS, 2 * COLS)), True),
            (shape((2, CHAN * ROWS, 128)), True),
            (shape((32, 8, 128)), False),
        ],
        [
            pltpu.VMEM((128, 128), F32),
            pltpu.VMEM((2, CHAN * ROWS, 128), F32),
            pltpu.VMEM((2, ROWS * 8, 128), F32),
            pltpu.VMEM((2 * CHAN * ROWS, 2 * COLS), F32),
            pltpu.SemaphoreType.DMA((3,)),
        ],
        1 << 32,
        1 << 23,
    )


def run_output(own, skip, feat, spec, filter_spec, raw, act, arrived, consts):
    names = ("last", "twiddle", "full")
    return call(
        output_kernel,
        "output",
        [own],
        [],
        [feat, spec, filter_spec, raw, act, arrived, skip] + [consts[name] for name in names],
        [(shape((ROWS, 8, COLS), BF16), False)],
        [pltpu.VMEM((ROWS * 8, 128), F32), pltpu.VMEM((2, ROWS * 8, 128), F32)],
        1 << 31,
        1 << 22,
    )[0]


def run_compose(packed, basis_parts):
    return call(
        compose_kernel,
        "compose",
        [],
        [packed, basis_parts],
        [],
        [(shape((ROWS, 8, COLS), BF16), False)],
        [],
        1 << 20,
        1 << 20,
        ROOMY,
    )[0]


def run_local(query_in, key_in, value_in, short):
    return call(
        local_kernel,
        "local",
        [],
        [],
        [query_in, key_in, value_in, short],
        [(shape((3, 128, COLS)), False), (shape((3, 128, 128)), False)],
        [],
        1 << 28,
        1 << 20,
    )


def run_unpack(arrived, feat, taps, grad_out):
    block = shape((128, COLS), BF16)
    return call(
        unpack_kernel,
        "unpack",
        [],
        [arrived],
        [feat, taps, grad_out],
        [(value, False) for value in [block] * 4 + [shape((FEAT, 128)), shape((EMB, FEAT))]],
        [pltpu.VMEM((2, ROWS * 8, 128), F32), pltpu.VMEM((64, 128), F32)],
        1 << 20,
        1 << 20,
        ROOMY,
    )


def make_consts():
    forward, last, twiddle, full = transform_tables()
    right, turn, pick, back, back_turn, place = basis_tables()
    return dict(
        forward=jnp.asarray(forward),
        last=jnp.asarray(last),
        twiddle=jnp.asarray(twiddle),
        full=jnp.asarray(full),
        right=jnp.asarray(right),
        turn=jnp.asarray(turn),
        pick=jnp.asarray(pick),
        back=jnp.asarray(back),
        back_turn=jnp.asarray(back_turn),
        place=jnp.asarray(place),
    )


CTX = ("zh", "yh", "yl", "core")
NEAR = ("yl", "core", "x", "zl")


def exchange(value, axes):
    return lax.all_to_all(value, axes, split_axis=0, concat_axis=0, tiled=True)


def on_device(
    query_in,
    key_in,
    value_in,
    short_kernel,
    basis_weight,
    basis_bias,
    filter_proj,
    decay_rate,
    skip_gain,
    grad_out,
):
    consts = make_consts()
    own = lax.axis_index(CTX).astype(jnp.int32).reshape(1)
    with jax.named_scope("spread"):
        arrived = exchange(run_pack(query_in, key_in, value_in, grad_out), CTX)
    short = short_kernel.transpose(0, 2, 1)
    block_feat, block_taps = run_local(query_in, key_in, value_in, short)
    act, cosine, envelope, filter_spec, columns = run_filter(
        own,
        basis_weight.T,
        basis_bias.reshape(1, FEAT),
        filter_proj.T,
        decay_rate.reshape(1, 128),
        consts,
    )
    feat, spec, raw, basis_own = run_gradient(
        own, arrived, short, cosine, envelope, columns, consts
    )
    with jax.named_scope("basis"):
        basis_parts = exchange(basis_own, NEAR)
    packed = run_output(
        own, skip_gain.reshape(1, 128), feat, spec, filter_spec, raw, act, arrived, consts
    )
    composed = run_compose(packed, basis_parts)
    with jax.named_scope("collect"):
        returned = exchange(composed, CTX)
    mixed, grad_query, grad_key, grad_value, grad_proj, grad_basis = run_unpack(
        returned, block_feat, block_taps, grad_out
    )
    return (mixed, grad_query, grad_key, grad_value, grad_proj.T, grad_basis.T)


def solution(mesh):
    finer = Mesh(mesh.devices.reshape(4, 4, 2, 2, 4, 2), CTX + ("x", "zl"))
    rows = ("x", "zl")
    block = P(rows, CTX)
    return jax.shard_map(
        on_device,
        mesh=finer,
        in_specs=(
            block,
            block,
            block,
            P(None, rows, None),
            P(),
            P(),
            P(rows, None),
            P(rows),
            P(rows),
            block,
        ),
        out_specs=(block, block, block, block, P(rows, None), P()),
        check_vma=False,
    )
```

```python
import math

import jax
import jax.numpy as jnp
import numpy as np
from jax import lax
from jax.experimental import pallas as pl
from jax.experimental.pallas import tpu as pltpu
from jax.sharding import Mesh
from jax.sharding import PartitionSpec as P
import ml_dtypes

F32 = jnp.float32
BF16 = jnp.bfloat16
EXACT = lax.Precision.HIGHEST

ROWS = 64
COLS = 256
TOTAL = ROWS * COLS
FEAT = 64
EMB = 33
TAPS = 7
CHAN = 2
GROUP = 40
TURN = 1.0 / (2.0 * math.pi)

SIN_COEF = (4.442879676818848, -7.307816505432129, 3.5977742671966553, -0.7911993861198425)
COS_COEF = (
    1.4142135381698608,
    -6.978850841522217,
    5.739460468292236,
    -1.883557915687561,
    0.3106880187988281,
)


def halves(table, count):
    parts = []
    rest = np.asarray(table, np.float64)
    for _ in range(count):
        part = rest.astype(np.float32).astype(ml_dtypes.bfloat16)
        parts.append(part)
        rest = rest - part.astype(np.float64)
    return parts


def transform_tables():
    rows = np.arange(ROWS)
    cols = np.arange(COLS)
    first = 2.0 * np.pi * ((4 * rows[:, None] + 1) * rows[None, :] % (4 * ROWS)) / (4 * ROWS)
    first_re, first_im = np.cos(first), -np.sin(first)
    forward = np.concatenate([first_re, first_im], axis=0)
    forward_cat = np.concatenate(halves(forward, 2), axis=1)
    last = np.concatenate([first_re.T, -first_im.T], axis=1) / TOTAL
    last_hi, last_lo = halves(last, 2)
    last_cat = np.concatenate([last_hi, last_lo, last_hi], axis=1)
    turn = 2.0 * np.pi * ((4 * rows[:, None] + 1) * cols[None, :]) / (4 * TOTAL)
    twiddle = np.stack([np.cos(turn), -np.sin(turn)]).astype(np.float32)
    inner = 2.0 * np.pi * (cols[:, None] * cols[None, :] % COLS) / COLS
    inner_re, inner_im = np.cos(inner), -np.sin(inner)
    full = np.concatenate(
        [
            np.concatenate([inner_re, inner_im], axis=1),
            np.concatenate([-inner_im, inner_re], axis=1),
        ],
        axis=0,
    )
    full_hi, full_lo = halves(full, 2)
    return forward_cat, last_cat, twiddle, np.stack([full_hi, full_lo])


def basis_tables():
    freq = np.arange(1, 17)
    cols = np.arange(COLS)
    rows = np.arange(ROWS)
    inner = 2.0 * np.pi * (freq[:, None] * cols[None, :] % TOTAL) / TOTAL
    short = np.concatenate(
        [np.cos(inner), np.sin(inner), cols[None, :] / TOTAL, np.ones((1, COLS))], axis=0
    )
    width = short.shape[0]
    hi, mid, lo = halves(short, 3)
    right = np.zeros((256, COLS), ml_dtypes.bfloat16)
    for place, part in ((0, hi), (GROUP, hi), (2 * GROUP, hi)):
        right[place : place + width] = part
    for place, part in ((128, mid), (128 + GROUP, lo), (128 + 2 * GROUP, mid)):
        right[place : place + width] = part
    outer = 2.0 * np.pi * (freq[None, :] * rows[:, None] % ROWS) / ROWS
    cos_out, sin_out = np.cos(outer), np.sin(outer)
    one = np.ones((ROWS, 1))
    block = rows[:, None] / ROWS
    cos_row = np.concatenate([cos_out, cos_out, one, one], axis=1)
    sin_row = np.concatenate([sin_out, sin_out, 0 * one, block], axis=1)
    turn = np.zeros((2, ROWS, 128), np.float32)
    for place in (0, GROUP, 2 * GROUP):
        turn[0, :, place : place + width] = cos_row
        turn[1, :, place : place + width] = sin_row
    pick = np.zeros((2, 128, 128), np.float32)
    for place in (0, GROUP, 2 * GROUP):
        for index in range(16):
            pick[0, 2 * index + 1, place + index] = 1.0
            pick[0, 2 * index + 2, place + 16 + index] = 1.0
            pick[1, 2 * index + 2, place + index] = 1.0
            pick[1, 2 * index + 1, place + 16 + index] = -1.0
        pick[0, 0, place + 32] = 1.0
        pick[0, EMB, place + 33] = 1.0
        pick[1, 0, place + 33] = 1.0
    back = np.zeros((COLS, 128))
    back[:, :width] = short.T
    back[:, 64:80] = short[16:32].T
    back[:, 80:96] = short[:16].T
    back_hi, back_lo = halves(back, 2)
    back_cat = np.concatenate([back_hi, back_lo], axis=1)
    back_turn = np.zeros((ROWS, 128), np.float32)
    back_turn[:, :32] = cos_row[:, :32]
    back_turn[:, 32] = 1.0
    back_turn[:, 33] = rows / ROWS
    back_turn[:, 64:80] = -sin_out
    back_turn[:, 80:96] = sin_out
    place = np.zeros((8, 8, 128), np.float32)
    for wanted in range(EMB):
        row, group = divmod(wanted, 8)
        if wanted == 0:
            lanes = (32, 33)
        elif wanted % 2:
            lanes = ((wanted - 1) // 2, 64 + (wanted - 1) // 2)
        else:
            lanes = (16 + (wanted - 2) // 2, 80 + (wanted - 2) // 2)
        for lane in lanes:
            place[group, row, lane] = 1.0
    return right, turn, pick, back_cat, back_turn, place


def split(value):
    hi = value.astype(BF16)
    lo = (value - hi.astype(F32)).astype(BF16)
    return hi, lo


def dot(left, right):
    return jnp.dot(left, right, preferred_element_type=F32)


def spectrum(signals, forward, twiddle_re, twiddle_im, full_hi, full_lo):
    wide = jnp.concatenate(signals, axis=1)
    section = dot(forward, jnp.concatenate([wide, wide], axis=0))
    turned = []
    for index in range(len(signals)):
        part = section[:, index * COLS : (index + 1) * COLS]
        part_re, part_im = part[:ROWS], part[ROWS:]
        turned.append(
            jnp.concatenate(
                [
                    part_re * twiddle_re - part_im * twiddle_im,
                    part_re * twiddle_im + part_im * twiddle_re,
                ],
                axis=1,
            )
        )
    return full_product(jnp.concatenate(turned, axis=0), full_hi, full_lo)


def full_product(value, full_hi, full_lo):
    hi, lo = split(value)
    return dot(hi, full_hi) + dot(lo, full_hi) + dot(hi, full_lo)


def restore(conj_spec, count, last, twiddle_re, twiddle_im, full_hi, full_lo):
    back = full_product(conj_spec, full_hi, full_lo)
    stacked = []
    for index in range(count):
        part = back[index * ROWS : (index + 1) * ROWS]
        part_re, part_im = part[:, :COLS], part[:, COLS:]
        stacked.append(
            jnp.concatenate(
                [
                    part_re * twiddle_re - part_im * twiddle_im,
                    part_re * twiddle_im + part_im * twiddle_re,
                ],
                axis=0,
            )
        )
    hi, lo = split(jnp.concatenate(stacked, axis=1))
    result = dot(last, jnp.concatenate([hi, hi, lo], axis=0))
    return [result[:, index * COLS : (index + 1) * COLS] for index in range(count)]


def take(ref, start, count, stride):
    return jnp.concatenate(
        [ref[half, pl.ds(start, count, stride=stride), :] for half in range(2)], axis=1
    )


def put(ref, start, count, stride, value):
    for half in range(2):
        ref[half, pl.ds(start, count, stride=stride), :] = value[:, half * 128 : half * 128 + 128]


def fill(ref, value):
    for half in range(2):
        ref[half] = value[..., half * 128 : half * 128 + 128].reshape(ref.shape[1], 128)


def begin(sems, pairs):
    copies = [
        pltpu.make_async_copy(source, target, sems.at[index])
        for index, (source, target) in enumerate(pairs)
    ]
    for copy in copies:
        copy.start()
    return copies


def picked(row, wanted):
    lane = lax.broadcasted_iota(jnp.int32, row.shape, 1)
    return jnp.sum(jnp.where(lane == wanted, row, 0.0), axis=1, keepdims=True)


def pack_kernel(query, key, value, grad, out, held, wide, sems):
    copies = begin(sems, [(ref, held.at[index]) for index, ref in enumerate((query, key, value, grad))])
    for index in range(4):
        copies[index].wait()
        block = held[index].astype(F32)
        for half in range(2):
            wide[half, index * 128 : (index + 1) * 128, :] = block[:, half * 128 : half * 128 + 128]
    for peer in range(ROWS):
        out[peer] = take(wide, peer, 8, ROWS).astype(BF16)


def expm1_small(value):
    series = jnp.ones_like(value)
    for order in range(9, 1, -1):
        series = 1.0 + value * series * (1.0 / order)
    return jnp.where(value > -0.5, value * series, jnp.exp(value) - 1.0)


def filter_kernel(
    own,
    weight_src,
    bias_src,
    proj_src,
    decay_src,
    pick_src,
    turn_src,
    right_src,
    forward_src,
    twiddle_src,
    full_src,
    act_out,
    cos_out,
    env_out,
    spec_out,
    column_out,
    weight,
    bias,
    proj,
    decay,
    pick,
    turn,
    right,
    forward,
    twiddle,
    full,
    layer,
    left,
    phase,
    phase_odd,
    filt,
    act,
    cosv,
    out_sems,
    sems,
):
    first = own[0]
    copies = begin(
        sems,
        [
            (weight_src, weight),
            (bias_src, bias),
            (pick_src, pick),
            (proj_src, proj),
            (turn_src, turn),
            (right_src, right),
            (decay_src, decay),
            (forward_src, forward),
            (twiddle_src, twiddle),
            (full_src, full),
        ],
    )
    layer[...] = jnp.zeros((128, 128), F32)
    for copy in copies[:3]:
        copy.wait()
    layer[0:EMB, 0:FEAT] = weight[...]
    layer[EMB : EMB + 1, 0:FEAT] = bias[...]
    layer_all = layer[...].T[0:FEAT, :]
    same = jnp.dot(layer_all, pick[0], precision=EXACT, preferred_element_type=F32) * TURN
    cross = jnp.dot(layer_all, pick[1], precision=EXACT, preferred_element_type=F32) * TURN
    lane = lax.broadcasted_iota(jnp.int32, (FEAT, 128), 1)
    sublane = lax.broadcasted_iota(jnp.int32, (8, 128), 0)
    for copy in copies[3:7]:
        copy.wait()
    columns = []
    for chan in range(CHAN):
        hit = lane == first + 64 * chan
        column = jnp.sum(jnp.where(hit, proj[...], 0.0), axis=1, keepdims=True)
        column_wide = jnp.broadcast_to(column, (FEAT, 128))
        column_out[chan * FEAT : (chan + 1) * FEAT, :] = column_wide
        columns.append(column_wide)

    def make_left(block, carry):
        value = same * turn[0, pl.ds(block, 1), :] + cross * turn[1, pl.ds(block, 1), :]
        hi = value.astype(BF16).astype(F32)
        rest = value - hi
        mid = rest.astype(BF16).astype(F32)
        lo = rest - mid
        one = jnp.where(lane < GROUP, hi, jnp.where(lane < 2 * GROUP, mid, lo))
        two = jnp.where(lane < 2 * GROUP, hi, mid)
        start = pl.multiple_of(block * FEAT, FEAT)
        left[pl.ds(start, FEAT), 0:128] = one.astype(BF16)
        left[pl.ds(start, FEAT), 128:256] = two.astype(BF16)
        return carry

    lax.fori_loop(0, ROWS, make_left, 0, unroll=4)

    def fetch(index, phase):
        base = pl.multiple_of(index * 512, 512)
        phase[...] = dot(left[pl.ds(base, 512), :], right[...])

    def finish(index, phase):
        base = pl.multiple_of(index * 512, 512)
        for half in range(2):
            lanes = slice(half * 128, half * 128 + 128)
            sums = [jnp.zeros((8, 128), F32)] * CHAN
            for inner in range(8):
                near = inner * FEAT
                turns = phase[near : near + FEAT, lanes]
                rest = turns - jnp.round(turns)
                square = rest * rest
                sine = SIN_COEF[-1] * square + SIN_COEF[-2]
                cosine = COS_COEF[-1] * square + COS_COEF[-2]
                for coef in SIN_COEF[-3::-1]:
                    sine = sine * square + coef
                for coef in COS_COEF[-3::-1]:
                    cosine = cosine * square + coef
                sine = sine * rest
                whole_sine = sine * cosine
                whole_cosine = 1.0 - sine * sine
                act[pl.ds(base + near, FEAT), lanes] = whole_sine.astype(BF16)
                cosv[pl.ds(base + near, FEAT), lanes] = whole_cosine.astype(BF16)
                for chan in range(CHAN):
                    total = jnp.sum(whole_sine * columns[chan], axis=0, keepdims=True)
                    sums[chan] = jnp.where(sublane == inner, total, sums[chan])
            for chan in range(CHAN):
                start = pl.multiple_of(chan * ROWS + index * 8, 8)
                filt[pl.ds(start, 8), lanes] = sums[chan]
        send(index, 0).start()
        send(index, 1).start()

    def pair(index, carry):
        fetch(2 * index + 1, phase_odd)
        finish(2 * index, phase)
        fetch(jnp.minimum(2 * index + 2, 7), phase)
        finish(2 * index + 1, phase_odd)
        return carry

    def send(index, which):
        rows = pl.ds(pl.multiple_of(index * 512, 512), 512)
        source, target = ((act, act_out), (cosv, cos_out))[which]
        return pltpu.make_async_copy(source.at[rows], target.at[rows], out_sems.at[which, index])

    fetch(0, phase)
    lax.fori_loop(0, 4, pair, 0)
    ratio = decay[...] * (1.0 / TOTAL)
    energy = expm1_small(-2.0 * decay[...]) / expm1_small(-2.0 * ratio)
    norm = 1.0 / jnp.sqrt(energy)
    for copy in copies[7:]:
        copy.wait()
    position = (
        lax.broadcasted_iota(jnp.int32, (ROWS, COLS), 0) * COLS
        + lax.broadcasted_iota(jnp.int32, (ROWS, COLS), 1)
    ).astype(F32)
    signals = []
    for chan in range(CHAN):
        rate = picked(decay[...], first + 64 * chan)
        envelope = jnp.exp(-(rate * position) * (1.0 / TOTAL)) * picked(norm, first + 64 * chan)
        env_out[chan * ROWS : (chan + 1) * ROWS, :] = envelope
        signals.append((filt[chan * ROWS : (chan + 1) * ROWS, :] * envelope).astype(BF16))
    spec_out[...] = spectrum(signals, forward[...], twiddle[0], twiddle[1], full[0], full[1])
    for index in range(8):
        send(index, 0).wait()
        send(index, 1).wait()


def own_taps(first, short, taps, order):
    row = lax.broadcasted_iota(jnp.int32, (TAPS, 128), 0)
    lane = lax.broadcasted_iota(jnp.int32, (TAPS, 128), 1)
    columns = jnp.where(row == 0, 1.0, 0.0)
    for place, which in order:
        for chan in range(CHAN):
            hit = lane == first + 64 * chan
            column = jnp.sum(jnp.where(hit, short[which], 0.0), axis=1, keepdims=True)
            columns = jnp.where(lane == place + chan, column, columns)
    taps[...] = jnp.zeros((128, 128), F32)
    taps[0:TAPS, :] = columns
    return taps[...].T[0:8, :]


def gradient_kernel(
    own,
    arrived_src,
    envelope_src,
    columns_src,
    cosine_src,
    short_src,
    back_src,
    back_turn_src,
    place_src,
    forward_src,
    last_src,
    twiddle_src,
    full_src,
    feat_out,
    spec_out,
    raw_out,
    basis_out,
    arrived,
    envelope,
    columns,
    cosine,
    short,
    back,
    back_turn,
    place,
    forward,
    last,
    twiddle,
    full,
    taps,
    raw,
    feat,
    spec,
    out_sems,
    sems,
):
    first = own[0]
    copies = begin(
        sems,
        [
            (short_src, short),
            (arrived_src, arrived),
            (forward_src, forward),
            (twiddle_src, twiddle),
            (full_src, full),
            (last_src, last),
            (envelope_src, envelope),
            (cosine_src, cosine),
            (columns_src, columns),
            (back_src, back),
            (back_turn_src, back_turn),
            (place_src, place),
        ],
    )
    copies[0].wait()
    weights = own_taps(first, short, taps, ((0, 0), (2, 1), (4, 2)))
    copies[1].wait()
    signal = arrived[...].astype(F32)
    lane = lax.broadcasted_iota(jnp.int32, (ROWS, 8, COLS), 2)
    result = weights[None, :, 0:1] * signal
    zeros = jnp.zeros((1, 8, COLS), F32)
    for offset in range(1, TAPS):
        moved = pltpu.roll(signal, offset, 2)
        before = jnp.concatenate([zeros, moved[:-1]], axis=0)
        shifted = jnp.where(lane < offset, before, moved)
        result = result + weights[None, :, offset : offset + 1] * shifted
    fill(feat, result)
    leaving = begin(out_sems.at[pl.ds(0, 1)], [(feat, feat_out)])

    def plane(index):
        return take(feat, index, ROWS, 8)

    signals = []
    for chan in range(CHAN):
        signals.append((plane(2 + chan) * plane(4 + chan)).astype(BF16))
    for chan in range(CHAN):
        signals.append((plane(chan) * plane(6 + chan)).astype(BF16))
    for copy in copies[2:5]:
        copy.wait()
    tables = (twiddle[0], twiddle[1], full[0], full[1])
    spec_all = spectrum(signals, forward[...], *tables)
    spec[...] = spec_all
    leaving += begin(out_sems.at[pl.ds(1, 1)], [(spec, spec_out)])
    carried, grad = spec_all[: CHAN * ROWS], spec_all[CHAN * ROWS :]
    carried_re, carried_im = carried[:, :COLS], carried[:, COLS:]
    grad_re, grad_im = grad[:, :COLS], grad[:, COLS:]
    crossed = jnp.concatenate(
        [
            carried_re * grad_re + carried_im * grad_im,
            carried_im * grad_re - carried_re * grad_im,
        ],
        axis=1,
    )
    for copy in copies[5:7]:
        copy.wait()
    filter_grad = restore(crossed, CHAN, last[...], *tables)
    for chan in range(CHAN):
        rounded = filter_grad[chan].astype(BF16).astype(F32)
        scaled = rounded * envelope[chan * ROWS : (chan + 1) * ROWS, :]
        for half in range(2):
            raw[half, chan * ROWS : (chan + 1) * ROWS, :] = scaled[:, half * 128 : half * 128 + 128]
    leaving += begin(out_sems.at[pl.ds(2, 1)], [(raw, raw_out)])
    for copy in copies[7:]:
        copy.wait()
    column0 = columns[0:FEAT, :]
    column1 = columns[FEAT : 2 * FEAT, :]
    back_all = back[...]

    def chunk(index, basis_sum):
        base = pl.multiple_of(index * 512, 512)
        start = pl.multiple_of(index * 8, 8)
        rows = [
            [raw[half, pl.ds(chan * ROWS + start, 8), :] for half in range(2)] for chan in range(CHAN)
        ]
        angles = back_turn[pl.ds(start, 8), :]
        parts = []
        for inner in range(8):
            near = inner * FEAT
            pieces = []
            for half in range(2):
                lanes = slice(half * 128, half * 128 + 128)
                value = (
                    column0 * rows[0][half][inner : inner + 1, :]
                    + column1 * rows[1][half][inner : inner + 1, :]
                )
                value = value * cosine[pl.ds(base + near, FEAT), lanes].astype(F32)
                pieces.append(value.astype(BF16))
            parts.append(jnp.concatenate(pieces, axis=1))
        product = dot(jnp.concatenate(parts, axis=0), back_all)
        for inner in range(8):
            near = inner * FEAT
            both = product[near : near + FEAT, 0:128] + product[near : near + FEAT, 128:256]
            basis_sum = basis_sum + both * angles[inner : inner + 1, :]
        return basis_sum

    basis_sum = lax.fori_loop(0, 8, chunk, jnp.zeros((FEAT, 128), F32), unroll=2)
    pieces = [
        lax.dot_general(
            place[group],
            basis_sum,
            (((1,), (1,)), ((), ())),
            precision=EXACT,
            preferred_element_type=F32,
        )
        for group in range(8)
    ]
    for quarter in range(4):
        row = jnp.concatenate(
            [piece[:, quarter * 16 : quarter * 16 + 16] for piece in pieces], axis=1
        )
        for peer in range(8):
            basis_out[quarter * 8 + peer] = row
    for copy in leaving:
        copy.wait()


HALO = TAPS - 1


def output_kernel(
    own,
    feat_src,
    spec_src,
    filter_spec_src,
    raw_src,
    act_src,
    skip_src,
    last_src,
    twiddle_src,
    full_src,
    out,
    feat,
    spec,
    filter_spec,
    raw,
    act,
    skip,
    last,
    twiddle,
    full,
    rows_out,
    sems,
):
    first = own[0]
    copies = begin(
        sems,
        [
            (raw_src, raw),
            (act_src, act),
            (spec_src, spec),
            (filter_spec_src, filter_spec),
            (full_src, full),
            (twiddle_src, twiddle),
            (last_src, last),
            (skip_src, skip),
            (feat_src, feat),
        ],
    )
    lane128 = lax.broadcasted_iota(jnp.int32, (FEAT, 128), 1)
    row_lane = lane128 % 8
    copies[0].wait()
    copies[1].wait()

    def chunk(index, proj_sum):
        base = pl.multiple_of(index * 512, 512)
        start = pl.multiple_of(index * 8, 8)
        rows = [
            jnp.concatenate(
                [raw[half, pl.ds(chan * ROWS + start, 8), :] for half in range(2)], axis=1
            )
            for chan in range(CHAN)
        ]
        wide = jnp.concatenate(rows, axis=0)
        hi = wide.astype(BF16).astype(F32)
        packed = jnp.concatenate([hi, wide - hi, jnp.zeros((128 - 4 * 8, COLS), F32)], axis=0)
        turned = jnp.concatenate(
            [packed[:, half * 128 : half * 128 + 128].T for half in range(2)], axis=0
        ).astype(BF16)
        product = dot(act[pl.ds(base, 512), :], turned)
        for inner in range(8):
            near = inner * FEAT
            proj_sum = proj_sum + jnp.where(row_lane == inner, product[near : near + FEAT, :], 0.0)
        return proj_sum

    proj_sum = lax.fori_loop(0, 8, chunk, jnp.zeros((FEAT, 128), F32), unroll=2)
    own_lane = lane128 % 16
    stacked = jnp.concatenate(
        [jnp.where(own_lane < 8, proj_sum, 0.0), jnp.where(own_lane >= 8, proj_sum, 0.0)], axis=0
    )
    proj_wide = lax.dot_general(
        jnp.ones((8, 128), F32),
        stacked,
        (((1,), (1,)), ((), ())),
        precision=EXACT,
        preferred_element_type=F32,
    )
    proj_hi = proj_wide.astype(BF16).astype(F32)
    for copy in copies[2:7]:
        copy.wait()
    tables = (twiddle[0], twiddle[1], full[0], full[1])
    carried, grad = spec[0 : CHAN * ROWS, :], spec[CHAN * ROWS : 2 * CHAN * ROWS, :]
    filt = filter_spec[...]
    carried_re, carried_im = carried[:, :COLS], carried[:, COLS:]
    grad_re, grad_im = grad[:, :COLS], grad[:, COLS:]
    filt_re, filt_im = filt[:, :COLS], filt[:, COLS:]
    crossed = jnp.concatenate(
        [
            jnp.concatenate(
                [
                    filt_re * carried_re - filt_im * carried_im,
                    -(filt_re * carried_im + filt_im * carried_re),
                ],
                axis=1,
            ),
            jnp.concatenate(
                [
                    filt_re * grad_re + filt_im * grad_im,
                    filt_im * grad_re - filt_re * grad_im,
                ],
                axis=1,
            ),
        ],
        axis=0,
    )
    sums = restore(crossed, 2 * CHAN, last[...], *tables)
    for copy in copies[7:]:
        copy.wait()

    def plane(index):
        return take(feat, index, ROWS, 8)

    blank = jnp.zeros((1, 128), F32)
    for chan in range(CHAN):
        gain = picked(skip[...], first + 64 * chan)
        query, key, value, cotangent = [plane(2 * index + chan) for index in range(4)]
        carried_own = (key * value).astype(BF16).astype(F32)
        grad_own = (query * cotangent).astype(BF16).astype(F32)
        long_out = (sums[chan] + gain * carried_own).astype(BF16).astype(F32)
        carried_grad = (sums[CHAN + chan] + gain * grad_own).astype(BF16).astype(F32)
        put(rows_out, chan, ROWS, 8, long_out)
        put(rows_out, 2 + chan, ROWS, 8, carried_grad)
        follow = jnp.zeros((ROWS, 128), F32)
        before = jnp.zeros((ROWS, 128), F32)
        heads = (
            cotangent[:, 0:128] * long_out[:, 0:128],
            carried_grad[:, 0:128] * value[:, 0:128],
            carried_grad[:, 0:128] * key[:, 0:128],
        )
        wanted = [head.astype(BF16).astype(F32) for head in heads]
        for signal in (query, key, value):
            wanted.append(signal[:, 0:128].astype(BF16).astype(F32))
        for signal in (query, key, value):
            wanted.append(signal[:, 0:128] - signal[:, 0:128].astype(BF16).astype(F32))
        for index, head in enumerate(wanted):
            place = HALO * index
            head = pltpu.roll(head, place, 1) if place else head
            inside = (lane128 >= place) & (lane128 < place + HALO)
            if index < 3:
                follow = jnp.where(inside, head, follow)
            else:
                before = jnp.where(inside, head, before)
        halo = jnp.concatenate([follow[1:], blank], axis=0) + before
        rows_out[chan, pl.ds(4, ROWS, stride=8), :] = halo
    row = lax.broadcasted_iota(jnp.int32, (ROWS, 8, 128), 1)
    for half, proj_part in enumerate((proj_hi, proj_wide - proj_hi)):
        extra = jnp.where(row == 7, proj_part[None], 0.0)
        value = jnp.where(row < 5, rows_out[half].reshape(ROWS, 8, 128), extra)
        out[:, :, half * 128 : half * 128 + 128] = value.astype(BF16)


def compose_kernel(packed, basis_parts, out):
    basis = basis_parts[0]
    for source in range(1, 32):
        basis = basis + basis_parts[source]
    row = lax.broadcasted_iota(jnp.int32, (8, 128), 0)
    lane = lax.broadcasted_iota(jnp.int32, (8, 128), 1)
    last = jnp.where((lane >= 64) & (lane < 80), pltpu.roll(basis, 64, 1)[4:5], 0.0)
    left = jnp.where(
        row == 4, last, jnp.where(row == 5, basis[0:1], jnp.where(row == 6, basis[2:3], 0.0))
    )
    right = jnp.where(row == 5, basis[1:2], jnp.where(row == 6, basis[3:4], 0.0))
    extra = jnp.concatenate([left, right], axis=1)
    out[...] = (packed[...].astype(F32) + extra[None]).astype(BF16)


def local_kernel(
    query_src, key_src, value_src, short_src, feat_out, taps_out, query, key, value, short, sems
):
    copies = begin(
        sems, [(query_src, query), (key_src, key), (value_src, value), (short_src, short)]
    )
    lane = lax.broadcasted_iota(jnp.int32, (128, 128), 1)
    for copy in copies:
        copy.wait()
    for index, ref in enumerate((query, key, value)):
        weights = jnp.concatenate([short[index], jnp.zeros((128 - TAPS, 128), F32)], axis=0).T
        for offset in range(TAPS):
            taps_out[index * TAPS + offset] = jnp.broadcast_to(
                weights[:, offset : offset + 1], (128, 128)
            )
        block = ref[...].astype(F32)
        left, right = block[:, 0:128], block[:, 128:256]
        out_left = taps_out[index * TAPS] * left
        out_right = taps_out[index * TAPS] * right
        for offset in range(1, TAPS):
            weight = taps_out[index * TAPS + offset]
            moved_left = pltpu.roll(left, offset, 1)
            moved_right = pltpu.roll(right, offset, 1)
            out_left = out_left + weight * jnp.where(lane < offset, 0.0, moved_left)
            out_right = out_right + weight * jnp.where(lane < offset, moved_left, moved_right)
        feat_out[index, :, 0:128] = out_left
        feat_out[index, :, 128:256] = out_right


def unpack_kernel(
    arrived,
    feat,
    taps,
    grad,
    mixed,
    grad_query,
    grad_key,
    grad_value,
    proj,
    basis,
    wide,
    sorted_rows,
):
    fill(wide, arrived[...].astype(F32))

    def both(half, row):
        return jnp.concatenate(
            [wide[half, pl.ds(row + chan, ROWS, stride=8), :] for chan in range(CHAN)], axis=0
        )

    long_out = [both(half, 0) for half in range(2)]
    carried_grad = [both(half, 2) for half in range(2)]
    halo = jnp.concatenate([wide[half, pl.ds(4, ROWS, stride=8), :] for half in range(2)], axis=0)
    lane = lax.broadcasted_iota(jnp.int32, (128, 128), 1)
    feats = []
    for index in range(3):
        high = pltpu.roll(halo, 128 - HALO * (3 + index), 1)
        low = pltpu.roll(halo, 128 - HALO * (6 + index), 1)
        left = jnp.where(lane < HALO, high + low, feat[index, :, 0:128])
        feats.append((left, feat[index, :, 128:256]))
    cotangent = grad[...].astype(F32)
    cotangent = (cotangent[:, 0:128], cotangent[:, 128:256])
    for half in range(2):
        mixed[:, half * 128 : half * 128 + 128] = (feats[0][half] * long_out[half]).astype(BF16)
    grads = (
        [cotangent[half] * long_out[half] for half in range(2)],
        [carried_grad[half] * feats[2][half] for half in range(2)],
        [carried_grad[half] * feats[1][half] for half in range(2)],
    )
    for index, ref in enumerate((grad_query, grad_key, grad_value)):
        left, right = [part.astype(BF16).astype(F32) for part in grads[index]]
        out_left = taps[index * TAPS] * left
        out_right = taps[index * TAPS] * right
        for offset in range(1, TAPS):
            weight = taps[index * TAPS + offset]
            moved_left = pltpu.roll(left, 128 - offset, 1)
            moved_right = pltpu.roll(right, 128 - offset, 1)
            moved_halo = pltpu.roll(halo, (128 - offset - HALO * index) % 128, 1)
            edge = lane >= 128 - offset
            out_left = out_left + weight * jnp.where(edge, moved_right, moved_left)
            out_right = out_right + weight * jnp.where(edge, moved_halo, moved_right)
        ref[:, 0:128] = out_left.astype(BF16)
        ref[:, 128:256] = out_right.astype(BF16)
    rows = wide[0, pl.ds(7, ROWS, stride=8), :] + wide[1, pl.ds(7, ROWS, stride=8), :]
    rows = rows * (1.0 / math.sqrt(TOTAL))
    rows = jnp.concatenate([rows, jnp.zeros_like(rows)], axis=0).T
    proj[:, 0:ROWS] = rows[0:FEAT, 0:ROWS]
    proj[:, ROWS : 2 * ROWS] = rows[FEAT : 2 * FEAT, 0:ROWS]
    totals = []
    for quarter in range(4):
        pair = []
        for half in range(2):
            total = wide[half, quarter * 8 : quarter * 8 + 8, :]
            for source in range(quarter + 4, ROWS, 4):
                total = total + wide[half, source * 8 : source * 8 + 8, :]
            pair.append(total)
        totals.append(pair)
    scale = math.sqrt(FEAT / (TOTAL * 1024))
    ordered = [
        jnp.concatenate([left[5:6], right[5:6], left[6:7], right[6:7]], axis=0)
        for left, right in totals
    ]
    for group in range(8):
        lanes = slice(group * 16, group * 16 + 16)
        merged = jnp.concatenate(
            [value[:, lanes] for value in ordered] + [jnp.zeros((4, 64), F32)], axis=1
        )
        sorted_rows[pl.ds(group, 4, stride=8), :] = merged * scale
    sorted_rows[32:33, :] = (
        jnp.concatenate([left[4:5, 64:80] for left, _ in totals] + [jnp.zeros((1, 64), F32)], axis=1)
        * scale
    )
    basis[...] = sorted_rows[0:EMB, 0:FEAT]


SMEM = pl.BlockSpec(memory_space=pltpu.SMEM)
VMEM = pl.BlockSpec(memory_space=pltpu.VMEM)
HBM = pl.BlockSpec(memory_space=pltpu.HBM)
LIMIT = 62 * 1024 * 1024
ROOMY = 32 * 1024 * 1024


def call(kernel, name, own, near, far, outs, scratch, flops, moved, limit=LIMIT):
    landing = [pltpu.VMEM(value.shape, value.dtype) for value in far]
    return pl.pallas_call(
        kernel,
        name=name,
        in_specs=[SMEM] * len(own) + [VMEM] * len(near) + [HBM] * len(far),
        out_specs=[HBM if direct else VMEM for _, direct in outs],
        out_shape=[value for value, _ in outs],
        scratch_shapes=(landing if kernel is not pack_kernel else [])
        + scratch
        + ([pltpu.SemaphoreType.DMA((len(far),))] if far else []),
        compiler_params=pltpu.CompilerParams(vmem_limit_bytes=limit),
        cost_estimate=pl.CostEstimate(flops=flops, bytes_accessed=moved, transcendentals=0),
    )(*own, *near, *far)


def shape(dims, kind=F32):
    return jax.ShapeDtypeStruct(dims, kind)


def run_pack(query_in, key_in, value_in, grad_out):
    return call(
        pack_kernel,
        "pack",
        [],
        [],
        [query_in, key_in, value_in, grad_out],
        [(shape((ROWS, 8, COLS), BF16), False)],
        [pltpu.VMEM((4, 128, COLS), BF16), pltpu.VMEM((2, 512, 128), F32)],
        1 << 20,
        1 << 19,
    )[0]


def run_filter(own, weight, bias, proj, decay, consts):
    names = ("pick", "turn", "right", "forward", "twiddle", "full")
    return call(
        filter_kernel,
        "filter",
        [own],
        [],
        [weight, bias, proj, decay] + [consts[name] for name in names],
        [
            (shape((ROWS * FEAT, COLS), BF16), True),
            (shape((ROWS * FEAT, COLS), BF16), True),
            (shape((CHAN * ROWS, COLS)), False),
            (shape((CHAN * ROWS, 2 * COLS)), False),
            (shape((CHAN * FEAT, 128)), False),
        ],
        [
            pltpu.VMEM((128, 128), F32),
            pltpu.VMEM((ROWS * FEAT, COLS), BF16),
            pltpu.VMEM((512, COLS), F32),
            pltpu.VMEM((512, COLS), F32),
            pltpu.VMEM((CHAN * ROWS, COLS), F32),
            pltpu.VMEM((ROWS * FEAT, COLS), BF16),
            pltpu.VMEM((ROWS * FEAT, COLS), BF16),
            pltpu.SemaphoreType.DMA((2, 8)),
        ],
        1 << 33,
        1 << 23,
    )


def run_gradient(own, arrived, short, cosine, envelope, columns, consts):
    names = ("back", "back_turn", "place", "forward", "last", "twiddle", "full")
    return call(
        gradient_kernel,
        "gradient",
        [own],
        [],
        [arrived, envelope, columns, cosine, short] + [consts[name] for name in names],
        [
            (shape((2, ROWS * 8, 128)), True),
            (shape((2 * CHAN * ROWS, 2 * COLS)), True),
            (shape((2, CHAN * ROWS, 128)), True),
            (shape((32, 8, 128)), False),
        ],
        [
            pltpu.VMEM((128, 128), F32),
            pltpu.VMEM((2, CHAN * ROWS, 128), F32),
            pltpu.VMEM((2, ROWS * 8, 128), F32),
            pltpu.VMEM((2 * CHAN * ROWS, 2 * COLS), F32),
            pltpu.SemaphoreType.DMA((3,)),
        ],
        1 << 32,
        1 << 23,
    )


def run_output(own, skip, feat, spec, filter_spec, raw, act, consts):
    names = ("last", "twiddle", "full")
    return call(
        output_kernel,
        "output",
        [own],
        [],
        [feat, spec, filter_spec, raw, act, skip] + [consts[name] for name in names],
        [(shape((ROWS, 8, COLS), BF16), False)],
        [pltpu.VMEM((2, ROWS * 8, 128), F32)],
        1 << 31,
        1 << 22,
    )[0]


def run_compose(packed, basis_parts):
    return call(
        compose_kernel,
        "compose",
        [],
        [packed, basis_parts],
        [],
        [(shape((ROWS, 8, COLS), BF16), False)],
        [],
        1 << 20,
        1 << 20,
        ROOMY,
    )[0]


def run_local(query_in, key_in, value_in, short):
    return call(
        local_kernel,
        "local",
        [],
        [],
        [query_in, key_in, value_in, short],
        [(shape((3, 128, COLS)), False), (shape((3 * TAPS, 128, 128)), False)],
        [],
        1 << 28,
        1 << 20,
        ROOMY,
    )


def run_unpack(arrived, feat, taps, grad_out):
    block = shape((128, COLS), BF16)
    return call(
        unpack_kernel,
        "unpack",
        [],
        [arrived, feat, taps, grad_out],
        [],
        [(value, False) for value in [block] * 4 + [shape((FEAT, 128)), shape((EMB, FEAT))]],
        [pltpu.VMEM((2, ROWS * 8, 128), F32), pltpu.VMEM((64, 128), F32)],
        1 << 20,
        1 << 20,
        ROOMY,
    )


def make_consts():
    forward, last, twiddle, full = transform_tables()
    right, turn, pick, back, back_turn, place = basis_tables()
    return dict(
        forward=jnp.asarray(forward),
        last=jnp.asarray(last),
        twiddle=jnp.asarray(twiddle),
        full=jnp.asarray(full),
        right=jnp.asarray(right),
        turn=jnp.asarray(turn),
        pick=jnp.asarray(pick),
        back=jnp.asarray(back),
        back_turn=jnp.asarray(back_turn),
        place=jnp.asarray(place),
    )


CTX = ("zh", "yh", "yl", "core")
NEAR = ("yl", "core", "x", "zl")


def exchange(value, axes):
    return lax.all_to_all(value, axes, split_axis=0, concat_axis=0, tiled=True)


def on_device(
    query_in,
    key_in,
    value_in,
    short_kernel,
    basis_weight,
    basis_bias,
    filter_proj,
    decay_rate,
    skip_gain,
    grad_out,
):
    consts = make_consts()
    own = lax.axis_index(CTX).astype(jnp.int32).reshape(1)
    with jax.named_scope("spread"):
        arrived = exchange(run_pack(query_in, key_in, value_in, grad_out), CTX)
    short = short_kernel.transpose(0, 2, 1)
    block_feat, block_taps = run_local(query_in, key_in, value_in, short)
    act, cosine, envelope, filter_spec, columns = run_filter(
        own,
        basis_weight.T,
        basis_bias.reshape(1, FEAT),
        filter_proj.T,
        decay_rate.reshape(1, 128),
        consts,
    )
    feat, spec, raw, basis_own = run_gradient(
        own, arrived, short, cosine, envelope, columns, consts
    )
    with jax.named_scope("basis"):
        basis_parts = exchange(basis_own, NEAR)
    packed = run_output(
        own, skip_gain.reshape(1, 128), feat, spec, filter_spec, raw, act, consts
    )
    composed = run_compose(packed, basis_parts)
    with jax.named_scope("collect"):
        returned = exchange(composed, CTX)
    mixed, grad_query, grad_key, grad_value, grad_proj, grad_basis = run_unpack(
        returned, block_feat, block_taps, grad_out
    )
    return (mixed, grad_query, grad_key, grad_value, grad_proj.T, grad_basis.T)


def solution(mesh):
    finer = Mesh(mesh.devices.reshape(4, 4, 2, 2, 4, 2), CTX + ("x", "zl"))
    rows = ("x", "zl")
    block = P(rows, CTX)
    return jax.shard_map(
        on_device,
        mesh=finer,
        in_specs=(
            block,
            block,
            block,
            P(None, rows, None),
            P(),
            P(),
            P(rows, None),
            P(rows),
            P(rows),
            block,
        ),
        out_specs=(block, block, block, block, P(rows, None), P()),
        check_vma=False,
    )
```

```python
import math

import jax
import jax.numpy as jnp
import numpy as np
from jax import lax
from jax.experimental import pallas as pl
from jax.experimental.pallas import tpu as pltpu
from jax.sharding import Mesh
from jax.sharding import PartitionSpec as P
import ml_dtypes

F32 = jnp.float32
BF16 = jnp.bfloat16
EXACT = lax.Precision.HIGHEST

ROWS = 64
COLS = 256
TOTAL = ROWS * COLS
FEAT = 64
EMB = 33
TAPS = 7
CHAN = 2
GROUP = 40
TURN = 1.0 / (2.0 * math.pi)

SIN_COEF = (4.442879676818848, -7.307816505432129, 3.5977742671966553, -0.7911993861198425)
COS_COEF = (
    1.4142135381698608,
    -6.978850841522217,
    5.739460468292236,
    -1.883557915687561,
    0.3106880187988281,
)


def halves(table, count):
    parts = []
    rest = np.asarray(table, np.float64)
    for _ in range(count):
        part = rest.astype(np.float32).astype(ml_dtypes.bfloat16)
        parts.append(part)
        rest = rest - part.astype(np.float64)
    return parts


def transform_tables():
    rows = np.arange(ROWS)
    cols = np.arange(COLS)
    first = 2.0 * np.pi * ((4 * rows[:, None] + 1) * rows[None, :] % (4 * ROWS)) / (4 * ROWS)
    first_re, first_im = np.cos(first), -np.sin(first)
    forward = np.concatenate([first_re, first_im], axis=0)
    forward_cat = np.concatenate(halves(forward, 2), axis=1)
    last = np.concatenate([first_re.T, -first_im.T], axis=1) / TOTAL
    last_hi, last_lo = halves(last, 2)
    last_cat = np.concatenate([last_hi, last_lo, last_hi], axis=1)
    turn = 2.0 * np.pi * ((4 * rows[:, None] + 1) * cols[None, :]) / (4 * TOTAL)
    twiddle = np.stack([np.cos(turn), -np.sin(turn)]).astype(np.float32)
    inner = 2.0 * np.pi * (cols[:, None] * cols[None, :] % COLS) / COLS
    inner_re, inner_im = np.cos(inner), -np.sin(inner)
    full = np.concatenate(
        [
            np.concatenate([inner_re, inner_im], axis=1),
            np.concatenate([-inner_im, inner_re], axis=1),
        ],
        axis=0,
    )
    full_hi, full_lo = halves(full, 2)
    return forward_cat, last_cat, twiddle, np.stack([full_hi, full_lo])


def basis_tables():
    freq = np.arange(1, 17)
    cols = np.arange(COLS)
    rows = np.arange(ROWS)
    inner = 2.0 * np.pi * (freq[:, None] * cols[None, :] % TOTAL) / TOTAL
    short = np.concatenate(
        [np.cos(inner), np.sin(inner), cols[None, :] / TOTAL, np.ones((1, COLS))], axis=0
    )
    width = short.shape[0]
    hi, mid, lo = halves(short, 3)
    right = np.zeros((256, COLS), ml_dtypes.bfloat16)
    for place, part in ((0, hi), (GROUP, hi), (2 * GROUP, hi)):
        right[place : place + width] = part
    for place, part in ((128, mid), (128 + GROUP, lo), (128 + 2 * GROUP, mid)):
        right[place : place + width] = part
    outer = 2.0 * np.pi * (freq[None, :] * rows[:, None] % ROWS) / ROWS
    cos_out, sin_out = np.cos(outer), np.sin(outer)
    one = np.ones((ROWS, 1))
    block = rows[:, None] / ROWS
    cos_row = np.concatenate([cos_out, cos_out, one, one], axis=1)
    sin_row = np.concatenate([sin_out, sin_out, 0 * one, block], axis=1)
    turn = np.zeros((2, ROWS, 128), np.float32)
    for place in (0, GROUP, 2 * GROUP):
        turn[0, :, place : place + width] = cos_row
        turn[1, :, place : place + width] = sin_row
    pick = np.zeros((2, 128, 128), np.float32)
    for place in (0, GROUP, 2 * GROUP):
        for index in range(16):
            pick[0, 2 * index + 1, place + index] = 1.0
            pick[0, 2 * index + 2, place + 16 + index] = 1.0
            pick[1, 2 * index + 2, place + index] = 1.0
            pick[1, 2 * index + 1, place + 16 + index] = -1.0
        pick[0, 0, place + 32] = 1.0
        pick[0, EMB, place + 33] = 1.0
        pick[1, 0, place + 33] = 1.0
    back = np.zeros((COLS, 128))
    back[:, :width] = short.T
    back[:, 64:80] = short[16:32].T
    back[:, 80:96] = short[:16].T
    back_hi, back_lo = halves(back, 2)
    back_cat = np.concatenate([back_hi, back_lo], axis=1)
    back_turn = np.zeros((ROWS, 128), np.float32)
    back_turn[:, :32] = cos_row[:, :32]
    back_turn[:, 32] = 1.0
    back_turn[:, 33] = rows / ROWS
    back_turn[:, 64:80] = -sin_out
    back_turn[:, 80:96] = sin_out
    place = np.zeros((8, 8, 128), np.float32)
    for wanted in range(EMB):
        row, group = divmod(wanted, 8)
        if wanted == 0:
            lanes = (32, 33)
        elif wanted % 2:
            lanes = ((wanted - 1) // 2, 64 + (wanted - 1) // 2)
        else:
            lanes = (16 + (wanted - 2) // 2, 80 + (wanted - 2) // 2)
        for lane in lanes:
            place[group, row, lane] = 1.0
    return right, turn, pick, back_cat, back_turn, place


def split(value):
    hi = value.astype(BF16)
    lo = (value - hi.astype(F32)).astype(BF16)
    return hi, lo


def dot(left, right):
    return jnp.dot(left, right, preferred_element_type=F32)


def spectrum(signals, forward, twiddle_re, twiddle_im, full_hi, full_lo):
    wide = jnp.concatenate(signals, axis=1)
    section = dot(forward, jnp.concatenate([wide, wide], axis=0))
    turned = []
    for index in range(len(signals)):
        part = section[:, index * COLS : (index + 1) * COLS]
        part_re, part_im = part[:ROWS], part[ROWS:]
        turned.append(
            jnp.concatenate(
                [
                    part_re * twiddle_re - part_im * twiddle_im,
                    part_re * twiddle_im + part_im * twiddle_re,
                ],
                axis=1,
            )
        )
    return full_product(jnp.concatenate(turned, axis=0), full_hi, full_lo)


def full_product(value, full_hi, full_lo):
    hi, lo = split(value)
    return dot(hi, full_hi) + dot(lo, full_hi) + dot(hi, full_lo)


def restore(conj_spec, count, last, twiddle_re, twiddle_im, full_hi, full_lo):
    back = full_product(conj_spec, full_hi, full_lo)
    stacked = []
    for index in range(count):
        part = back[index * ROWS : (index + 1) * ROWS]
        part_re, part_im = part[:, :COLS], part[:, COLS:]
        stacked.append(
            jnp.concatenate(
                [
                    part_re * twiddle_re - part_im * twiddle_im,
                    part_re * twiddle_im + part_im * twiddle_re,
                ],
                axis=0,
            )
        )
    hi, lo = split(jnp.concatenate(stacked, axis=1))
    result = dot(last, jnp.concatenate([hi, hi, lo], axis=0))
    return [result[:, index * COLS : (index + 1) * COLS] for index in range(count)]


def take(ref, start, count, stride):
    return jnp.concatenate(
        [ref[half, pl.ds(start, count, stride=stride), :] for half in range(2)], axis=1
    )


def put(ref, start, count, stride, value):
    for half in range(2):
        ref[half, pl.ds(start, count, stride=stride), :] = value[:, half * 128 : half * 128 + 128]


AT_FEAT = 0
AT_SPEC = 2 * ROWS * 8
AT_RAW = AT_SPEC + 4 * 2 * CHAN * ROWS
AT_FILTER = AT_RAW + 2 * CHAN * ROWS
HANDED = AT_FILTER + 4 * CHAN * ROWS


def tiles(ref, start, stride, count, picked_tiles):
    return jnp.concatenate(
        [ref[start + tile * stride : start + tile * stride + count, :] for tile in picked_tiles], axis=1
    )


def fill(ref, value):
    for half in range(2):
        ref[half] = value[..., half * 128 : half * 128 + 128].reshape(ref.shape[1], 128)


def begin(sems, pairs):
    copies = [
        pltpu.make_async_copy(source, target, sems.at[index])
        for index, (source, target) in enumerate(pairs)
    ]
    for copy in copies:
        copy.start()
    return copies


def picked(row, wanted):
    lane = lax.broadcasted_iota(jnp.int32, row.shape, 1)
    return jnp.sum(jnp.where(lane == wanted, row, 0.0), axis=1, keepdims=True)


def pack_kernel(query, key, value, grad, out, held, wide, sems):
    copies = begin(sems, [(ref, held.at[index]) for index, ref in enumerate((query, key, value, grad))])
    for index in range(4):
        copies[index].wait()
        block = held[index].astype(F32)
        for half in range(2):
            wide[half, index * 128 : (index + 1) * 128, :] = block[:, half * 128 : half * 128 + 128]
    for peer in range(ROWS):
        out[peer] = take(wide, peer, 8, ROWS).astype(BF16)


def expm1_small(value):
    series = jnp.ones_like(value)
    for order in range(9, 1, -1):
        series = 1.0 + value * series * (1.0 / order)
    return jnp.where(value > -0.5, value * series, jnp.exp(value) - 1.0)


def filter_kernel(
    own,
    weight_src,
    bias_src,
    proj_src,
    decay_src,
    pick_src,
    turn_src,
    right_src,
    forward_src,
    twiddle_src,
    full_src,
    act_out,
    cos_out,
    env_out,
    spec_out,
    column_out,
    weight,
    bias,
    proj,
    decay,
    pick,
    turn,
    right,
    forward,
    twiddle,
    full,
    layer,
    left,
    phase,
    phase_odd,
    filt,
    act,
    cosv,
    out_sems,
    sems,
):
    first = own[0]
    copies = begin(
        sems,
        [
            (weight_src, weight),
            (bias_src, bias),
            (pick_src, pick),
            (proj_src, proj),
            (turn_src, turn),
            (right_src, right),
            (decay_src, decay),
            (forward_src, forward),
            (twiddle_src, twiddle),
            (full_src, full),
        ],
    )
    layer[...] = jnp.zeros((128, 128), F32)
    for copy in copies[:3]:
        copy.wait()
    layer[0:EMB, 0:FEAT] = weight[...]
    layer[EMB : EMB + 1, 0:FEAT] = bias[...]
    layer_all = layer[...].T[0:FEAT, :]
    same = jnp.dot(layer_all, pick[0], precision=EXACT, preferred_element_type=F32) * TURN
    cross = jnp.dot(layer_all, pick[1], precision=EXACT, preferred_element_type=F32) * TURN
    lane = lax.broadcasted_iota(jnp.int32, (FEAT, 128), 1)
    sublane = lax.broadcasted_iota(jnp.int32, (8, 128), 0)
    for copy in copies[3:7]:
        copy.wait()
    columns = []
    for chan in range(CHAN):
        hit = lane == first + 64 * chan
        column = jnp.sum(jnp.where(hit, proj[...], 0.0), axis=1, keepdims=True)
        column_wide = jnp.broadcast_to(column, (FEAT, 128))
        column_out[chan * FEAT : (chan + 1) * FEAT, :] = column_wide
        columns.append(column_wide)

    def make_left(block, carry):
        value = same * turn[0, pl.ds(block, 1), :] + cross * turn[1, pl.ds(block, 1), :]
        hi = value.astype(BF16).astype(F32)
        rest = value - hi
        mid = rest.astype(BF16).astype(F32)
        lo = rest - mid
        one = jnp.where(lane < GROUP, hi, jnp.where(lane < 2 * GROUP, mid, lo))
        two = jnp.where(lane < 2 * GROUP, hi, mid)
        start = pl.multiple_of(block * FEAT, FEAT)
        left[pl.ds(start, FEAT), 0:128] = one.astype(BF16)
        left[pl.ds(start, FEAT), 128:256] = two.astype(BF16)
        return carry

    lax.fori_loop(0, ROWS, make_left, 0, unroll=4)

    def fetch(index, phase):
        base = pl.multiple_of(index * 512, 512)
        phase[...] = dot(left[pl.ds(base, 512), :], right[...])

    def finish(index, phase):
        base = pl.multiple_of(index * 512, 512)
        for half in range(2):
            lanes = slice(half * 128, half * 128 + 128)
            sums = [jnp.zeros((8, 128), F32)] * CHAN
            for inner in range(8):
                near = inner * FEAT
                turns = phase[near : near + FEAT, lanes]
                rest = turns - jnp.round(turns)
                square = rest * rest
                sine = SIN_COEF[-1] * square + SIN_COEF[-2]
                cosine = COS_COEF[-1] * square + COS_COEF[-2]
                for coef in SIN_COEF[-3::-1]:
                    sine = sine * square + coef
                for coef in COS_COEF[-3::-1]:
                    cosine = cosine * square + coef
                sine = sine * rest
                whole_sine = sine * cosine
                whole_cosine = 1.0 - sine * sine
                act[pl.ds(base + near, FEAT), lanes] = whole_sine.astype(BF16)
                cosv[pl.ds(base + near, FEAT), lanes] = whole_cosine.astype(BF16)
                for chan in range(CHAN):
                    total = jnp.sum(whole_sine * columns[chan], axis=0, keepdims=True)
                    sums[chan] = jnp.where(sublane == inner, total, sums[chan])
            for chan in range(CHAN):
                start = pl.multiple_of(chan * ROWS + index * 8, 8)
                filt[pl.ds(start, 8), lanes] = sums[chan]
        send(index, 0).start()
        send(index, 1).start()

    def pair(index, carry):
        fetch(2 * index + 1, phase_odd)
        finish(2 * index, phase)
        fetch(jnp.minimum(2 * index + 2, 7), phase)
        finish(2 * index + 1, phase_odd)
        return carry

    def send(index, which):
        rows = pl.ds(pl.multiple_of(index * 512, 512), 512)
        source, target = ((act, act_out), (cosv, cos_out))[which]
        return pltpu.make_async_copy(source.at[rows], target.at[rows], out_sems.at[which, index])

    fetch(0, phase)
    lax.fori_loop(0, 4, pair, 0)
    ratio = decay[...] * (1.0 / TOTAL)
    energy = expm1_small(-2.0 * decay[...]) / expm1_small(-2.0 * ratio)
    norm = 1.0 / jnp.sqrt(energy)
    for copy in copies[7:]:
        copy.wait()
    position = (
        lax.broadcasted_iota(jnp.int32, (ROWS, COLS), 0) * COLS
        + lax.broadcasted_iota(jnp.int32, (ROWS, COLS), 1)
    ).astype(F32)
    signals = []
    for chan in range(CHAN):
        rate = picked(decay[...], first + 64 * chan)
        envelope = jnp.exp(-(rate * position) * (1.0 / TOTAL)) * picked(norm, first + 64 * chan)
        env_out[chan * ROWS : (chan + 1) * ROWS, :] = envelope
        signals.append((filt[chan * ROWS : (chan + 1) * ROWS, :] * envelope).astype(BF16))
    spec_out[...] = spectrum(signals, forward[...], twiddle[0], twiddle[1], full[0], full[1])
    for index in range(8):
        send(index, 0).wait()
        send(index, 1).wait()


def own_taps(first, short, taps, order):
    row = lax.broadcasted_iota(jnp.int32, (TAPS, 128), 0)
    lane = lax.broadcasted_iota(jnp.int32, (TAPS, 128), 1)
    columns = jnp.where(row == 0, 1.0, 0.0)
    for place, which in order:
        for chan in range(CHAN):
            hit = lane == first + 64 * chan
            column = jnp.sum(jnp.where(hit, short[which], 0.0), axis=1, keepdims=True)
            columns = jnp.where(lane == place + chan, column, columns)
    taps[...] = jnp.zeros((128, 128), F32)
    taps[0:TAPS, :] = columns
    return taps[...].T[0:8, :]


def gradient_kernel(
    own,
    arrived_src,
    envelope_src,
    columns_src,
    cosine_src,
    filter_spec_src,
    short_src,
    back_src,
    back_turn_src,
    place_src,
    forward_src,
    last_src,
    twiddle_src,
    full_src,
    handed_out,
    basis_out,
    arrived,
    envelope,
    columns,
    cosine,
    filter_spec,
    short,
    back,
    back_turn,
    place,
    forward,
    last,
    twiddle,
    full,
    taps,
    raw,
    handed,
    out_sems,
    sems,
):
    first = own[0]
    copies = begin(
        sems,
        [
            (short_src, short),
            (arrived_src, arrived),
            (forward_src, forward),
            (twiddle_src, twiddle),
            (full_src, full),
            (last_src, last),
            (envelope_src, envelope),
            (cosine_src, cosine),
            (columns_src, columns),
            (filter_spec_src, filter_spec),
            (back_src, back),
            (back_turn_src, back_turn),
            (place_src, place),
        ],
    )
    copies[0].wait()
    weights = own_taps(first, short, taps, ((0, 0), (2, 1), (4, 2)))
    copies[1].wait()
    signal = arrived[...].astype(F32)
    lane = lax.broadcasted_iota(jnp.int32, (ROWS, 8, 128), 2)
    zeros = jnp.zeros((1, 8, 128), F32)
    left, right = signal[:, :, 0:128], signal[:, :, 128:256]
    sum_left = weights[None, :, 0:1] * left
    sum_right = weights[None, :, 0:1] * right
    for offset in range(1, TAPS):
        weight = weights[None, :, offset : offset + 1]
        moved_left = pltpu.roll(left, offset, 2)
        moved_right = pltpu.roll(right, offset, 2)
        before = jnp.concatenate([zeros, moved_right[:-1]], axis=0)
        sum_left = sum_left + weight * jnp.where(lane < offset, before, moved_left)
        sum_right = sum_right + weight * jnp.where(lane < offset, moved_left, moved_right)
    for half, result in enumerate((sum_left, sum_right)):
        handed[AT_FEAT + half * 512 : AT_FEAT + half * 512 + 512, :] = result.reshape(512, 128)

    def leave(part, start, size):
        rows = pl.ds(start, size)
        return begin(out_sems.at[pl.ds(part, 1)], [(handed.at[rows], handed_out.at[rows])])

    leaving = leave(0, AT_FEAT, AT_SPEC - AT_FEAT)

    def plane(index):
        return jnp.concatenate(
            [handed[pl.ds(AT_FEAT + half * 512 + index, ROWS, stride=8), :] for half in range(2)],
            axis=1,
        )

    signals = []
    for chan in range(CHAN):
        signals.append((plane(2 + chan) * plane(4 + chan)).astype(BF16))
    for chan in range(CHAN):
        signals.append((plane(chan) * plane(6 + chan)).astype(BF16))
    for copy in copies[2:5]:
        copy.wait()
    tables = (twiddle[0], twiddle[1], full[0], full[1])
    spec_all = spectrum(signals, forward[...], *tables)
    for tile in range(4):
        handed[AT_SPEC + tile * 256 : AT_SPEC + tile * 256 + 256, :] = spec_all[
            :, tile * 128 : tile * 128 + 128
        ]
    leaving += leave(1, AT_SPEC, AT_RAW - AT_SPEC)
    carried, grad = spec_all[: CHAN * ROWS], spec_all[CHAN * ROWS :]
    carried_re, carried_im = carried[:, :COLS], carried[:, COLS:]
    grad_re, grad_im = grad[:, :COLS], grad[:, COLS:]
    crossed = jnp.concatenate(
        [
            carried_re * grad_re + carried_im * grad_im,
            carried_im * grad_re - carried_re * grad_im,
        ],
        axis=1,
    )
    for copy in copies[5:7]:
        copy.wait()
    filter_grad = restore(crossed, CHAN, last[...], *tables)
    for chan in range(CHAN):
        rounded = filter_grad[chan].astype(BF16).astype(F32)
        scaled = rounded * envelope[chan * ROWS : (chan + 1) * ROWS, :]
        for half in range(2):
            raw[half, chan * ROWS : (chan + 1) * ROWS, :] = scaled[:, half * 128 : half * 128 + 128]
    for copy in copies[7:]:
        copy.wait()
    for half in range(2):
        handed[AT_RAW + half * 128 : AT_RAW + half * 128 + 128, :] = raw[half]
    for tile in range(4):
        handed[AT_FILTER + tile * 128 : AT_FILTER + tile * 128 + 128, :] = filter_spec[
            :, tile * 128 : tile * 128 + 128
        ]
    leaving += leave(2, AT_RAW, HANDED - AT_RAW)
    column0 = columns[0:FEAT, :]
    column1 = columns[FEAT : 2 * FEAT, :]
    back_all = back[...]

    def chunk(index, basis_sum):
        base = pl.multiple_of(index * 512, 512)
        start = pl.multiple_of(index * 8, 8)
        rows = [
            [raw[half, pl.ds(chan * ROWS + start, 8), :] for half in range(2)] for chan in range(CHAN)
        ]
        angles = back_turn[pl.ds(start, 8), :]
        parts = []
        for inner in range(8):
            near = inner * FEAT
            pieces = []
            for half in range(2):
                lanes = slice(half * 128, half * 128 + 128)
                value = (
                    column0 * rows[0][half][inner : inner + 1, :]
                    + column1 * rows[1][half][inner : inner + 1, :]
                )
                value = value * cosine[pl.ds(base + near, FEAT), lanes].astype(F32)
                pieces.append(value.astype(BF16))
            parts.append(jnp.concatenate(pieces, axis=1))
        product = dot(jnp.concatenate(parts, axis=0), back_all)
        for inner in range(8):
            near = inner * FEAT
            both = product[near : near + FEAT, 0:128] + product[near : near + FEAT, 128:256]
            basis_sum = basis_sum + both * angles[inner : inner + 1, :]
        return basis_sum

    basis_sum = lax.fori_loop(0, 8, chunk, jnp.zeros((FEAT, 128), F32), unroll=2)
    pieces = [
        lax.dot_general(
            place[group],
            basis_sum,
            (((1,), (1,)), ((), ())),
            precision=EXACT,
            preferred_element_type=F32,
        )
        for group in range(8)
    ]
    for quarter in range(4):
        row = jnp.concatenate(
            [piece[:, quarter * 16 : quarter * 16 + 16] for piece in pieces], axis=1
        )
        for peer in range(8):
            basis_out[quarter * 8 + peer] = row
    for copy in leaving:
        copy.wait()


HALO = TAPS - 1


def output_kernel(
    own,
    handed_src,
    act_src,
    skip_src,
    last_src,
    twiddle_src,
    full_src,
    out,
    handed,
    act,
    skip,
    last,
    twiddle,
    full,
    rows_out,
    sems,
):
    first = own[0]
    copies = begin(
        sems,
        [
            (handed_src, handed),
            (full_src, full),
            (twiddle_src, twiddle),
            (last_src, last),
            (skip_src, skip),
            (act_src, act),
        ],
    )
    lane128 = lax.broadcasted_iota(jnp.int32, (FEAT, 128), 1)
    row_lane = lane128 % 8
    for copy in copies[0:4]:
        copy.wait()
    tables = (twiddle[0], twiddle[1], full[0], full[1])
    own_rows = CHAN * ROWS
    carried_re = tiles(handed, AT_SPEC, 256, own_rows, (0, 1))
    carried_im = tiles(handed, AT_SPEC, 256, own_rows, (2, 3))
    grad_re = tiles(handed, AT_SPEC + own_rows, 256, own_rows, (0, 1))
    grad_im = tiles(handed, AT_SPEC + own_rows, 256, own_rows, (2, 3))
    filt_re = tiles(handed, AT_FILTER, 128, own_rows, (0, 1))
    filt_im = tiles(handed, AT_FILTER, 128, own_rows, (2, 3))
    crossed = jnp.concatenate(
        [
            jnp.concatenate(
                [
                    filt_re * carried_re - filt_im * carried_im,
                    -(filt_re * carried_im + filt_im * carried_re),
                ],
                axis=1,
            ),
            jnp.concatenate(
                [
                    filt_re * grad_re + filt_im * grad_im,
                    filt_im * grad_re - filt_re * grad_im,
                ],
                axis=1,
            ),
        ],
        axis=0,
    )
    sums = restore(crossed, 2 * CHAN, last[...], *tables)
    copies[4].wait()

    def plane(index):
        return jnp.concatenate(
            [handed[pl.ds(AT_FEAT + half * 512 + index, ROWS, stride=8), :] for half in range(2)],
            axis=1,
        )

    blank = jnp.zeros((1, 128), F32)
    for chan in range(CHAN):
        gain = picked(skip[...], first + 64 * chan)
        query, key, value, cotangent = [plane(2 * index + chan) for index in range(4)]
        carried_own = (key * value).astype(BF16).astype(F32)
        grad_own = (query * cotangent).astype(BF16).astype(F32)
        long_out = (sums[chan] + gain * carried_own).astype(BF16).astype(F32)
        carried_grad = (sums[CHAN + chan] + gain * grad_own).astype(BF16).astype(F32)
        put(rows_out, chan, ROWS, 8, long_out)
        put(rows_out, 2 + chan, ROWS, 8, carried_grad)
        follow = jnp.zeros((ROWS, 128), F32)
        before = jnp.zeros((ROWS, 128), F32)
        heads = (
            cotangent[:, 0:128] * long_out[:, 0:128],
            carried_grad[:, 0:128] * value[:, 0:128],
            carried_grad[:, 0:128] * key[:, 0:128],
        )
        wanted = [head.astype(BF16).astype(F32) for head in heads]
        for signal in (query, key, value):
            wanted.append(signal[:, 0:128].astype(BF16).astype(F32))
        for signal in (query, key, value):
            wanted.append(signal[:, 0:128] - signal[:, 0:128].astype(BF16).astype(F32))
        for index, head in enumerate(wanted):
            place = HALO * index
            head = pltpu.roll(head, place, 1) if place else head
            inside = (lane128 >= place) & (lane128 < place + HALO)
            if index < 3:
                follow = jnp.where(inside, head, follow)
            else:
                before = jnp.where(inside, head, before)
        halo = jnp.concatenate([follow[1:], blank], axis=0) + before
        rows_out[chan, pl.ds(4, ROWS, stride=8), :] = halo
    copies[5].wait()

    def chunk(index, proj_sum):
        base = pl.multiple_of(index * 512, 512)
        start = pl.multiple_of(index * 8, 8)
        rows = [
            jnp.concatenate(
                [
                    handed[pl.ds(AT_RAW + half * 128 + chan * ROWS + start, 8), :]
                    for half in range(2)
                ],
                axis=1,
            )
            for chan in range(CHAN)
        ]
        wide = jnp.concatenate(rows, axis=0)
        hi = wide.astype(BF16).astype(F32)
        packed = jnp.concatenate([hi, wide - hi, jnp.zeros((128 - 4 * 8, COLS), F32)], axis=0)
        turned = jnp.concatenate(
            [packed[:, half * 128 : half * 128 + 128].T for half in range(2)], axis=0
        ).astype(BF16)
        product = dot(act[pl.ds(base, 512), :], turned)
        for inner in range(8):
            near = inner * FEAT
            proj_sum = proj_sum + jnp.where(row_lane == inner, product[near : near + FEAT, :], 0.0)
        return proj_sum

    proj_sum = lax.fori_loop(0, 8, chunk, jnp.zeros((FEAT, 128), F32), unroll=2)
    own_lane = lane128 % 16
    stacked = jnp.concatenate(
        [jnp.where(own_lane < 8, proj_sum, 0.0), jnp.where(own_lane >= 8, proj_sum, 0.0)], axis=0
    )
    proj_wide = lax.dot_general(
        jnp.ones((8, 128), F32),
        stacked,
        (((1,), (1,)), ((), ())),
        precision=EXACT,
        preferred_element_type=F32,
    )
    proj_hi = proj_wide.astype(BF16).astype(F32)
    row = lax.broadcasted_iota(jnp.int32, (ROWS, 8, 128), 1)
    for half, proj_part in enumerate((proj_hi, proj_wide - proj_hi)):
        extra = jnp.where(row == 7, proj_part[None], 0.0)
        value = jnp.where(row < 5, rows_out[half].reshape(ROWS, 8, 128), extra)
        out[:, :, half * 128 : half * 128 + 128] = value.astype(BF16)


def compose_kernel(packed, basis_parts, out):
    basis = basis_parts[0]
    for source in range(1, 32):
        basis = basis + basis_parts[source]
    row = lax.broadcasted_iota(jnp.int32, (8, 128), 0)
    lane = lax.broadcasted_iota(jnp.int32, (8, 128), 1)
    last = jnp.where((lane >= 64) & (lane < 80), pltpu.roll(basis, 64, 1)[4:5], 0.0)
    left = jnp.where(
        row == 4, last, jnp.where(row == 5, basis[0:1], jnp.where(row == 6, basis[2:3], 0.0))
    )
    right = jnp.where(row == 5, basis[1:2], jnp.where(row == 6, basis[3:4], 0.0))
    extra = jnp.concatenate([left, right], axis=1)
    out[...] = (packed[...].astype(F32) + extra[None]).astype(BF16)


def local_kernel(
    query_src, key_src, value_src, short_src, feat_out, taps_out, query, key, value, short, sems
):
    copies = begin(
        sems, [(query_src, query), (key_src, key), (value_src, value), (short_src, short)]
    )
    lane = lax.broadcasted_iota(jnp.int32, (128, 128), 1)
    for copy in copies:
        copy.wait()
    for index, ref in enumerate((query, key, value)):
        weights = jnp.concatenate([short[index], jnp.zeros((128 - TAPS, 128), F32)], axis=0).T
        for offset in range(TAPS):
            taps_out[index * TAPS + offset] = jnp.broadcast_to(
                weights[:, offset : offset + 1], (128, 128)
            )
        block = ref[...].astype(F32)
        left, right = block[:, 0:128], block[:, 128:256]
        out_left = taps_out[index * TAPS] * left
        out_right = taps_out[index * TAPS] * right
        for offset in range(1, TAPS):
            weight = taps_out[index * TAPS + offset]
            moved_left = pltpu.roll(left, offset, 1)
            moved_right = pltpu.roll(right, offset, 1)
            out_left = out_left + weight * jnp.where(lane < offset, 0.0, moved_left)
            out_right = out_right + weight * jnp.where(lane < offset, moved_left, moved_right)
        feat_out[index, :, 0:128] = out_left
        feat_out[index, :, 128:256] = out_right


def unpack_kernel(
    arrived,
    feat,
    taps,
    grad,
    mixed,
    grad_query,
    grad_key,
    grad_value,
    proj,
    basis,
    wide,
    sorted_rows,
):
    fill(wide, arrived[...].astype(F32))

    def both(half, row):
        return jnp.concatenate(
            [wide[half, pl.ds(row + chan, ROWS, stride=8), :] for chan in range(CHAN)], axis=0
        )

    long_out = [both(half, 0) for half in range(2)]
    carried_grad = [both(half, 2) for half in range(2)]
    halo = jnp.concatenate([wide[half, pl.ds(4, ROWS, stride=8), :] for half in range(2)], axis=0)
    lane = lax.broadcasted_iota(jnp.int32, (128, 128), 1)
    feats = []
    for index in range(3):
        high = pltpu.roll(halo, 128 - HALO * (3 + index), 1)
        low = pltpu.roll(halo, 128 - HALO * (6 + index), 1)
        left = jnp.where(lane < HALO, high + low, feat[index, :, 0:128])
        feats.append((left, feat[index, :, 128:256]))
    cotangent = grad[...].astype(F32)
    cotangent = (cotangent[:, 0:128], cotangent[:, 128:256])
    for half in range(2):
        mixed[:, half * 128 : half * 128 + 128] = (feats[0][half] * long_out[half]).astype(BF16)
    grads = (
        [cotangent[half] * long_out[half] for half in range(2)],
        [carried_grad[half] * feats[2][half] for half in range(2)],
        [carried_grad[half] * feats[1][half] for half in range(2)],
    )
    for index, ref in enumerate((grad_query, grad_key, grad_value)):
        left, right = [part.astype(BF16).astype(F32) for part in grads[index]]
        out_left = taps[index * TAPS] * left
        out_right = taps[index * TAPS] * right
        for offset in range(1, TAPS):
            weight = taps[index * TAPS + offset]
            moved_left = pltpu.roll(left, 128 - offset, 1)
            moved_right = pltpu.roll(right, 128 - offset, 1)
            moved_halo = pltpu.roll(halo, (128 - offset - HALO * index) % 128, 1)
            edge = lane >= 128 - offset
            out_left = out_left + weight * jnp.where(edge, moved_right, moved_left)
            out_right = out_right + weight * jnp.where(edge, moved_halo, moved_right)
        ref[:, 0:128] = out_left.astype(BF16)
        ref[:, 128:256] = out_right.astype(BF16)
    rows = wide[0, pl.ds(7, ROWS, stride=8), :] + wide[1, pl.ds(7, ROWS, stride=8), :]
    rows = rows * (1.0 / math.sqrt(TOTAL))
    rows = jnp.concatenate([rows, jnp.zeros_like(rows)], axis=0).T
    proj[:, 0:ROWS] = rows[0:FEAT, 0:ROWS]
    proj[:, ROWS : 2 * ROWS] = rows[FEAT : 2 * FEAT, 0:ROWS]
    totals = []
    for quarter in range(4):
        pair = []
        for half in range(2):
            total = wide[half, quarter * 8 : quarter * 8 + 8, :]
            for source in range(quarter + 4, ROWS, 4):
                total = total + wide[half, source * 8 : source * 8 + 8, :]
            pair.append(total)
        totals.append(pair)
    scale = math.sqrt(FEAT / (TOTAL * 1024))
    ordered = [
        jnp.concatenate([left[5:6], right[5:6], left[6:7], right[6:7]], axis=0)
        for left, right in totals
    ]
    for group in range(8):
        lanes = slice(group * 16, group * 16 + 16)
        merged = jnp.concatenate(
            [value[:, lanes] for value in ordered] + [jnp.zeros((4, 64), F32)], axis=1
        )
        sorted_rows[pl.ds(group, 4, stride=8), :] = merged * scale
    sorted_rows[32:33, :] = (
        jnp.concatenate([left[4:5, 64:80] for left, _ in totals] + [jnp.zeros((1, 64), F32)], axis=1)
        * scale
    )
    basis[...] = sorted_rows[0:EMB, 0:FEAT]


SMEM = pl.BlockSpec(memory_space=pltpu.SMEM)
VMEM = pl.BlockSpec(memory_space=pltpu.VMEM)
HBM = pl.BlockSpec(memory_space=pltpu.HBM)
LIMIT = 62 * 1024 * 1024
ROOMY = 32 * 1024 * 1024


def call(kernel, name, own, near, far, outs, scratch, flops, moved, limit=LIMIT):
    landing = [pltpu.VMEM(value.shape, value.dtype) for value in far]
    return pl.pallas_call(
        kernel,
        name=name,
        in_specs=[SMEM] * len(own) + [VMEM] * len(near) + [HBM] * len(far),
        out_specs=[HBM if direct else VMEM for _, direct in outs],
        out_shape=[value for value, _ in outs],
        scratch_shapes=(landing if kernel is not pack_kernel else [])
        + scratch
        + ([pltpu.SemaphoreType.DMA((len(far),))] if far else []),
        compiler_params=pltpu.CompilerParams(vmem_limit_bytes=limit),
        cost_estimate=pl.CostEstimate(flops=flops, bytes_accessed=moved, transcendentals=0),
    )(*own, *near, *far)


def shape(dims, kind=F32):
    return jax.ShapeDtypeStruct(dims, kind)


def run_pack(query_in, key_in, value_in, grad_out):
    return call(
        pack_kernel,
        "pack",
        [],
        [],
        [query_in, key_in, value_in, grad_out],
        [(shape((ROWS, 8, COLS), BF16), False)],
        [pltpu.VMEM((4, 128, COLS), BF16), pltpu.VMEM((2, 512, 128), F32)],
        1 << 20,
        1 << 19,
    )[0]


def run_filter(own, weight, bias, proj, decay, consts):
    names = ("pick", "turn", "right", "forward", "twiddle", "full")
    return call(
        filter_kernel,
        "filter",
        [own],
        [],
        [weight, bias, proj, decay] + [consts[name] for name in names],
        [
            (shape((ROWS * FEAT, COLS), BF16), True),
            (shape((ROWS * FEAT, COLS), BF16), True),
            (shape((CHAN * ROWS, COLS)), False),
            (shape((CHAN * ROWS, 2 * COLS)), False),
            (shape((CHAN * FEAT, 128)), False),
        ],
        [
            pltpu.VMEM((128, 128), F32),
            pltpu.VMEM((ROWS * FEAT, COLS), BF16),
            pltpu.VMEM((512, COLS), F32),
            pltpu.VMEM((512, COLS), F32),
            pltpu.VMEM((CHAN * ROWS, COLS), F32),
            pltpu.VMEM((ROWS * FEAT, COLS), BF16),
            pltpu.VMEM((ROWS * FEAT, COLS), BF16),
            pltpu.SemaphoreType.DMA((2, 8)),
        ],
        1 << 33,
        1 << 23,
    )


def run_gradient(own, arrived, short, cosine, envelope, columns, filter_spec, consts):
    names = ("back", "back_turn", "place", "forward", "last", "twiddle", "full")
    return call(
        gradient_kernel,
        "gradient",
        [own],
        [],
        [arrived, envelope, columns, cosine, filter_spec, short] + [consts[name] for name in names],
        [
            (shape((HANDED, 128)), True),
            (shape((32, 8, 128)), False),
        ],
        [
            pltpu.VMEM((128, 128), F32),
            pltpu.VMEM((2, CHAN * ROWS, 128), F32),
            pltpu.VMEM((HANDED, 128), F32),
            pltpu.SemaphoreType.DMA((3,)),
        ],
        1 << 32,
        1 << 23,
    )


def run_output(own, skip, handed, act, consts):
    names = ("last", "twiddle", "full")
    return call(
        output_kernel,
        "output",
        [own],
        [],
        [handed, act, skip] + [consts[name] for name in names],
        [(shape((ROWS, 8, COLS), BF16), False)],
        [pltpu.VMEM((2, ROWS * 8, 128), F32)],
        1 << 31,
        1 << 22,
        52 * 1024 * 1024,
    )[0]


def run_compose(packed, basis_parts):
    return call(
        compose_kernel,
        "compose",
        [],
        [packed, basis_parts],
        [],
        [(shape((ROWS, 8, COLS), BF16), False)],
        [],
        1 << 20,
        1 << 20,
        ROOMY,
    )[0]


def run_local(query_in, key_in, value_in, short):
    return call(
        local_kernel,
        "local",
        [],
        [],
        [query_in, key_in, value_in, short],
        [(shape((3, 128, COLS)), False), (shape((3 * TAPS, 128, 128)), False)],
        [],
        1 << 28,
        1 << 20,
        ROOMY,
    )


def run_unpack(arrived, feat, taps, grad_out):
    block = shape((128, COLS), BF16)
    return call(
        unpack_kernel,
        "unpack",
        [],
        [arrived, feat, taps, grad_out],
        [],
        [(value, False) for value in [block] * 4 + [shape((FEAT, 128)), shape((EMB, FEAT))]],
        [pltpu.VMEM((2, ROWS * 8, 128), F32), pltpu.VMEM((64, 128), F32)],
        1 << 20,
        1 << 20,
        ROOMY,
    )


def make_consts():
    forward, last, twiddle, full = transform_tables()
    right, turn, pick, back, back_turn, place = basis_tables()
    return dict(
        forward=jnp.asarray(forward),
        last=jnp.asarray(last),
        twiddle=jnp.asarray(twiddle),
        full=jnp.asarray(full),
        right=jnp.asarray(right),
        turn=jnp.asarray(turn),
        pick=jnp.asarray(pick),
        back=jnp.asarray(back),
        back_turn=jnp.asarray(back_turn),
        place=jnp.asarray(place),
    )


CTX = ("zh", "yh", "yl", "core")
NEAR = ("yl", "core", "x", "zl")


def exchange(value, axes):
    return lax.all_to_all(value, axes, split_axis=0, concat_axis=0, tiled=True)


def on_device(
    query_in,
    key_in,
    value_in,
    short_kernel,
    basis_weight,
    basis_bias,
    filter_proj,
    decay_rate,
    skip_gain,
    grad_out,
):
    consts = make_consts()
    own = lax.axis_index(CTX).astype(jnp.int32).reshape(1)
    with jax.named_scope("spread"):
        arrived = exchange(run_pack(query_in, key_in, value_in, grad_out), CTX)
    short = short_kernel.transpose(0, 2, 1)
    block_feat, block_taps = run_local(query_in, key_in, value_in, short)
    act, cosine, envelope, filter_spec, columns = run_filter(
        own,
        basis_weight.T,
        basis_bias.reshape(1, FEAT),
        filter_proj.T,
        decay_rate.reshape(1, 128),
        consts,
    )
    handed, basis_own = run_gradient(
        own, arrived, short, cosine, envelope, columns, filter_spec, consts
    )
    with jax.named_scope("basis"):
        basis_parts = exchange(basis_own, NEAR)
    packed = run_output(
        own, skip_gain.reshape(1, 128), handed, act, consts
    )
    composed = run_compose(packed, basis_parts)
    with jax.named_scope("collect"):
        returned = exchange(composed, CTX)
    mixed, grad_query, grad_key, grad_value, grad_proj, grad_basis = run_unpack(
        returned, block_feat, block_taps, grad_out
    )
    return (mixed, grad_query, grad_key, grad_value, grad_proj.T, grad_basis.T)


def solution(mesh):
    finer = Mesh(mesh.devices.reshape(4, 4, 2, 2, 4, 2), CTX + ("x", "zl"))
    rows = ("x", "zl")
    block = P(rows, CTX)
    return jax.shard_map(
        on_device,
        mesh=finer,
        in_specs=(
            block,
            block,
            block,
            P(None, rows, None),
            P(),
            P(),
            P(rows, None),
            P(rows),
            P(rows),
            block,
        ),
        out_specs=(block, block, block, block, P(rows, None), P()),
        check_vma=False,
    )
```

```python
import math

import jax
import jax.numpy as jnp
import numpy as np
from jax import lax
from jax.experimental import pallas as pl
from jax.experimental.pallas import tpu as pltpu
from jax.sharding import Mesh
from jax.sharding import PartitionSpec as P
import ml_dtypes

F32 = jnp.float32
BF16 = jnp.bfloat16
EXACT = lax.Precision.HIGHEST

ROWS = 64
COLS = 256
TOTAL = ROWS * COLS
FEAT = 64
EMB = 33
TAPS = 7
CHAN = 2
GROUP = 40
TURN = 1.0 / (2.0 * math.pi)

SIN_COEF = (4.442879676818848, -7.307816505432129, 3.5977742671966553, -0.7911993861198425)
COS_COEF = (
    1.4142135381698608,
    -6.978850841522217,
    5.739460468292236,
    -1.883557915687561,
    0.3106880187988281,
)


def halves(table, count):
    parts = []
    rest = np.asarray(table, np.float64)
    for _ in range(count):
        part = rest.astype(np.float32).astype(ml_dtypes.bfloat16)
        parts.append(part)
        rest = rest - part.astype(np.float64)
    return parts


def transform_tables():
    rows = np.arange(ROWS)
    cols = np.arange(COLS)
    first = 2.0 * np.pi * ((4 * rows[:, None] + 1) * rows[None, :] % (4 * ROWS)) / (4 * ROWS)
    first_re, first_im = np.cos(first), -np.sin(first)
    forward = np.concatenate([first_re, first_im], axis=0)
    forward_cat = np.concatenate(halves(forward, 2), axis=1)
    last = np.concatenate([first_re.T, -first_im.T], axis=1) / TOTAL
    last_hi, last_lo = halves(last, 2)
    last_cat = np.concatenate([last_hi, last_lo, last_hi], axis=1)
    turn = 2.0 * np.pi * ((4 * rows[:, None] + 1) * cols[None, :]) / (4 * TOTAL)
    twiddle = np.stack([np.cos(turn), -np.sin(turn)]).astype(np.float32)
    inner = 2.0 * np.pi * (cols[:, None] * cols[None, :] % COLS) / COLS
    inner_re, inner_im = np.cos(inner), -np.sin(inner)
    full = np.concatenate(
        [
            np.concatenate([inner_re, inner_im], axis=1),
            np.concatenate([-inner_im, inner_re], axis=1),
        ],
        axis=0,
    )
    full_hi, full_lo = halves(full, 2)
    return forward_cat, last_cat, twiddle, np.stack([full_hi, full_lo])


def basis_tables():
    freq = np.arange(1, 17)
    cols = np.arange(COLS)
    rows = np.arange(ROWS)
    inner = 2.0 * np.pi * (freq[:, None] * cols[None, :] % TOTAL) / TOTAL
    short = np.concatenate(
        [np.cos(inner), np.sin(inner), cols[None, :] / TOTAL, np.ones((1, COLS))], axis=0
    )
    width = short.shape[0]
    hi, mid, lo = halves(short, 3)
    right = np.zeros((256, COLS), ml_dtypes.bfloat16)
    for place, part in ((0, hi), (GROUP, hi), (2 * GROUP, hi)):
        right[place : place + width] = part
    for place, part in ((128, mid), (128 + GROUP, lo), (128 + 2 * GROUP, mid)):
        right[place : place + width] = part
    outer = 2.0 * np.pi * (freq[None, :] * rows[:, None] % ROWS) / ROWS
    cos_out, sin_out = np.cos(outer), np.sin(outer)
    one = np.ones((ROWS, 1))
    block = rows[:, None] / ROWS
    cos_row = np.concatenate([cos_out, cos_out, one, one], axis=1)
    sin_row = np.concatenate([sin_out, sin_out, 0 * one, block], axis=1)
    turn = np.zeros((2, ROWS, 128), np.float32)
    for place in (0, GROUP, 2 * GROUP):
        turn[0, :, place : place + width] = cos_row
        turn[1, :, place : place + width] = sin_row
    pick = np.zeros((2, 128, 128), np.float32)
    for place in (0, GROUP, 2 * GROUP):
        for index in range(16):
            pick[0, 2 * index + 1, place + index] = 1.0
            pick[0, 2 * index + 2, place + 16 + index] = 1.0
            pick[1, 2 * index + 2, place + index] = 1.0
            pick[1, 2 * index + 1, place + 16 + index] = -1.0
        pick[0, 0, place + 32] = 1.0
        pick[0, EMB, place + 33] = 1.0
        pick[1, 0, place + 33] = 1.0
    back = np.zeros((COLS, 128))
    back[:, :width] = short.T
    back[:, 64:80] = short[16:32].T
    back[:, 80:96] = short[:16].T
    back_hi, back_lo = halves(back, 2)
    back_cat = np.concatenate([back_hi, back_lo], axis=1)
    back_turn = np.zeros((ROWS, 128), np.float32)
    back_turn[:, :32] = cos_row[:, :32]
    back_turn[:, 32] = 1.0
    back_turn[:, 33] = rows / ROWS
    back_turn[:, 64:80] = -sin_out
    back_turn[:, 80:96] = sin_out
    place = np.zeros((8, 8, 128), np.float32)
    for wanted in range(EMB):
        row, group = divmod(wanted, 8)
        if wanted == 0:
            lanes = (32, 33)
        elif wanted % 2:
            lanes = ((wanted - 1) // 2, 64 + (wanted - 1) // 2)
        else:
            lanes = (16 + (wanted - 2) // 2, 80 + (wanted - 2) // 2)
        for lane in lanes:
            place[group, row, lane] = 1.0
    return right, turn, pick, back_cat, back_turn, place


def split(value):
    hi = value.astype(BF16)
    lo = (value - hi.astype(F32)).astype(BF16)
    return hi, lo


def dot(left, right):
    return jnp.dot(left, right, preferred_element_type=F32)


def spectrum(signals, forward, twiddle_re, twiddle_im, full_hi, full_lo):
    wide = jnp.concatenate(signals, axis=1)
    section = dot(forward, jnp.concatenate([wide, wide], axis=0))
    turned = []
    for index in range(len(signals)):
        part = section[:, index * COLS : (index + 1) * COLS]
        part_re, part_im = part[:ROWS], part[ROWS:]
        turned.append(
            jnp.concatenate(
                [
                    part_re * twiddle_re - part_im * twiddle_im,
                    part_re * twiddle_im + part_im * twiddle_re,
                ],
                axis=1,
            )
        )
    return full_product(jnp.concatenate(turned, axis=0), full_hi, full_lo)


def full_product(value, full_hi, full_lo):
    hi, lo = split(value)
    return dot(hi, full_hi) + dot(lo, full_hi) + dot(hi, full_lo)


def restore(conj_spec, count, last, twiddle_re, twiddle_im, full_hi, full_lo):
    back = full_product(conj_spec, full_hi, full_lo)
    stacked = []
    for index in range(count):
        part = back[index * ROWS : (index + 1) * ROWS]
        part_re, part_im = part[:, :COLS], part[:, COLS:]
        stacked.append(
            jnp.concatenate(
                [
                    part_re * twiddle_re - part_im * twiddle_im,
                    part_re * twiddle_im + part_im * twiddle_re,
                ],
                axis=0,
            )
        )
    hi, lo = split(jnp.concatenate(stacked, axis=1))
    result = dot(last, jnp.concatenate([hi, hi, lo], axis=0))
    return [result[:, index * COLS : (index + 1) * COLS] for index in range(count)]


def take(ref, start, count, stride):
    return jnp.concatenate(
        [ref[half, pl.ds(start, count, stride=stride), :] for half in range(2)], axis=1
    )


def put(ref, start, count, stride, value):
    for half in range(2):
        ref[half, pl.ds(start, count, stride=stride), :] = value[:, half * 128 : half * 128 + 128]


AT_FEAT = 0
AT_SPEC = 2 * ROWS * 8
AT_RAW = AT_SPEC + 4 * 2 * CHAN * ROWS
AT_FILTER = AT_RAW + 2 * CHAN * ROWS
HANDED = AT_FILTER + 4 * CHAN * ROWS


def tiles(ref, start, stride, count, picked_tiles):
    return jnp.concatenate(
        [ref[start + tile * stride : start + tile * stride + count, :] for tile in picked_tiles], axis=1
    )


def fill(ref, value):
    for half in range(2):
        ref[half] = value[..., half * 128 : half * 128 + 128].reshape(ref.shape[1], 128)


def begin(sems, pairs):
    copies = [
        pltpu.make_async_copy(source, target, sems.at[index])
        for index, (source, target) in enumerate(pairs)
    ]
    for copy in copies:
        copy.start()
    return copies


def picked(row, wanted):
    lane = lax.broadcasted_iota(jnp.int32, row.shape, 1)
    return jnp.sum(jnp.where(lane == wanted, row, 0.0), axis=1, keepdims=True)


def pack_kernel(query, key, value, grad, out, held, wide, stage, out_sems, sems):
    copies = begin(sems, [(ref, held.at[index]) for index, ref in enumerate((query, key, value, grad))])
    for index in range(4):
        copies[index].wait()
        block = held[index].astype(F32)
        for half in range(2):
            wide[half, index * 128 : (index + 1) * 128, :] = block[:, half * 128 : half * 128 + 128]
    leaving = []
    for part in range(4):
        for peer in range(part * 16, part * 16 + 16):
            stage[peer] = take(wide, peer, 8, ROWS).astype(BF16)
        rows = pl.ds(part * 16, 16)
        leaving += begin(out_sems.at[pl.ds(part, 1)], [(stage.at[rows], out.at[rows])])
    for copy in leaving:
        copy.wait()


def expm1_small(value):
    series = jnp.ones_like(value)
    for order in range(9, 1, -1):
        series = 1.0 + value * series * (1.0 / order)
    return jnp.where(value > -0.5, value * series, jnp.exp(value) - 1.0)


def filter_kernel(
    own,
    weight_src,
    bias_src,
    proj_src,
    decay_src,
    pick_src,
    turn_src,
    right_src,
    forward_src,
    twiddle_src,
    full_src,
    act_out,
    cos_out,
    env_out,
    spec_out,
    column_out,
    weight,
    bias,
    proj,
    decay,
    pick,
    turn,
    right,
    forward,
    twiddle,
    full,
    layer,
    left,
    phase,
    phase_odd,
    filt,
    act,
    cosv,
    out_sems,
    sems,
):
    first = own[0]
    copies = begin(
        sems,
        [
            (weight_src, weight),
            (bias_src, bias),
            (pick_src, pick),
            (proj_src, proj),
            (turn_src, turn),
            (right_src, right),
            (decay_src, decay),
            (forward_src, forward),
            (twiddle_src, twiddle),
            (full_src, full),
        ],
    )
    layer[...] = jnp.zeros((128, 128), F32)
    for copy in copies[:3]:
        copy.wait()
    layer[0:EMB, 0:FEAT] = weight[...]
    layer[EMB : EMB + 1, 0:FEAT] = bias[...]
    layer_all = layer[...].T[0:FEAT, :]
    same = jnp.dot(layer_all, pick[0], precision=EXACT, preferred_element_type=F32) * TURN
    cross = jnp.dot(layer_all, pick[1], precision=EXACT, preferred_element_type=F32) * TURN
    lane = lax.broadcasted_iota(jnp.int32, (FEAT, 128), 1)
    sublane = lax.broadcasted_iota(jnp.int32, (8, 128), 0)
    for copy in copies[3:7]:
        copy.wait()
    columns = []
    for chan in range(CHAN):
        hit = lane == first + 64 * chan
        column = jnp.sum(jnp.where(hit, proj[...], 0.0), axis=1, keepdims=True)
        column_wide = jnp.broadcast_to(column, (FEAT, 128))
        column_out[chan * FEAT : (chan + 1) * FEAT, :] = column_wide
        columns.append(column_wide)

    def make_left(block, carry):
        value = same * turn[0, pl.ds(block, 1), :] + cross * turn[1, pl.ds(block, 1), :]
        hi = value.astype(BF16).astype(F32)
        rest = value - hi
        mid = rest.astype(BF16).astype(F32)
        lo = rest - mid
        one = jnp.where(lane < GROUP, hi, jnp.where(lane < 2 * GROUP, mid, lo))
        two = jnp.where(lane < 2 * GROUP, hi, mid)
        start = pl.multiple_of(block * FEAT, FEAT)
        left[pl.ds(start, FEAT), 0:128] = one.astype(BF16)
        left[pl.ds(start, FEAT), 128:256] = two.astype(BF16)
        return carry

    lax.fori_loop(0, ROWS, make_left, 0, unroll=4)

    def fetch(index, phase):
        base = pl.multiple_of(index * 512, 512)
        phase[...] = dot(left[pl.ds(base, 512), :], right[...])

    def finish(index, phase):
        base = pl.multiple_of(index * 512, 512)
        for half in range(2):
            lanes = slice(half * 128, half * 128 + 128)
            sums = [jnp.zeros((8, 128), F32)] * CHAN
            for inner in range(8):
                near = inner * FEAT
                turns = phase[near : near + FEAT, lanes]
                rest = turns - jnp.round(turns)
                square = rest * rest
                sine = SIN_COEF[-1] * square + SIN_COEF[-2]
                cosine = COS_COEF[-1] * square + COS_COEF[-2]
                for coef in SIN_COEF[-3::-1]:
                    sine = sine * square + coef
                for coef in COS_COEF[-3::-1]:
                    cosine = cosine * square + coef
                sine = sine * rest
                whole_sine = sine * cosine
                whole_cosine = 1.0 - sine * sine
                act[pl.ds(base + near, FEAT), lanes] = whole_sine.astype(BF16)
                cosv[pl.ds(base + near, FEAT), lanes] = whole_cosine.astype(BF16)
                for chan in range(CHAN):
                    total = jnp.sum(whole_sine * columns[chan], axis=0, keepdims=True)
                    sums[chan] = jnp.where(sublane == inner, total, sums[chan])
            for chan in range(CHAN):
                start = pl.multiple_of(chan * ROWS + index * 8, 8)
                filt[pl.ds(start, 8), lanes] = sums[chan]
        send(index, 0).start()
        send(index, 1).start()

    def pair(index, carry):
        fetch(2 * index + 1, phase_odd)
        finish(2 * index, phase)
        fetch(jnp.minimum(2 * index + 2, 7), phase)
        finish(2 * index + 1, phase_odd)
        return carry

    def send(index, which):
        rows = pl.ds(pl.multiple_of(index * 512, 512), 512)
        source, target = ((act, act_out), (cosv, cos_out))[which]
        return pltpu.make_async_copy(source.at[rows], target.at[rows], out_sems.at[which, index])

    fetch(0, phase)
    lax.fori_loop(0, 4, pair, 0)
    ratio = decay[...] * (1.0 / TOTAL)
    energy = expm1_small(-2.0 * decay[...]) / expm1_small(-2.0 * ratio)
    norm = 1.0 / jnp.sqrt(energy)
    for copy in copies[7:]:
        copy.wait()
    position = (
        lax.broadcasted_iota(jnp.int32, (ROWS, COLS), 0) * COLS
        + lax.broadcasted_iota(jnp.int32, (ROWS, COLS), 1)
    ).astype(F32)
    signals = []
    for chan in range(CHAN):
        rate = picked(decay[...], first + 64 * chan)
        envelope = jnp.exp(-(rate * position) * (1.0 / TOTAL)) * picked(norm, first + 64 * chan)
        env_out[chan * ROWS : (chan + 1) * ROWS, :] = envelope
        signals.append((filt[chan * ROWS : (chan + 1) * ROWS, :] * envelope).astype(BF16))
    spec_out[...] = spectrum(signals, forward[...], twiddle[0], twiddle[1], full[0], full[1])
    for index in range(8):
        send(index, 0).wait()
        send(index, 1).wait()


def own_taps(first, short, taps, order):
    row = lax.broadcasted_iota(jnp.int32, (TAPS, 128), 0)
    lane = lax.broadcasted_iota(jnp.int32, (TAPS, 128), 1)
    columns = jnp.where(row == 0, 1.0, 0.0)
    for place, which in order:
        for chan in range(CHAN):
            hit = lane == first + 64 * chan
            column = jnp.sum(jnp.where(hit, short[which], 0.0), axis=1, keepdims=True)
            columns = jnp.where(lane == place + chan, column, columns)
    taps[...] = jnp.zeros((128, 128), F32)
    taps[0:TAPS, :] = columns
    return taps[...].T[0:8, :]


def gradient_kernel(
    own,
    arrived_src,
    envelope_src,
    columns_src,
    cosine_src,
    filter_spec_src,
    short_src,
    back_src,
    back_turn_src,
    place_src,
    forward_src,
    last_src,
    twiddle_src,
    full_src,
    handed_out,
    basis_out,
    arrived,
    envelope,
    columns,
    cosine,
    filter_spec,
    short,
    back,
    back_turn,
    place,
    forward,
    last,
    twiddle,
    full,
    taps,
    raw,
    handed,
    out_sems,
    sems,
):
    first = own[0]
    copies = begin(
        sems,
        [
            (short_src, short),
            (arrived_src, arrived),
            (forward_src, forward),
            (twiddle_src, twiddle),
            (full_src, full),
            (last_src, last),
            (envelope_src, envelope),
            (cosine_src, cosine),
            (columns_src, columns),
            (filter_spec_src, filter_spec),
            (back_src, back),
            (back_turn_src, back_turn),
            (place_src, place),
        ],
    )
    copies[0].wait()
    weights = own_taps(first, short, taps, ((0, 0), (2, 1), (4, 2)))
    copies[1].wait()
    signal = arrived[...].astype(F32)
    lane = lax.broadcasted_iota(jnp.int32, (ROWS, 8, 128), 2)
    zeros = jnp.zeros((1, 8, 128), F32)
    left, right = signal[:, :, 0:128], signal[:, :, 128:256]
    sum_left = weights[None, :, 0:1] * left
    sum_right = weights[None, :, 0:1] * right
    for offset in range(1, TAPS):
        weight = weights[None, :, offset : offset + 1]
        moved_left = pltpu.roll(left, offset, 2)
        moved_right = pltpu.roll(right, offset, 2)
        before = jnp.concatenate([zeros, moved_right[:-1]], axis=0)
        sum_left = sum_left + weight * jnp.where(lane < offset, before, moved_left)
        sum_right = sum_right + weight * jnp.where(lane < offset, moved_left, moved_right)
    for half, result in enumerate((sum_left, sum_right)):
        handed[AT_FEAT + half * 512 : AT_FEAT + half * 512 + 512, :] = result.reshape(512, 128)

    def leave(part, start, size):
        rows = pl.ds(start, size)
        return begin(out_sems.at[pl.ds(part, 1)], [(handed.at[rows], handed_out.at[rows])])

    leaving = leave(0, AT_FEAT, AT_SPEC - AT_FEAT)

    def plane(index):
        return jnp.concatenate(
            [handed[pl.ds(AT_FEAT + half * 512 + index, ROWS, stride=8), :] for half in range(2)],
            axis=1,
        )

    signals = []
    for chan in range(CHAN):
        signals.append((plane(2 + chan) * plane(4 + chan)).astype(BF16))
    for chan in range(CHAN):
        signals.append((plane(chan) * plane(6 + chan)).astype(BF16))
    for copy in copies[2:5]:
        copy.wait()
    tables = (twiddle[0], twiddle[1], full[0], full[1])
    spec_all = spectrum(signals, forward[...], *tables)
    for tile in range(4):
        handed[AT_SPEC + tile * 256 : AT_SPEC + tile * 256 + 256, :] = spec_all[
            :, tile * 128 : tile * 128 + 128
        ]
    leaving += leave(1, AT_SPEC, AT_RAW - AT_SPEC)
    carried, grad = spec_all[: CHAN * ROWS], spec_all[CHAN * ROWS :]
    carried_re, carried_im = carried[:, :COLS], carried[:, COLS:]
    grad_re, grad_im = grad[:, :COLS], grad[:, COLS:]
    crossed = jnp.concatenate(
        [
            carried_re * grad_re + carried_im * grad_im,
            carried_im * grad_re - carried_re * grad_im,
        ],
        axis=1,
    )
    for copy in copies[5:7]:
        copy.wait()
    filter_grad = restore(crossed, CHAN, last[...], *tables)
    for chan in range(CHAN):
        rounded = filter_grad[chan].astype(BF16).astype(F32)
        scaled = rounded * envelope[chan * ROWS : (chan + 1) * ROWS, :]
        for half in range(2):
            raw[half, chan * ROWS : (chan + 1) * ROWS, :] = scaled[:, half * 128 : half * 128 + 128]
    for copy in copies[7:]:
        copy.wait()
    for half in range(2):
        handed[AT_RAW + half * 128 : AT_RAW + half * 128 + 128, :] = raw[half]
    for tile in range(4):
        handed[AT_FILTER + tile * 128 : AT_FILTER + tile * 128 + 128, :] = filter_spec[
            :, tile * 128 : tile * 128 + 128
        ]
    leaving += leave(2, AT_RAW, HANDED - AT_RAW)
    column0 = columns[0:FEAT, :]
    column1 = columns[FEAT : 2 * FEAT, :]
    back_all = back[...]

    def chunk(index, basis_sum):
        base = pl.multiple_of(index * 512, 512)
        start = pl.multiple_of(index * 8, 8)
        rows = [
            [raw[half, pl.ds(chan * ROWS + start, 8), :] for half in range(2)] for chan in range(CHAN)
        ]
        angles = back_turn[pl.ds(start, 8), :]
        parts = []
        for inner in range(8):
            near = inner * FEAT
            pieces = []
            for half in range(2):
                lanes = slice(half * 128, half * 128 + 128)
                value = (
                    column0 * rows[0][half][inner : inner + 1, :]
                    + column1 * rows[1][half][inner : inner + 1, :]
                )
                value = value * cosine[pl.ds(base + near, FEAT), lanes].astype(F32)
                pieces.append(value.astype(BF16))
            parts.append(jnp.concatenate(pieces, axis=1))
        product = dot(jnp.concatenate(parts, axis=0), back_all)
        for inner in range(8):
            near = inner * FEAT
            both = product[near : near + FEAT, 0:128] + product[near : near + FEAT, 128:256]
            basis_sum = basis_sum + both * angles[inner : inner + 1, :]
        return basis_sum

    basis_sum = lax.fori_loop(0, 8, chunk, jnp.zeros((FEAT, 128), F32), unroll=4)
    pieces = [
        lax.dot_general(
            place[group],
            basis_sum,
            (((1,), (1,)), ((), ())),
            precision=EXACT,
            preferred_element_type=F32,
        )
        for group in range(8)
    ]
    for quarter in range(4):
        row = jnp.concatenate(
            [piece[:, quarter * 16 : quarter * 16 + 16] for piece in pieces], axis=1
        )
        for peer in range(8):
            basis_out[quarter * 8 + peer] = row
    for copy in leaving:
        copy.wait()


HALO = TAPS - 1


def output_kernel(
    own,
    handed_src,
    act_src,
    skip_src,
    last_src,
    twiddle_src,
    full_src,
    out,
    handed,
    act,
    skip,
    last,
    twiddle,
    full,
    rows_out,
    sems,
):
    first = own[0]
    copies = begin(
        sems,
        [
            (handed_src, handed),
            (full_src, full),
            (twiddle_src, twiddle),
            (last_src, last),
            (skip_src, skip),
            (act_src, act),
        ],
    )
    lane128 = lax.broadcasted_iota(jnp.int32, (FEAT, 128), 1)
    row_lane = lane128 % 8
    for copy in copies[0:4]:
        copy.wait()
    tables = (twiddle[0], twiddle[1], full[0], full[1])
    own_rows = CHAN * ROWS
    carried_re = tiles(handed, AT_SPEC, 256, own_rows, (0, 1))
    carried_im = tiles(handed, AT_SPEC, 256, own_rows, (2, 3))
    grad_re = tiles(handed, AT_SPEC + own_rows, 256, own_rows, (0, 1))
    grad_im = tiles(handed, AT_SPEC + own_rows, 256, own_rows, (2, 3))
    filt_re = tiles(handed, AT_FILTER, 128, own_rows, (0, 1))
    filt_im = tiles(handed, AT_FILTER, 128, own_rows, (2, 3))
    crossed = jnp.concatenate(
        [
            jnp.concatenate(
                [
                    filt_re * carried_re - filt_im * carried_im,
                    -(filt_re * carried_im + filt_im * carried_re),
                ],
                axis=1,
            ),
            jnp.concatenate(
                [
                    filt_re * grad_re + filt_im * grad_im,
                    filt_im * grad_re - filt_re * grad_im,
                ],
                axis=1,
            ),
        ],
        axis=0,
    )
    sums = restore(crossed, 2 * CHAN, last[...], *tables)
    copies[4].wait()

    def plane(index):
        return jnp.concatenate(
            [handed[pl.ds(AT_FEAT + half * 512 + index, ROWS, stride=8), :] for half in range(2)],
            axis=1,
        )

    blank = jnp.zeros((1, 128), F32)
    for chan in range(CHAN):
        gain = picked(skip[...], first + 64 * chan)
        query, key, value, cotangent = [plane(2 * index + chan) for index in range(4)]
        carried_own = (key * value).astype(BF16).astype(F32)
        grad_own = (query * cotangent).astype(BF16).astype(F32)
        long_out = (sums[chan] + gain * carried_own).astype(BF16).astype(F32)
        carried_grad = (sums[CHAN + chan] + gain * grad_own).astype(BF16).astype(F32)
        put(rows_out, chan, ROWS, 8, long_out)
        put(rows_out, 2 + chan, ROWS, 8, carried_grad)
        follow = jnp.zeros((ROWS, 128), F32)
        before = jnp.zeros((ROWS, 128), F32)
        heads = (
            cotangent[:, 0:128] * long_out[:, 0:128],
            carried_grad[:, 0:128] * value[:, 0:128],
            carried_grad[:, 0:128] * key[:, 0:128],
        )
        wanted = [head.astype(BF16).astype(F32) for head in heads]
        for signal in (query, key, value):
            wanted.append(signal[:, 0:128].astype(BF16).astype(F32))
        for signal in (query, key, value):
            wanted.append(signal[:, 0:128] - signal[:, 0:128].astype(BF16).astype(F32))
        for index, head in enumerate(wanted):
            place = HALO * index
            head = pltpu.roll(head, place, 1) if place else head
            inside = (lane128 >= place) & (lane128 < place + HALO)
            if index < 3:
                follow = jnp.where(inside, head, follow)
            else:
                before = jnp.where(inside, head, before)
        halo = jnp.concatenate([follow[1:], blank], axis=0) + before
        rows_out[chan, pl.ds(4, ROWS, stride=8), :] = halo
    copies[5].wait()

    def chunk(index, proj_sum):
        base = pl.multiple_of(index * 512, 512)
        start = pl.multiple_of(index * 8, 8)
        rows = [
            jnp.concatenate(
                [
                    handed[pl.ds(AT_RAW + half * 128 + chan * ROWS + start, 8), :]
                    for half in range(2)
                ],
                axis=1,
            )
            for chan in range(CHAN)
        ]
        wide = jnp.concatenate(rows, axis=0)
        hi = wide.astype(BF16).astype(F32)
        packed = jnp.concatenate([hi, wide - hi, jnp.zeros((128 - 4 * 8, COLS), F32)], axis=0)
        turned = jnp.concatenate(
            [packed[:, half * 128 : half * 128 + 128].T for half in range(2)], axis=0
        ).astype(BF16)
        product = dot(act[pl.ds(base, 512), :], turned)
        for inner in range(8):
            near = inner * FEAT
            proj_sum = proj_sum + jnp.where(row_lane == inner, product[near : near + FEAT, :], 0.0)
        return proj_sum

    proj_sum = lax.fori_loop(0, 8, chunk, jnp.zeros((FEAT, 128), F32), unroll=2)
    own_lane = lane128 % 16
    stacked = jnp.concatenate(
        [jnp.where(own_lane < 8, proj_sum, 0.0), jnp.where(own_lane >= 8, proj_sum, 0.0)], axis=0
    )
    proj_wide = lax.dot_general(
        jnp.ones((8, 128), F32),
        stacked,
        (((1,), (1,)), ((), ())),
        precision=EXACT,
        preferred_element_type=F32,
    )
    proj_hi = proj_wide.astype(BF16).astype(F32)
    row = lax.broadcasted_iota(jnp.int32, (ROWS, 8, 128), 1)
    for half, proj_part in enumerate((proj_hi, proj_wide - proj_hi)):
        extra = jnp.where(row == 7, proj_part[None], 0.0)
        value = jnp.where(row < 5, rows_out[half].reshape(ROWS, 8, 128), extra)
        out[:, :, half * 128 : half * 128 + 128] = value.astype(BF16)


def compose_kernel(packed, basis_parts, out, stage, out_sems):
    basis = basis_parts[0]
    for source in range(1, 32):
        basis = basis + basis_parts[source]
    row = lax.broadcasted_iota(jnp.int32, (8, 128), 0)
    lane = lax.broadcasted_iota(jnp.int32, (8, 128), 1)
    last = jnp.where((lane >= 64) & (lane < 80), pltpu.roll(basis, 64, 1)[4:5], 0.0)
    left = jnp.where(
        row == 4, last, jnp.where(row == 5, basis[0:1], jnp.where(row == 6, basis[2:3], 0.0))
    )
    right = jnp.where(row == 5, basis[1:2], jnp.where(row == 6, basis[3:4], 0.0))
    extra = jnp.concatenate([left, right], axis=1)
    leaving = []
    for part in range(4):
        rows = pl.ds(part * 16, 16)
        stage[rows] = (packed[rows].astype(F32) + extra[None]).astype(BF16)
        leaving += begin(out_sems.at[pl.ds(part, 1)], [(stage.at[rows], out.at[rows])])
    for copy in leaving:
        copy.wait()


def local_kernel(
    query_src, key_src, value_src, short_src, feat_out, taps_out, query, key, value, short, sems
):
    copies = begin(
        sems, [(query_src, query), (key_src, key), (value_src, value), (short_src, short)]
    )
    lane = lax.broadcasted_iota(jnp.int32, (128, 128), 1)
    for copy in copies:
        copy.wait()
    for index, ref in enumerate((query, key, value)):
        weights = jnp.concatenate([short[index], jnp.zeros((128 - TAPS, 128), F32)], axis=0).T
        for offset in range(TAPS):
            taps_out[index * TAPS + offset] = jnp.broadcast_to(
                weights[:, offset : offset + 1], (128, 128)
            )
        block = ref[...].astype(F32)
        left, right = block[:, 0:128], block[:, 128:256]
        out_left = taps_out[index * TAPS] * left
        out_right = taps_out[index * TAPS] * right
        for offset in range(1, TAPS):
            weight = taps_out[index * TAPS + offset]
            moved_left = pltpu.roll(left, offset, 1)
            moved_right = pltpu.roll(right, offset, 1)
            out_left = out_left + weight * jnp.where(lane < offset, 0.0, moved_left)
            out_right = out_right + weight * jnp.where(lane < offset, moved_left, moved_right)
        feat_out[index, :, 0:128] = out_left
        feat_out[index, :, 128:256] = out_right


def unpack_kernel(
    arrived,
    feat,
    taps,
    grad,
    mixed,
    grad_query,
    grad_key,
    grad_value,
    proj,
    basis,
    wide,
    sorted_rows,
):
    fill(wide, arrived[...].astype(F32))

    def both(half, row):
        return jnp.concatenate(
            [wide[half, pl.ds(row + chan, ROWS, stride=8), :] for chan in range(CHAN)], axis=0
        )

    long_out = [both(half, 0) for half in range(2)]
    carried_grad = [both(half, 2) for half in range(2)]
    halo = jnp.concatenate([wide[half, pl.ds(4, ROWS, stride=8), :] for half in range(2)], axis=0)
    lane = lax.broadcasted_iota(jnp.int32, (128, 128), 1)
    feats = []
    for index in range(3):
        high = pltpu.roll(halo, 128 - HALO * (3 + index), 1)
        low = pltpu.roll(halo, 128 - HALO * (6 + index), 1)
        left = jnp.where(lane < HALO, high + low, feat[index, :, 0:128])
        feats.append((left, feat[index, :, 128:256]))
    cotangent = grad[...].astype(F32)
    cotangent = (cotangent[:, 0:128], cotangent[:, 128:256])
    for half in range(2):
        mixed[:, half * 128 : half * 128 + 128] = (feats[0][half] * long_out[half]).astype(BF16)
    grads = (
        [cotangent[half] * long_out[half] for half in range(2)],
        [carried_grad[half] * feats[2][half] for half in range(2)],
        [carried_grad[half] * feats[1][half] for half in range(2)],
    )
    for index, ref in enumerate((grad_query, grad_key, grad_value)):
        left, right = [part.astype(BF16).astype(F32) for part in grads[index]]
        out_left = taps[index * TAPS] * left
        out_right = taps[index * TAPS] * right
        for offset in range(1, TAPS):
            weight = taps[index * TAPS + offset]
            moved_left = pltpu.roll(left, 128 - offset, 1)
            moved_right = pltpu.roll(right, 128 - offset, 1)
            moved_halo = pltpu.roll(halo, (128 - offset - HALO * index) % 128, 1)
            edge = lane >= 128 - offset
            out_left = out_left + weight * jnp.where(edge, moved_right, moved_left)
            out_right = out_right + weight * jnp.where(edge, moved_halo, moved_right)
        ref[:, 0:128] = out_left.astype(BF16)
        ref[:, 128:256] = out_right.astype(BF16)
    rows = wide[0, pl.ds(7, ROWS, stride=8), :] + wide[1, pl.ds(7, ROWS, stride=8), :]
    rows = rows * (1.0 / math.sqrt(TOTAL))
    rows = jnp.concatenate([rows, jnp.zeros_like(rows)], axis=0).T
    proj[:, 0:ROWS] = rows[0:FEAT, 0:ROWS]
    proj[:, ROWS : 2 * ROWS] = rows[FEAT : 2 * FEAT, 0:ROWS]
    totals = []
    for quarter in range(4):
        pair = []
        for half in range(2):
            total = wide[half, quarter * 8 : quarter * 8 + 8, :]
            for source in range(quarter + 4, ROWS, 4):
                total = total + wide[half, source * 8 : source * 8 + 8, :]
            pair.append(total)
        totals.append(pair)
    scale = math.sqrt(FEAT / (TOTAL * 1024))
    ordered = [
        jnp.concatenate([left[5:6], right[5:6], left[6:7], right[6:7]], axis=0)
        for left, right in totals
    ]
    for group in range(8):
        lanes = slice(group * 16, group * 16 + 16)
        merged = jnp.concatenate(
            [value[:, lanes] for value in ordered] + [jnp.zeros((4, 64), F32)], axis=1
        )
        sorted_rows[pl.ds(group, 4, stride=8), :] = merged * scale
    sorted_rows[32:33, :] = (
        jnp.concatenate([left[4:5, 64:80] for left, _ in totals] + [jnp.zeros((1, 64), F32)], axis=1)
        * scale
    )
    basis[...] = sorted_rows[0:EMB, 0:FEAT]


SMEM = pl.BlockSpec(memory_space=pltpu.SMEM)
VMEM = pl.BlockSpec(memory_space=pltpu.VMEM)
HBM = pl.BlockSpec(memory_space=pltpu.HBM)
LIMIT = 62 * 1024 * 1024
ROOMY = 32 * 1024 * 1024


def call(kernel, name, own, near, far, outs, scratch, flops, moved, limit=LIMIT):
    landing = [pltpu.VMEM(value.shape, value.dtype) for value in far]
    return pl.pallas_call(
        kernel,
        name=name,
        in_specs=[SMEM] * len(own) + [VMEM] * len(near) + [HBM] * len(far),
        out_specs=[HBM if direct else VMEM for _, direct in outs],
        out_shape=[value for value, _ in outs],
        scratch_shapes=(landing if kernel is not pack_kernel else [])
        + scratch
        + ([pltpu.SemaphoreType.DMA((len(far),))] if far else []),
        compiler_params=pltpu.CompilerParams(vmem_limit_bytes=limit),
        cost_estimate=pl.CostEstimate(flops=flops, bytes_accessed=moved, transcendentals=0),
    )(*own, *near, *far)


def shape(dims, kind=F32):
    return jax.ShapeDtypeStruct(dims, kind)


def run_pack(query_in, key_in, value_in, grad_out):
    return call(
        pack_kernel,
        "pack",
        [],
        [],
        [query_in, key_in, value_in, grad_out],
        [(shape((ROWS, 8, COLS), BF16), True)],
        [
            pltpu.VMEM((4, 128, COLS), BF16),
            pltpu.VMEM((2, 512, 128), F32),
            pltpu.VMEM((ROWS, 8, COLS), BF16),
            pltpu.SemaphoreType.DMA((4,)),
        ],
        1 << 20,
        1 << 19,
    )[0]


def run_filter(own, weight, bias, proj, decay, consts):
    names = ("pick", "turn", "right", "forward", "twiddle", "full")
    return call(
        filter_kernel,
        "filter",
        [own],
        [],
        [weight, bias, proj, decay] + [consts[name] for name in names],
        [
            (shape((ROWS * FEAT, COLS), BF16), True),
            (shape((ROWS * FEAT, COLS), BF16), True),
            (shape((CHAN * ROWS, COLS)), False),
            (shape((CHAN * ROWS, 2 * COLS)), False),
            (shape((CHAN * FEAT, 128)), False),
        ],
        [
            pltpu.VMEM((128, 128), F32),
            pltpu.VMEM((ROWS * FEAT, COLS), BF16),
            pltpu.VMEM((512, COLS), F32),
            pltpu.VMEM((512, COLS), F32),
            pltpu.VMEM((CHAN * ROWS, COLS), F32),
            pltpu.VMEM((ROWS * FEAT, COLS), BF16),
            pltpu.VMEM((ROWS * FEAT, COLS), BF16),
            pltpu.SemaphoreType.DMA((2, 8)),
        ],
        1 << 33,
        1 << 23,
    )


def run_gradient(own, arrived, short, cosine, envelope, columns, filter_spec, consts):
    names = ("back", "back_turn", "place", "forward", "last", "twiddle", "full")
    return call(
        gradient_kernel,
        "gradient",
        [own],
        [],
        [arrived, envelope, columns, cosine, filter_spec, short] + [consts[name] for name in names],
        [
            (shape((HANDED, 128)), True),
            (shape((32, 8, 128)), False),
        ],
        [
            pltpu.VMEM((128, 128), F32),
            pltpu.VMEM((2, CHAN * ROWS, 128), F32),
            pltpu.VMEM((HANDED, 128), F32),
            pltpu.SemaphoreType.DMA((3,)),
        ],
        1 << 32,
        1 << 23,
    )


def run_output(own, skip, handed, act, consts):
    names = ("last", "twiddle", "full")
    return call(
        output_kernel,
        "output",
        [own],
        [],
        [handed, act, skip] + [consts[name] for name in names],
        [(shape((ROWS, 8, COLS), BF16), False)],
        [pltpu.VMEM((2, ROWS * 8, 128), F32)],
        1 << 31,
        1 << 22,
        52 * 1024 * 1024,
    )[0]


def run_compose(packed, basis_parts):
    return call(
        compose_kernel,
        "compose",
        [],
        [packed, basis_parts],
        [],
        [(shape((ROWS, 8, COLS), BF16), True)],
        [pltpu.VMEM((ROWS, 8, COLS), BF16), pltpu.SemaphoreType.DMA((4,))],
        1 << 20,
        1 << 20,
        ROOMY,
    )[0]


def run_local(query_in, key_in, value_in, short):
    return call(
        local_kernel,
        "local",
        [],
        [],
        [query_in, key_in, value_in, short],
        [(shape((3, 128, COLS)), False), (shape((3 * TAPS, 128, 128)), False)],
        [],
        1 << 28,
        1 << 20,
        ROOMY,
    )


def run_unpack(arrived, feat, taps, grad_out):
    block = shape((128, COLS), BF16)
    return call(
        unpack_kernel,
        "unpack",
        [],
        [arrived, feat, taps, grad_out],
        [],
        [(value, False) for value in [block] * 4 + [shape((FEAT, 128)), shape((EMB, FEAT))]],
        [pltpu.VMEM((2, ROWS * 8, 128), F32), pltpu.VMEM((64, 128), F32)],
        1 << 20,
        1 << 20,
        ROOMY,
    )


def make_consts():
    forward, last, twiddle, full = transform_tables()
    right, turn, pick, back, back_turn, place = basis_tables()
    return dict(
        forward=jnp.asarray(forward),
        last=jnp.asarray(last),
        twiddle=jnp.asarray(twiddle),
        full=jnp.asarray(full),
        right=jnp.asarray(right),
        turn=jnp.asarray(turn),
        pick=jnp.asarray(pick),
        back=jnp.asarray(back),
        back_turn=jnp.asarray(back_turn),
        place=jnp.asarray(place),
    )


CTX = ("zh", "yh", "yl", "core")
NEAR = ("yl", "core", "x", "zl")


def exchange(value, axes):
    return lax.all_to_all(value, axes, split_axis=0, concat_axis=0, tiled=True)


def on_device(
    query_in,
    key_in,
    value_in,
    short_kernel,
    basis_weight,
    basis_bias,
    filter_proj,
    decay_rate,
    skip_gain,
    grad_out,
):
    consts = make_consts()
    own = lax.axis_index(CTX).astype(jnp.int32).reshape(1)
    with jax.named_scope("spread"):
        arrived = exchange(run_pack(query_in, key_in, value_in, grad_out), CTX)
    short = short_kernel.transpose(0, 2, 1)
    block_feat, block_taps = run_local(query_in, key_in, value_in, short)
    act, cosine, envelope, filter_spec, columns = run_filter(
        own,
        basis_weight.T,
        basis_bias.reshape(1, FEAT),
        filter_proj.T,
        decay_rate.reshape(1, 128),
        consts,
    )
    handed, basis_own = run_gradient(
        own, arrived, short, cosine, envelope, columns, filter_spec, consts
    )
    with jax.named_scope("basis"):
        basis_parts = exchange(basis_own, NEAR)
    packed = run_output(
        own, skip_gain.reshape(1, 128), handed, act, consts
    )
    composed = run_compose(packed, basis_parts)
    with jax.named_scope("collect"):
        returned = exchange(composed, CTX)
    mixed, grad_query, grad_key, grad_value, grad_proj, grad_basis = run_unpack(
        returned, block_feat, block_taps, grad_out
    )
    return (mixed, grad_query, grad_key, grad_value, grad_proj.T, grad_basis.T)


def solution(mesh):
    finer = Mesh(mesh.devices.reshape(4, 4, 2, 2, 4, 2), CTX + ("x", "zl"))
    rows = ("x", "zl")
    block = P(rows, CTX)
    return jax.shard_map(
        on_device,
        mesh=finer,
        in_specs=(
            block,
            block,
            block,
            P(None, rows, None),
            P(),
            P(),
            P(rows, None),
            P(rows),
            P(rows),
            block,
        ),
        out_specs=(block, block, block, block, P(rows, None), P()),
        check_vma=False,
    )
```

```python
import math

import jax
import jax.numpy as jnp
import numpy as np
from jax import lax
from jax.experimental import pallas as pl
from jax.experimental.pallas import tpu as pltpu
from jax.sharding import Mesh
from jax.sharding import PartitionSpec as P
import ml_dtypes

F32 = jnp.float32
BF16 = jnp.bfloat16
EXACT = lax.Precision.HIGHEST

ROWS = 64
COLS = 256
TOTAL = ROWS * COLS
FEAT = 64
EMB = 33
TAPS = 7
CHAN = 2
GROUP = 40
TURN = 1.0 / (2.0 * math.pi)

SIN_COEF = (4.442879676818848, -7.307816505432129, 3.5977742671966553, -0.7911993861198425)
COS_COEF = (
    1.4142135381698608,
    -6.978850841522217,
    5.739460468292236,
    -1.883557915687561,
    0.3106880187988281,
)


def halves(table, count):
    parts = []
    rest = np.asarray(table, np.float64)
    for _ in range(count):
        part = rest.astype(np.float32).astype(ml_dtypes.bfloat16)
        parts.append(part)
        rest = rest - part.astype(np.float64)
    return parts


def transform_tables():
    rows = np.arange(ROWS)
    cols = np.arange(COLS)
    first = 2.0 * np.pi * ((4 * rows[:, None] + 1) * rows[None, :] % (4 * ROWS)) / (4 * ROWS)
    first_re, first_im = np.cos(first), -np.sin(first)
    forward = np.concatenate([first_re, first_im], axis=0)
    forward_cat = np.concatenate(halves(forward, 2), axis=1)
    last = np.concatenate([first_re.T, -first_im.T], axis=1) / TOTAL
    last_hi, last_lo = halves(last, 2)
    last_cat = np.concatenate([last_hi, last_lo, last_hi], axis=1)
    turn = 2.0 * np.pi * ((4 * rows[:, None] + 1) * cols[None, :]) / (4 * TOTAL)
    twiddle = np.stack([np.cos(turn), -np.sin(turn)]).astype(np.float32)
    inner = 2.0 * np.pi * (cols[:, None] * cols[None, :] % COLS) / COLS
    inner_re, inner_im = np.cos(inner), -np.sin(inner)
    full = np.concatenate(
        [
            np.concatenate([inner_re, inner_im], axis=1),
            np.concatenate([-inner_im, inner_re], axis=1),
        ],
        axis=0,
    )
    full_hi, full_lo = halves(full, 2)
    return forward_cat, last_cat, twiddle, np.stack([full_hi, full_lo])


def basis_tables():
    freq = np.arange(1, 17)
    cols = np.arange(COLS)
    rows = np.arange(ROWS)
    inner = 2.0 * np.pi * (freq[:, None] * cols[None, :] % TOTAL) / TOTAL
    short = np.concatenate(
        [np.cos(inner), np.sin(inner), cols[None, :] / TOTAL, np.ones((1, COLS))], axis=0
    )
    width = short.shape[0]
    hi, mid, lo = halves(short, 3)
    right = np.zeros((256, COLS), ml_dtypes.bfloat16)
    for place, part in ((0, hi), (GROUP, hi), (2 * GROUP, hi)):
        right[place : place + width] = part
    for place, part in ((128, mid), (128 + GROUP, lo), (128 + 2 * GROUP, mid)):
        right[place : place + width] = part
    outer = 2.0 * np.pi * (freq[None, :] * rows[:, None] % ROWS) / ROWS
    cos_out, sin_out = np.cos(outer), np.sin(outer)
    one = np.ones((ROWS, 1))
    block = rows[:, None] / ROWS
    cos_row = np.concatenate([cos_out, cos_out, one, one], axis=1)
    sin_row = np.concatenate([sin_out, sin_out, 0 * one, block], axis=1)
    turn = np.zeros((2, ROWS, 128), np.float32)
    for place in (0, GROUP, 2 * GROUP):
        turn[0, :, place : place + width] = cos_row
        turn[1, :, place : place + width] = sin_row
    pick = np.zeros((2, 128, 128), np.float32)
    for place in (0, GROUP, 2 * GROUP):
        for index in range(16):
            pick[0, 2 * index + 1, place + index] = 1.0
            pick[0, 2 * index + 2, place + 16 + index] = 1.0
            pick[1, 2 * index + 2, place + index] = 1.0
            pick[1, 2 * index + 1, place + 16 + index] = -1.0
        pick[0, 0, place + 32] = 1.0
        pick[0, EMB, place + 33] = 1.0
        pick[1, 0, place + 33] = 1.0
    back = np.zeros((COLS, 128))
    back[:, :width] = short.T
    back[:, 64:80] = short[16:32].T
    back[:, 80:96] = short[:16].T
    back_hi, back_lo = halves(back, 2)
    back_cat = np.concatenate([back_hi, back_lo], axis=1)
    back_turn = np.zeros((ROWS, 128), np.float32)
    back_turn[:, :32] = cos_row[:, :32]
    back_turn[:, 32] = 1.0
    back_turn[:, 33] = rows / ROWS
    back_turn[:, 64:80] = -sin_out
    back_turn[:, 80:96] = sin_out
    place = np.zeros((8, 8, 128), np.float32)
    for wanted in range(EMB):
        row, group = divmod(wanted, 8)
        if wanted == 0:
            lanes = (32, 33)
        elif wanted % 2:
            lanes = ((wanted - 1) // 2, 64 + (wanted - 1) // 2)
        else:
            lanes = (16 + (wanted - 2) // 2, 80 + (wanted - 2) // 2)
        for lane in lanes:
            place[group, row, lane] = 1.0
    return right, turn, pick, back_cat, back_turn, place


def split(value):
    hi = value.astype(BF16)
    lo = (value - hi.astype(F32)).astype(BF16)
    return hi, lo


def dot(left, right):
    return jnp.dot(left, right, preferred_element_type=F32)


def spectrum(signals, forward, twiddle_re, twiddle_im, full_hi, full_lo):
    wide = jnp.concatenate(signals, axis=1)
    section = dot(forward, jnp.concatenate([wide, wide], axis=0))
    turned = []
    for index in range(len(signals)):
        part = section[:, index * COLS : (index + 1) * COLS]
        part_re, part_im = part[:ROWS], part[ROWS:]
        turned.append(
            jnp.concatenate(
                [
                    part_re * twiddle_re - part_im * twiddle_im,
                    part_re * twiddle_im + part_im * twiddle_re,
                ],
                axis=1,
            )
        )
    return full_product(jnp.concatenate(turned, axis=0), full_hi, full_lo)


def full_product(value, full_hi, full_lo):
    hi, lo = split(value)
    return dot(hi, full_hi) + dot(lo, full_hi) + dot(hi, full_lo)


def restore(conj_spec, count, last, twiddle_re, twiddle_im, full_hi, full_lo):
    back = full_product(conj_spec, full_hi, full_lo)
    stacked = []
    for index in range(count):
        part = back[index * ROWS : (index + 1) * ROWS]
        part_re, part_im = part[:, :COLS], part[:, COLS:]
        stacked.append(
            jnp.concatenate(
                [
                    part_re * twiddle_re - part_im * twiddle_im,
                    part_re * twiddle_im + part_im * twiddle_re,
                ],
                axis=0,
            )
        )
    hi, lo = split(jnp.concatenate(stacked, axis=1))
    result = dot(last, jnp.concatenate([hi, hi, lo], axis=0))
    return [result[:, index * COLS : (index + 1) * COLS] for index in range(count)]


def take(ref, start, count, stride):
    return jnp.concatenate(
        [ref[half, pl.ds(start, count, stride=stride), :] for half in range(2)], axis=1
    )


def put(ref, start, count, stride, value):
    for half in range(2):
        ref[half, pl.ds(start, count, stride=stride), :] = value[:, half * 128 : half * 128 + 128]


AT_FEAT = 0
AT_SPEC = 2 * ROWS * 8
AT_RAW = AT_SPEC + 4 * 2 * CHAN * ROWS
AT_FILTER = AT_RAW + 2 * CHAN * ROWS
HANDED = AT_FILTER + 4 * CHAN * ROWS


def tiles(ref, start, stride, count, picked_tiles):
    return jnp.concatenate(
        [ref[start + tile * stride : start + tile * stride + count, :] for tile in picked_tiles], axis=1
    )


def fill(ref, value):
    for half in range(2):
        ref[half] = value[..., half * 128 : half * 128 + 128].reshape(ref.shape[1], 128)


def begin(sems, pairs):
    copies = [
        pltpu.make_async_copy(source, target, sems.at[index])
        for index, (source, target) in enumerate(pairs)
    ]
    for copy in copies:
        copy.start()
    return copies


def picked(row, wanted):
    lane = lax.broadcasted_iota(jnp.int32, row.shape, 1)
    return jnp.sum(jnp.where(lane == wanted, row, 0.0), axis=1, keepdims=True)


def pack_kernel(query, key, value, grad, out, held, wide, stage, out_sems, sems):
    copies = begin(sems, [(ref, held.at[index]) for index, ref in enumerate((query, key, value, grad))])
    for index in range(4):
        copies[index].wait()
        block = held[index].astype(F32)
        for half in range(2):
            wide[half, index * 128 : (index + 1) * 128, :] = block[:, half * 128 : half * 128 + 128]
    leaving = []
    for part in range(4):
        for peer in range(part * 16, part * 16 + 16):
            stage[peer] = take(wide, peer, 8, ROWS).astype(BF16)
        rows = pl.ds(part * 16, 16)
        leaving += begin(out_sems.at[pl.ds(part, 1)], [(stage.at[rows], out.at[rows])])
    for copy in leaving:
        copy.wait()


def expm1_small(value):
    series = jnp.ones_like(value)
    for order in range(9, 1, -1):
        series = 1.0 + value * series * (1.0 / order)
    return jnp.where(value > -0.5, value * series, jnp.exp(value) - 1.0)


def filter_kernel(
    own,
    weight_src,
    bias_src,
    proj_src,
    decay_src,
    pick_src,
    turn_src,
    right_src,
    forward_src,
    twiddle_src,
    full_src,
    act_out,
    cos_out,
    env_out,
    spec_out,
    column_out,
    weight,
    bias,
    proj,
    decay,
    pick,
    turn,
    right,
    forward,
    twiddle,
    full,
    layer,
    left,
    phase,
    phase_odd,
    filt,
    act,
    cosv,
    out_sems,
    sems,
):
    first = own[0]
    copies = begin(
        sems,
        [
            (weight_src, weight),
            (bias_src, bias),
            (pick_src, pick),
            (proj_src, proj),
            (turn_src, turn),
            (right_src, right),
            (decay_src, decay),
            (forward_src, forward),
            (twiddle_src, twiddle),
            (full_src, full),
        ],
    )
    layer[...] = jnp.zeros((128, 128), F32)
    for copy in copies[:3]:
        copy.wait()
    layer[0:EMB, 0:FEAT] = weight[...]
    layer[EMB : EMB + 1, 0:FEAT] = bias[...]
    layer_all = layer[...].T[0:FEAT, :]
    same = jnp.dot(layer_all, pick[0], precision=EXACT, preferred_element_type=F32) * TURN
    cross = jnp.dot(layer_all, pick[1], precision=EXACT, preferred_element_type=F32) * TURN
    lane = lax.broadcasted_iota(jnp.int32, (FEAT, 128), 1)
    sublane = lax.broadcasted_iota(jnp.int32, (8, 128), 0)
    for copy in copies[3:7]:
        copy.wait()
    columns = []
    for chan in range(CHAN):
        hit = lane == first + 64 * chan
        column = jnp.sum(jnp.where(hit, proj[...], 0.0), axis=1, keepdims=True)
        column_wide = jnp.broadcast_to(column, (FEAT, 128))
        column_out[chan * FEAT : (chan + 1) * FEAT, :] = column_wide
        columns.append(column_wide)

    def make_left(block, carry):
        value = same * turn[0, pl.ds(block, 1), :] + cross * turn[1, pl.ds(block, 1), :]
        hi = value.astype(BF16).astype(F32)
        rest = value - hi
        mid = rest.astype(BF16).astype(F32)
        lo = rest - mid
        one = jnp.where(lane < GROUP, hi, jnp.where(lane < 2 * GROUP, mid, lo))
        two = jnp.where(lane < 2 * GROUP, hi, mid)
        start = pl.multiple_of(block * FEAT, FEAT)
        left[pl.ds(start, FEAT), 0:128] = one.astype(BF16)
        left[pl.ds(start, FEAT), 128:256] = two.astype(BF16)
        return carry

    lax.fori_loop(0, ROWS, make_left, 0, unroll=4)

    def fetch(index, phase):
        base = pl.multiple_of(index * 512, 512)
        phase[...] = dot(left[pl.ds(base, 512), :], right[...])

    def finish(index, phase):
        base = pl.multiple_of(index * 512, 512)
        for half in range(2):
            lanes = slice(half * 128, half * 128 + 128)
            sums = [jnp.zeros((8, 128), F32)] * CHAN
            for inner in range(8):
                near = inner * FEAT
                turns = phase[near : near + FEAT, lanes]
                rest = turns - jnp.round(turns)
                square = rest * rest
                sine = SIN_COEF[-1] * square + SIN_COEF[-2]
                cosine = COS_COEF[-1] * square + COS_COEF[-2]
                for coef in SIN_COEF[-3::-1]:
                    sine = sine * square + coef
                for coef in COS_COEF[-3::-1]:
                    cosine = cosine * square + coef
                sine = sine * rest
                whole_sine = sine * cosine
                whole_cosine = 1.0 - sine * sine
                act[pl.ds(base + near, FEAT), lanes] = whole_sine.astype(BF16)
                cosv[pl.ds(base + near, FEAT), lanes] = whole_cosine.astype(BF16)
                for chan in range(CHAN):
                    total = jnp.sum(whole_sine * columns[chan], axis=0, keepdims=True)
                    sums[chan] = jnp.where(sublane == inner, total, sums[chan])
            for chan in range(CHAN):
                start = pl.multiple_of(chan * ROWS + index * 8, 8)
                filt[pl.ds(start, 8), lanes] = sums[chan]
        send(index, 0).start()
        send(index, 1).start()

    def pair(index, carry):
        fetch(2 * index + 1, phase_odd)
        finish(2 * index, phase)
        fetch(jnp.minimum(2 * index + 2, 7), phase)
        finish(2 * index + 1, phase_odd)
        return carry

    def send(index, which):
        rows = pl.ds(pl.multiple_of(index * 512, 512), 512)
        source, target = ((act, act_out), (cosv, cos_out))[which]
        return pltpu.make_async_copy(source.at[rows], target.at[rows], out_sems.at[which, index])

    fetch(0, phase)
    lax.fori_loop(0, 4, pair, 0)
    ratio = decay[...] * (1.0 / TOTAL)
    energy = expm1_small(-2.0 * decay[...]) / expm1_small(-2.0 * ratio)
    norm = 1.0 / jnp.sqrt(energy)
    for copy in copies[7:]:
        copy.wait()
    position = (
        lax.broadcasted_iota(jnp.int32, (ROWS, COLS), 0) * COLS
        + lax.broadcasted_iota(jnp.int32, (ROWS, COLS), 1)
    ).astype(F32)
    signals = []
    for chan in range(CHAN):
        rate = picked(decay[...], first + 64 * chan)
        envelope = jnp.exp(-(rate * position) * (1.0 / TOTAL)) * picked(norm, first + 64 * chan)
        env_out[chan * ROWS : (chan + 1) * ROWS, :] = envelope
        signals.append((filt[chan * ROWS : (chan + 1) * ROWS, :] * envelope).astype(BF16))
    spec_out[...] = spectrum(signals, forward[...], twiddle[0], twiddle[1], full[0], full[1])
    for index in range(8):
        send(index, 0).wait()
        send(index, 1).wait()


def own_taps(first, short, taps, order):
    row = lax.broadcasted_iota(jnp.int32, (TAPS, 128), 0)
    lane = lax.broadcasted_iota(jnp.int32, (TAPS, 128), 1)
    columns = jnp.where(row == 0, 1.0, 0.0)
    for place, which in order:
        for chan in range(CHAN):
            hit = lane == first + 64 * chan
            column = jnp.sum(jnp.where(hit, short[which], 0.0), axis=1, keepdims=True)
            columns = jnp.where(lane == place + chan, column, columns)
    taps[...] = jnp.zeros((128, 128), F32)
    taps[0:TAPS, :] = columns
    return taps[...].T[0:8, :]


def gradient_kernel(
    own,
    arrived_src,
    envelope_src,
    columns_src,
    cosine_src,
    filter_spec_src,
    short_src,
    back_src,
    back_turn_src,
    place_src,
    forward_src,
    last_src,
    twiddle_src,
    full_src,
    handed_out,
    basis_out,
    arrived,
    envelope,
    columns,
    cosine,
    filter_spec,
    short,
    back,
    back_turn,
    place,
    forward,
    last,
    twiddle,
    full,
    taps,
    raw,
    handed,
    out_sems,
    sems,
):
    first = own[0]
    copies = begin(
        sems,
        [
            (short_src, short),
            (arrived_src, arrived),
            (forward_src, forward),
            (twiddle_src, twiddle),
            (full_src, full),
            (last_src, last),
            (envelope_src, envelope),
            (cosine_src, cosine),
            (columns_src, columns),
            (filter_spec_src, filter_spec),
            (back_src, back),
            (back_turn_src, back_turn),
            (place_src, place),
        ],
    )
    copies[0].wait()
    weights = own_taps(first, short, taps, ((0, 0), (2, 1), (4, 2)))
    copies[1].wait()
    signal = arrived[...].astype(F32)
    lane = lax.broadcasted_iota(jnp.int32, (ROWS, 8, 128), 2)
    zeros = jnp.zeros((1, 8, 128), F32)
    left, right = signal[:, :, 0:128], signal[:, :, 128:256]
    sum_left = weights[None, :, 0:1] * left
    sum_right = weights[None, :, 0:1] * right
    for offset in range(1, TAPS):
        weight = weights[None, :, offset : offset + 1]
        moved_left = pltpu.roll(left, offset, 2)
        moved_right = pltpu.roll(right, offset, 2)
        before = jnp.concatenate([zeros, moved_right[:-1]], axis=0)
        sum_left = sum_left + weight * jnp.where(lane < offset, before, moved_left)
        sum_right = sum_right + weight * jnp.where(lane < offset, moved_left, moved_right)
    for half, result in enumerate((sum_left, sum_right)):
        handed[AT_FEAT + half * 512 : AT_FEAT + half * 512 + 512, :] = result.reshape(512, 128)

    def leave(part, start, size):
        rows = pl.ds(start, size)
        return begin(out_sems.at[pl.ds(part, 1)], [(handed.at[rows], handed_out.at[rows])])

    leaving = leave(0, AT_FEAT, AT_SPEC - AT_FEAT)

    def plane(index):
        return jnp.concatenate(
            [handed[pl.ds(AT_FEAT + half * 512 + index, ROWS, stride=8), :] for half in range(2)],
            axis=1,
        )

    signals = []
    for chan in range(CHAN):
        signals.append((plane(2 + chan) * plane(4 + chan)).astype(BF16))
    for chan in range(CHAN):
        signals.append((plane(chan) * plane(6 + chan)).astype(BF16))
    for copy in copies[2:5]:
        copy.wait()
    tables = (twiddle[0], twiddle[1], full[0], full[1])
    spec_all = spectrum(signals, forward[...], *tables)
    for tile in range(4):
        handed[AT_SPEC + tile * 256 : AT_SPEC + tile * 256 + 256, :] = spec_all[
            :, tile * 128 : tile * 128 + 128
        ]
    leaving += leave(1, AT_SPEC, AT_RAW - AT_SPEC)
    carried, grad = spec_all[: CHAN * ROWS], spec_all[CHAN * ROWS :]
    carried_re, carried_im = carried[:, :COLS], carried[:, COLS:]
    grad_re, grad_im = grad[:, :COLS], grad[:, COLS:]
    crossed = jnp.concatenate(
        [
            carried_re * grad_re + carried_im * grad_im,
            carried_im * grad_re - carried_re * grad_im,
        ],
        axis=1,
    )
    for copy in copies[5:7]:
        copy.wait()
    filter_grad = restore(crossed, CHAN, last[...], *tables)
    for chan in range(CHAN):
        rounded = filter_grad[chan].astype(BF16).astype(F32)
        scaled = rounded * envelope[chan * ROWS : (chan + 1) * ROWS, :]
        for half in range(2):
            raw[half, chan * ROWS : (chan + 1) * ROWS, :] = scaled[:, half * 128 : half * 128 + 128]
    for copy in copies[7:]:
        copy.wait()
    for half in range(2):
        handed[AT_RAW + half * 128 : AT_RAW + half * 128 + 128, :] = raw[half]
    for tile in range(4):
        handed[AT_FILTER + tile * 128 : AT_FILTER + tile * 128 + 128, :] = filter_spec[
            :, tile * 128 : tile * 128 + 128
        ]
    leaving += leave(2, AT_RAW, HANDED - AT_RAW)
    column0 = columns[0:FEAT, :]
    column1 = columns[FEAT : 2 * FEAT, :]
    back_all = back[...]

    def chunk(index, basis_sum):
        base = pl.multiple_of(index * 512, 512)
        start = pl.multiple_of(index * 8, 8)
        rows = [
            [raw[half, pl.ds(chan * ROWS + start, 8), :] for half in range(2)] for chan in range(CHAN)
        ]
        angles = back_turn[pl.ds(start, 8), :]
        parts = []
        for inner in range(8):
            near = inner * FEAT
            pieces = []
            for half in range(2):
                lanes = slice(half * 128, half * 128 + 128)
                value = (
                    column0 * rows[0][half][inner : inner + 1, :]
                    + column1 * rows[1][half][inner : inner + 1, :]
                )
                value = value * cosine[pl.ds(base + near, FEAT), lanes].astype(F32)
                pieces.append(value.astype(BF16))
            parts.append(jnp.concatenate(pieces, axis=1))
        product = dot(jnp.concatenate(parts, axis=0), back_all)
        for inner in range(8):
            near = inner * FEAT
            both = product[near : near + FEAT, 0:128] + product[near : near + FEAT, 128:256]
            basis_sum = basis_sum + both * angles[inner : inner + 1, :]
        return basis_sum

    basis_sum = lax.fori_loop(0, 8, chunk, jnp.zeros((FEAT, 128), F32), unroll=4)
    pieces = [
        lax.dot_general(
            place[group],
            basis_sum,
            (((1,), (1,)), ((), ())),
            precision=EXACT,
            preferred_element_type=F32,
        )
        for group in range(8)
    ]
    for quarter in range(4):
        row = jnp.concatenate(
            [piece[:, quarter * 16 : quarter * 16 + 16] for piece in pieces], axis=1
        )
        for peer in range(8):
            basis_out[quarter * 8 + peer] = row
    for copy in leaving:
        copy.wait()


HALO = TAPS - 1


def output_kernel(
    own,
    handed_src,
    act_src,
    skip_src,
    last_src,
    twiddle_src,
    full_src,
    out,
    handed,
    act,
    skip,
    last,
    twiddle,
    full,
    rows_out,
    sems,
):
    first = own[0]
    copies = begin(
        sems,
        [
            (handed_src, handed),
            (full_src, full),
            (twiddle_src, twiddle),
            (last_src, last),
            (skip_src, skip),
            (act_src, act),
        ],
    )
    lane128 = lax.broadcasted_iota(jnp.int32, (FEAT, 128), 1)
    row_lane = lane128 % 8
    for copy in copies[0:4]:
        copy.wait()
    tables = (twiddle[0], twiddle[1], full[0], full[1])
    own_rows = CHAN * ROWS
    carried_re = tiles(handed, AT_SPEC, 256, own_rows, (0, 1))
    carried_im = tiles(handed, AT_SPEC, 256, own_rows, (2, 3))
    grad_re = tiles(handed, AT_SPEC + own_rows, 256, own_rows, (0, 1))
    grad_im = tiles(handed, AT_SPEC + own_rows, 256, own_rows, (2, 3))
    filt_re = tiles(handed, AT_FILTER, 128, own_rows, (0, 1))
    filt_im = tiles(handed, AT_FILTER, 128, own_rows, (2, 3))
    crossed = jnp.concatenate(
        [
            jnp.concatenate(
                [
                    filt_re * carried_re - filt_im * carried_im,
                    -(filt_re * carried_im + filt_im * carried_re),
                ],
                axis=1,
            ),
            jnp.concatenate(
                [
                    filt_re * grad_re + filt_im * grad_im,
                    filt_im * grad_re - filt_re * grad_im,
                ],
                axis=1,
            ),
        ],
        axis=0,
    )
    sums = restore(crossed, 2 * CHAN, last[...], *tables)
    copies[4].wait()

    def plane(index):
        return jnp.concatenate(
            [handed[pl.ds(AT_FEAT + half * 512 + index, ROWS, stride=8), :] for half in range(2)],
            axis=1,
        )

    blank = jnp.zeros((1, 128), F32)
    for chan in range(CHAN):
        gain = picked(skip[...], first + 64 * chan)
        query, key, value, cotangent = [plane(2 * index + chan) for index in range(4)]
        carried_own = (key * value).astype(BF16).astype(F32)
        grad_own = (query * cotangent).astype(BF16).astype(F32)
        long_out = (sums[chan] + gain * carried_own).astype(BF16).astype(F32)
        carried_grad = (sums[CHAN + chan] + gain * grad_own).astype(BF16).astype(F32)
        put(rows_out, chan, ROWS, 8, long_out)
        put(rows_out, 2 + chan, ROWS, 8, carried_grad)
        follow = jnp.zeros((ROWS, 128), F32)
        before = jnp.zeros((ROWS, 128), F32)
        heads = (
            cotangent[:, 0:128] * long_out[:, 0:128],
            carried_grad[:, 0:128] * value[:, 0:128],
            carried_grad[:, 0:128] * key[:, 0:128],
        )
        wanted = [head.astype(BF16).astype(F32) for head in heads]
        for signal in (query, key, value):
            wanted.append(signal[:, 0:128].astype(BF16).astype(F32))
        for signal in (query, key, value):
            wanted.append(signal[:, 0:128] - signal[:, 0:128].astype(BF16).astype(F32))
        for index, head in enumerate(wanted):
            place = HALO * index
            head = pltpu.roll(head, place, 1) if place else head
            inside = (lane128 >= place) & (lane128 < place + HALO)
            if index < 3:
                follow = jnp.where(inside, head, follow)
            else:
                before = jnp.where(inside, head, before)
        halo = jnp.concatenate([follow[1:], blank], axis=0) + before
        rows_out[chan, pl.ds(4, ROWS, stride=8), :] = halo
    copies[5].wait()

    def chunk(index, proj_sum):
        base = pl.multiple_of(index * 512, 512)
        start = pl.multiple_of(index * 8, 8)
        rows = [
            jnp.concatenate(
                [
                    handed[pl.ds(AT_RAW + half * 128 + chan * ROWS + start, 8), :]
                    for half in range(2)
                ],
                axis=1,
            )
            for chan in range(CHAN)
        ]
        wide = jnp.concatenate(rows, axis=0)
        hi = wide.astype(BF16).astype(F32)
        packed = jnp.concatenate([hi, wide - hi, jnp.zeros((128 - 4 * 8, COLS), F32)], axis=0)
        turned = jnp.concatenate(
            [packed[:, half * 128 : half * 128 + 128].T for half in range(2)], axis=0
        ).astype(BF16)
        product = dot(act[pl.ds(base, 512), :], turned)
        for inner in range(8):
            near = inner * FEAT
            proj_sum = proj_sum + jnp.where(row_lane == inner, product[near : near + FEAT, :], 0.0)
        return proj_sum

    proj_sum = lax.fori_loop(0, 8, chunk, jnp.zeros((FEAT, 128), F32), unroll=4)
    own_lane = lane128 % 16
    stacked = jnp.concatenate(
        [jnp.where(own_lane < 8, proj_sum, 0.0), jnp.where(own_lane >= 8, proj_sum, 0.0)], axis=0
    )
    proj_wide = lax.dot_general(
        jnp.ones((8, 128), F32),
        stacked,
        (((1,), (1,)), ((), ())),
        precision=EXACT,
        preferred_element_type=F32,
    )
    proj_hi = proj_wide.astype(BF16).astype(F32)
    row = lax.broadcasted_iota(jnp.int32, (ROWS, 8, 128), 1)
    for half, proj_part in enumerate((proj_hi, proj_wide - proj_hi)):
        extra = jnp.where(row == 7, proj_part[None], 0.0)
        value = jnp.where(row < 5, rows_out[half].reshape(ROWS, 8, 128), extra)
        out[:, :, half * 128 : half * 128 + 128] = value.astype(BF16)


def compose_kernel(packed, basis_parts, out, stage, out_sems):
    basis = basis_parts[0]
    for source in range(1, 32):
        basis = basis + basis_parts[source]
    row = lax.broadcasted_iota(jnp.int32, (8, 128), 0)
    lane = lax.broadcasted_iota(jnp.int32, (8, 128), 1)
    last = jnp.where((lane >= 64) & (lane < 80), pltpu.roll(basis, 64, 1)[4:5], 0.0)
    left = jnp.where(
        row == 4, last, jnp.where(row == 5, basis[0:1], jnp.where(row == 6, basis[2:3], 0.0))
    )
    right = jnp.where(row == 5, basis[1:2], jnp.where(row == 6, basis[3:4], 0.0))
    extra = jnp.concatenate([left, right], axis=1)
    leaving = []
    for part in range(4):
        rows = pl.ds(part * 16, 16)
        stage[rows] = (packed[rows].astype(F32) + extra[None]).astype(BF16)
        leaving += begin(out_sems.at[pl.ds(part, 1)], [(stage.at[rows], out.at[rows])])
    for copy in leaving:
        copy.wait()


def local_kernel(
    query_src, key_src, value_src, short_src, feat_out, taps_out, query, key, value, short, sems
):
    copies = begin(
        sems, [(query_src, query), (key_src, key), (value_src, value), (short_src, short)]
    )
    lane = lax.broadcasted_iota(jnp.int32, (128, 128), 1)
    for copy in copies:
        copy.wait()
    for index, ref in enumerate((query, key, value)):
        weights = jnp.concatenate([short[index], jnp.zeros((128 - TAPS, 128), F32)], axis=0).T
        for offset in range(TAPS):
            taps_out[index * TAPS + offset] = jnp.broadcast_to(
                weights[:, offset : offset + 1], (128, 128)
            )
        block = ref[...].astype(F32)
        left, right = block[:, 0:128], block[:, 128:256]
        out_left = taps_out[index * TAPS] * left
        out_right = taps_out[index * TAPS] * right
        for offset in range(1, TAPS):
            weight = taps_out[index * TAPS + offset]
            moved_left = pltpu.roll(left, offset, 1)
            moved_right = pltpu.roll(right, offset, 1)
            out_left = out_left + weight * jnp.where(lane < offset, 0.0, moved_left)
            out_right = out_right + weight * jnp.where(lane < offset, moved_left, moved_right)
        feat_out[index, :, 0:128] = out_left
        feat_out[index, :, 128:256] = out_right


def unpack_kernel(
    arrived,
    feat,
    taps,
    grad,
    mixed,
    grad_query,
    grad_key,
    grad_value,
    proj,
    basis,
    wide,
    sorted_rows,
):
    fill(wide, arrived[...].astype(F32))

    def both(half, row):
        return jnp.concatenate(
            [wide[half, pl.ds(row + chan, ROWS, stride=8), :] for chan in range(CHAN)], axis=0
        )

    long_out = [both(half, 0) for half in range(2)]
    carried_grad = [both(half, 2) for half in range(2)]
    halo = jnp.concatenate([wide[half, pl.ds(4, ROWS, stride=8), :] for half in range(2)], axis=0)
    lane = lax.broadcasted_iota(jnp.int32, (128, 128), 1)
    feats = []
    for index in range(3):
        high = pltpu.roll(halo, 128 - HALO * (3 + index), 1)
        low = pltpu.roll(halo, 128 - HALO * (6 + index), 1)
        left = jnp.where(lane < HALO, high + low, feat[index, :, 0:128])
        feats.append((left, feat[index, :, 128:256]))
    cotangent = grad[...].astype(F32)
    cotangent = (cotangent[:, 0:128], cotangent[:, 128:256])
    for half in range(2):
        mixed[:, half * 128 : half * 128 + 128] = (feats[0][half] * long_out[half]).astype(BF16)
    grads = (
        [cotangent[half] * long_out[half] for half in range(2)],
        [carried_grad[half] * feats[2][half] for half in range(2)],
        [carried_grad[half] * feats[1][half] for half in range(2)],
    )
    for index, ref in enumerate((grad_query, grad_key, grad_value)):
        left, right = [part.astype(BF16).astype(F32) for part in grads[index]]
        out_left = taps[index * TAPS] * left
        out_right = taps[index * TAPS] * right
        for offset in range(1, TAPS):
            weight = taps[index * TAPS + offset]
            moved_left = pltpu.roll(left, 128 - offset, 1)
            moved_right = pltpu.roll(right, 128 - offset, 1)
            moved_halo = pltpu.roll(halo, (128 - offset - HALO * index) % 128, 1)
            edge = lane >= 128 - offset
            out_left = out_left + weight * jnp.where(edge, moved_right, moved_left)
            out_right = out_right + weight * jnp.where(edge, moved_halo, moved_right)
        ref[:, 0:128] = out_left.astype(BF16)
        ref[:, 128:256] = out_right.astype(BF16)
    rows = wide[0, pl.ds(7, ROWS, stride=8), :] + wide[1, pl.ds(7, ROWS, stride=8), :]
    rows = rows * (1.0 / math.sqrt(TOTAL))
    rows = jnp.concatenate([rows, jnp.zeros_like(rows)], axis=0).T
    proj[:, 0:ROWS] = rows[0:FEAT, 0:ROWS]
    proj[:, ROWS : 2 * ROWS] = rows[FEAT : 2 * FEAT, 0:ROWS]
    totals = []
    for quarter in range(4):
        pair = []
        for half in range(2):
            total = wide[half, quarter * 8 : quarter * 8 + 8, :]
            for source in range(quarter + 4, ROWS, 4):
                total = total + wide[half, source * 8 : source * 8 + 8, :]
            pair.append(total)
        totals.append(pair)
    scale = math.sqrt(FEAT / (TOTAL * 1024))
    ordered = [
        jnp.concatenate([left[5:6], right[5:6], left[6:7], right[6:7]], axis=0)
        for left, right in totals
    ]
    for group in range(8):
        lanes = slice(group * 16, group * 16 + 16)
        merged = jnp.concatenate(
            [value[:, lanes] for value in ordered] + [jnp.zeros((4, 64), F32)], axis=1
        )
        sorted_rows[pl.ds(group, 4, stride=8), :] = merged * scale
    sorted_rows[32:33, :] = (
        jnp.concatenate([left[4:5, 64:80] for left, _ in totals] + [jnp.zeros((1, 64), F32)], axis=1)
        * scale
    )
    basis[...] = sorted_rows[0:EMB, 0:FEAT]


SMEM = pl.BlockSpec(memory_space=pltpu.SMEM)
VMEM = pl.BlockSpec(memory_space=pltpu.VMEM)
HBM = pl.BlockSpec(memory_space=pltpu.HBM)
LIMIT = 62 * 1024 * 1024
ROOMY = 32 * 1024 * 1024


def call(kernel, name, own, near, far, outs, scratch, flops, moved, limit=LIMIT):
    landing = [pltpu.VMEM(value.shape, value.dtype) for value in far]
    return pl.pallas_call(
        kernel,
        name=name,
        in_specs=[SMEM] * len(own) + [VMEM] * len(near) + [HBM] * len(far),
        out_specs=[HBM if direct else VMEM for _, direct in outs],
        out_shape=[value for value, _ in outs],
        scratch_shapes=(landing if kernel is not pack_kernel else [])
        + scratch
        + ([pltpu.SemaphoreType.DMA((len(far),))] if far else []),
        compiler_params=pltpu.CompilerParams(vmem_limit_bytes=limit),
        cost_estimate=pl.CostEstimate(flops=flops, bytes_accessed=moved, transcendentals=0),
    )(*own, *near, *far)


def shape(dims, kind=F32):
    return jax.ShapeDtypeStruct(dims, kind)


def run_pack(query_in, key_in, value_in, grad_out):
    return call(
        pack_kernel,
        "pack",
        [],
        [],
        [query_in, key_in, value_in, grad_out],
        [(shape((ROWS, 8, COLS), BF16), True)],
        [
            pltpu.VMEM((4, 128, COLS), BF16),
            pltpu.VMEM((2, 512, 128), F32),
            pltpu.VMEM((ROWS, 8, COLS), BF16),
            pltpu.SemaphoreType.DMA((4,)),
        ],
        1 << 20,
        1 << 19,
    )[0]


def run_filter(own, weight, bias, proj, decay, consts):
    names = ("pick", "turn", "right", "forward", "twiddle", "full")
    return call(
        filter_kernel,
        "filter",
        [own],
        [],
        [weight, bias, proj, decay] + [consts[name] for name in names],
        [
            (shape((ROWS * FEAT, COLS), BF16), True),
            (shape((ROWS * FEAT, COLS), BF16), True),
            (shape((CHAN * ROWS, COLS)), False),
            (shape((CHAN * ROWS, 2 * COLS)), False),
            (shape((CHAN * FEAT, 128)), False),
        ],
        [
            pltpu.VMEM((128, 128), F32),
            pltpu.VMEM((ROWS * FEAT, COLS), BF16),
            pltpu.VMEM((512, COLS), F32),
            pltpu.VMEM((512, COLS), F32),
            pltpu.VMEM((CHAN * ROWS, COLS), F32),
            pltpu.VMEM((ROWS * FEAT, COLS), BF16),
            pltpu.VMEM((ROWS * FEAT, COLS), BF16),
            pltpu.SemaphoreType.DMA((2, 8)),
        ],
        1 << 33,
        1 << 23,
    )


def run_gradient(own, arrived, short, cosine, envelope, columns, filter_spec, consts):
    names = ("back", "back_turn", "place", "forward", "last", "twiddle", "full")
    return call(
        gradient_kernel,
        "gradient",
        [own],
        [],
        [arrived, envelope, columns, cosine, filter_spec, short] + [consts[name] for name in names],
        [
            (shape((HANDED, 128)), True),
            (shape((32, 8, 128)), False),
        ],
        [
            pltpu.VMEM((128, 128), F32),
            pltpu.VMEM((2, CHAN * ROWS, 128), F32),
            pltpu.VMEM((HANDED, 128), F32),
            pltpu.SemaphoreType.DMA((3,)),
        ],
        1 << 32,
        1 << 23,
    )


def run_output(own, skip, handed, act, consts):
    names = ("last", "twiddle", "full")
    return call(
        output_kernel,
        "output",
        [own],
        [],
        [handed, act, skip] + [consts[name] for name in names],
        [(shape((ROWS, 8, COLS), BF16), False)],
        [pltpu.VMEM((2, ROWS * 8, 128), F32)],
        1 << 31,
        1 << 22,
        52 * 1024 * 1024,
    )[0]


def run_compose(packed, basis_parts):
    return call(
        compose_kernel,
        "compose",
        [],
        [packed, basis_parts],
        [],
        [(shape((ROWS, 8, COLS), BF16), True)],
        [pltpu.VMEM((ROWS, 8, COLS), BF16), pltpu.SemaphoreType.DMA((4,))],
        1 << 20,
        1 << 20,
        ROOMY,
    )[0]


def run_local(query_in, key_in, value_in, short):
    return call(
        local_kernel,
        "local",
        [],
        [],
        [query_in, key_in, value_in, short],
        [(shape((3, 128, COLS)), False), (shape((3 * TAPS, 128, 128)), False)],
        [],
        1 << 28,
        1 << 20,
        ROOMY,
    )


def run_unpack(arrived, feat, taps, grad_out):
    block = shape((128, COLS), BF16)
    return call(
        unpack_kernel,
        "unpack",
        [],
        [arrived, feat, taps, grad_out],
        [],
        [(value, False) for value in [block] * 4 + [shape((FEAT, 128)), shape((EMB, FEAT))]],
        [pltpu.VMEM((2, ROWS * 8, 128), F32), pltpu.VMEM((64, 128), F32)],
        1 << 20,
        1 << 20,
        ROOMY,
    )


def make_consts():
    forward, last, twiddle, full = transform_tables()
    right, turn, pick, back, back_turn, place = basis_tables()
    return dict(
        forward=jnp.asarray(forward),
        last=jnp.asarray(last),
        twiddle=jnp.asarray(twiddle),
        full=jnp.asarray(full),
        right=jnp.asarray(right),
        turn=jnp.asarray(turn),
        pick=jnp.asarray(pick),
        back=jnp.asarray(back),
        back_turn=jnp.asarray(back_turn),
        place=jnp.asarray(place),
    )


CTX = ("zh", "yh", "yl", "core")
NEAR = ("yl", "core", "x", "zl")


def exchange(value, axes):
    return lax.all_to_all(value, axes, split_axis=0, concat_axis=0, tiled=True)


def on_device(
    query_in,
    key_in,
    value_in,
    short_kernel,
    basis_weight,
    basis_bias,
    filter_proj,
    decay_rate,
    skip_gain,
    grad_out,
):
    consts = make_consts()
    own = lax.axis_index(CTX).astype(jnp.int32).reshape(1)
    with jax.named_scope("spread"):
        arrived = exchange(run_pack(query_in, key_in, value_in, grad_out), CTX)
    short = short_kernel.transpose(0, 2, 1)
    block_feat, block_taps = run_local(query_in, key_in, value_in, short)
    act, cosine, envelope, filter_spec, columns = run_filter(
        own,
        basis_weight.T,
        basis_bias.reshape(1, FEAT),
        filter_proj.T,
        decay_rate.reshape(1, 128),
        consts,
    )
    handed, basis_own = run_gradient(
        own, arrived, short, cosine, envelope, columns, filter_spec, consts
    )
    with jax.named_scope("basis"):
        basis_parts = exchange(basis_own, NEAR)
    packed = run_output(
        own, skip_gain.reshape(1, 128), handed, act, consts
    )
    composed = run_compose(packed, basis_parts)
    with jax.named_scope("collect"):
        returned = exchange(composed, CTX)
    mixed, grad_query, grad_key, grad_value, grad_proj, grad_basis = run_unpack(
        returned, block_feat, block_taps, grad_out
    )
    return (mixed, grad_query, grad_key, grad_value, grad_proj.T, grad_basis.T)


def solution(mesh):
    finer = Mesh(mesh.devices.reshape(4, 4, 2, 2, 4, 2), CTX + ("x", "zl"))
    rows = ("x", "zl")
    block = P(rows, CTX)
    return jax.shard_map(
        on_device,
        mesh=finer,
        in_specs=(
            block,
            block,
            block,
            P(None, rows, None),
            P(),
            P(),
            P(rows, None),
            P(rows),
            P(rows),
            block,
        ),
        out_specs=(block, block, block, block, P(rows, None), P()),
        check_vma=False,
    )
```
